32 devices in a mesh: blk: 4 (over z), shard: 4 (over x, core), head: 2 (over y).
Axes of the slice: x: 2, y: 2, z: 4, core: 2. Of those that a mesh axis runs over, the one named last changes fastest.
Arguments:
- inputs: float32 [2048, 768], P(('blk', 'shard')), may hold values from -6 to 6
- cotangent: float32 [2048, 768], P(('blk', 'shard')), may hold values from -6 to 6
- weights: float32 [768, 6528], P(('blk', 'shard'), 'head'), may hold values from -80 to 80
- gains: float32 [2, 768], P(None, ('blk', 'shard')), may hold values from 0.25 to 1.75
- weight_moment: float32 [768, 6528], P(('blk', 'shard'), 'head'), may hold values from -4 to 4
- weight_second: float32 [768, 6528], P(('blk', 'shard'), 'head'), may hold values from 0.5 to 5
- gain_moment: float32 [2, 768], P(None, ('blk', 'shard')), may hold values from -4 to 4
- gain_second: float32 [2, 768], P(None, ('blk', 'shard')), may hold values from 512 to 20480
Outputs:
- outputs: float32 [2048, 768], P(('blk', 'shard'))
- input_grad: float32 [2048, 768], P(('blk', 'shard'))
- weight_grad: float32 [768, 6528], P(('blk', 'shard'), 'head')
- gain_grad: float32 [2, 768], P(None, ('blk', 'shard'))
- new_weights: float32 [768, 6528], P(('blk', 'shard'), 'head')
- new_weight_moment: float32 [768, 6528], P(('blk', 'shard'), 'head')
- new_weight_second: float32 [768, 6528], P(('blk', 'shard'), 'head')
- new_gains: float32 [2, 768], P(None, ('blk', 'shard'))
- new_gain_moment: float32 [2, 768], P(None, ('blk', 'shard'))
- new_gain_second: float32 [2, 768], P(None, ('blk', 'shard'))
The draws below stay inside these ranges and needn't reach their ends.
All inputs are finite; a program needn't handle non-finite values.
Results may differ from the reference program's by a relative error of at most 0.025.
The reference program's roundings to bfloat16 on the way count: a program that leaves them out, or rounds other values in their place, can miss the bound.
Values may be sent and summed in bfloat16 or wider, within the bound.
No kernel may reach another device: no remote copies, remote signals or barrier semaphores. Data moves between devices by JAX's collectives and lax.ppermute only.
A program may use at most 192 MiB of HBM per device.

```python
import math
import jax
import jax.numpy as jnp
from jax import lax

D = 768
HEADS = 12
HEAD_DIM = 64
FF = 1152
SEQS = 1
STEP = 3
TOKENS = 2048
SEQ_LEN = 2048
PW = 3264
N_HEAD = 2


def draw_weights(key, part):
    head_width = HEADS * HEAD_DIM // N_HEAD
    unit_width = FF // N_HEAD
    root_model = D ** 0.5
    out_factor = 2.0 * SEQ_LEN ** 0.25
    column_scale = jnp.concatenate([jnp.full((head_width,), 2.5 / root_model, jnp.float32), jnp.full((head_width,), 1.0 / root_model, jnp.float32), jnp.full((head_width,), 1.0 / root_model, jnp.float32), jnp.full((head_width,), out_factor / root_model, jnp.float32), jnp.full((unit_width,), 1.0 / root_model, jnp.float32), jnp.full((unit_width,), 1.0 / root_model, jnp.float32), jnp.full((unit_width,), 1.5 / FF ** 0.5, jnp.float32)])
    base_draw = jnp.clip(jax.random.normal(key, (D, N_HEAD, PW), jnp.float32), -4.0, 4.0)
    scaled_draw = base_draw * column_scale
    return scaled_draw.reshape(D, N_HEAD * PW)


def block_levels(rng, shape, shards, low, top_value):
    def one(axis_at, blocks):
        steps = jax.random.uniform(jax.random.fold_in(jax.random.fold_in(rng, 6), axis_at), (blocks,), jnp.float32, low / len(shards), top_value / len(shards))
        return jnp.repeat(jnp.exp(steps), shape[axis_at] // blocks).reshape((-1,) + (1,) * (len(shape) - axis_at - 1))

    loudness = one(*shards[0])
    for cut in shards[1:]:
        loudness = loudness * one(*cut)
    return loudness


def centred(stream_key, extent, scale, limit, shards=(), held_as=jnp.bfloat16):
    level = block_levels(stream_key, extent, shards, -0.22, 0.18) if shards else 1.0
    array = jax.random.normal(stream_key, extent, jnp.float32) * scale * level
    return jnp.minimum(jnp.maximum(array, -limit), limit).astype(held_as)


def setup_inputs(seed: int = 0) -> dict:
    key_list = jax.random.split(jax.random.key(seed), 9)
    return {
        "inputs": centred(key_list[0], (TOKENS, D), 1.0, 6.0, ((0, 16),), jnp.float32),
        "cotangent": centred(key_list[1], (TOKENS, D), 1.0, 6.0, ((0, 16),), jnp.float32),
        "weights": draw_weights(jax.random.fold_in(key_list[8], 71), 0),
        "gains": jnp.clip(1.0 + 0.15 * jax.random.normal(key_list[3], (2, D), jnp.float32), 0.25, 1.75),
        "weight_moment": centred(key_list[4], (D, N_HEAD * PW), 1.0, 4.0, ((0, 16), (1, 2)), jnp.float32),
        "weight_second": jnp.clip(jnp.exp(math.log(5.0) - 2.3025851 * jax.random.uniform(key_list[5], (D, N_HEAD * PW), jnp.float32) ** block_levels(key_list[5], (D, N_HEAD * PW), ((0, 16), (1, 2)), -0.2, 0.2)), 0.5, 5.0),
        "gain_moment": centred(key_list[6], (2, D), 1.0, 4.0, ((1, 16),), jnp.float32),
        "gain_second": jnp.clip(jnp.exp(math.log(20480.0) - 3.6888795 * jax.random.uniform(key_list[7], (2, D), jnp.float32) ** block_levels(key_list[7], (2, D), ((1, 16),), -0.2, 0.2)), 512.0, 20480.0),
    }


NORM_EPS = 1e-05
THETA = 160000.0
BETA_ONE = 0.9
BETA_TWO = 0.98
LEARN_RATE = 0.2
ADAM_EPS = 1e-06
DECAY = 0.01

def layer_norm_forward(values, gain_row):
    centre = values - lax.optimization_barrier(jnp.mean(values, axis=-1, keepdims=True))
    inv_std = lax.rsqrt(lax.optimization_barrier(jnp.mean(centre * centre, axis=-1, keepdims=True)) + NORM_EPS)
    normed = centre * inv_std
    return (normed * gain_row, normed, inv_std)

def layer_norm_backward(upstream, normed, inv_std, gain_row):
    scaled = upstream * gain_row
    result = inv_std * (scaled - lax.optimization_barrier(jnp.mean(scaled, axis=-1, keepdims=True)) - normed * lax.optimization_barrier(jnp.mean(scaled * normed, axis=-1, keepdims=True)))
    return (result, lax.optimization_barrier(jnp.sum(upstream * normed, axis=0)))

def rotary_tables(positions, head_dim):
    half_dim = head_dim // 2
    inverse = jnp.exp(jnp.arange(half_dim, dtype=jnp.float32) * (-2.0 * math.log(THETA) / head_dim))
    angles = positions.astype(jnp.float32)[:, None] * inverse[None, :]
    angles = jnp.concatenate([angles, angles], axis=-1)
    return (jnp.cos(angles)[:, None, :], jnp.sin(angles)[:, None, :])

def rotate(tensor_in, cosine_rows, sine_rows):
    half_dim = tensor_in.shape[-1] // 2
    turned = jnp.concatenate([-tensor_in[..., half_dim:], tensor_in[..., :half_dim]], axis=-1)
    return tensor_in * cosine_rows + turned * sine_rows

def rotate_back(gradient, cosine_rows, sine_rows):
    half_dim = gradient.shape[-1] // 2
    with_sine = gradient * sine_rows
    return gradient * cosine_rows + jnp.concatenate([with_sine[..., half_dim:], -with_sine[..., :half_dim]], axis=-1)

def gelu_parts(pre_values):
    normal_cdf = 0.5 * (1.0 + lax.erf(pre_values * 0.7071067811865476))
    density = jnp.exp(-0.5 * pre_values * pre_values) * 0.3989422804014327
    return (pre_values * normal_cdf, normal_cdf + pre_values * density)

def adam_update(tensor, gradient, moment, second):
    moment = BETA_ONE * moment + (1.0 - BETA_ONE) * gradient
    second = BETA_TWO * second + (1.0 - BETA_TWO) * gradient * gradient
    first_hat = moment / (1.0 - BETA_ONE ** STEP)
    second_hat = second / (1.0 - BETA_TWO ** STEP)
    tensor = tensor - LEARN_RATE * (first_hat / (jnp.sqrt(second_hat) + ADAM_EPS) + DECAY * tensor)
    return (tensor, moment, second)

def head_forward(query_rows, key_rows, value_rows, block_rows, score_scale):
    blocks = query_rows.reshape(-1, block_rows, query_rows.shape[-1])

    def one_block(query_block):
        scores = jnp.dot(query_block, key_rows.T, preferred_element_type=jnp.float32) * score_scale
        row_max = lax.optimization_barrier(jnp.max(scores, axis=-1, keepdims=True))
        exp_scores = jnp.exp(scores - row_max)
        row_sum = lax.optimization_barrier(jnp.sum(exp_scores, axis=-1, keepdims=True))
        result = jnp.dot(exp_scores.astype(jnp.bfloat16), value_rows, preferred_element_type=jnp.float32) / row_sum
        return (result, (row_max + jnp.log(row_sum))[:, 0])
    result_rows, log_total = lax.map(one_block, blocks)
    return (result_rows.reshape(-1, query_rows.shape[-1]), log_total.reshape(-1))

def head_backward(query_rows, key_rows, value_rows, grad_rows, log_total, row_dots, block_rows, score_scale):
    head_dim = query_rows.shape[-1]
    count_blocks = query_rows.shape[0] // block_rows

    def one_block(running, parts):
        key_grad, value_grad = running
        query_block, grad_block, total_block, dots_block = parts
        scores = jnp.dot(query_block, key_rows.T, preferred_element_type=jnp.float32) * score_scale
        soft_rows = jnp.exp(scores - total_block[:, None])
        prob_grad = jnp.dot(grad_block, value_rows.T, preferred_element_type=jnp.float32)
        score_grad = (soft_rows * (prob_grad - dots_block[:, None])).astype(jnp.bfloat16)
        query_grad = jnp.dot(score_grad, key_rows, preferred_element_type=jnp.float32) * score_scale
        key_grad = key_grad + jnp.dot(score_grad.T, query_block, preferred_element_type=jnp.float32) * score_scale
        value_grad = value_grad + jnp.dot(soft_rows.astype(jnp.bfloat16).T, grad_block, preferred_element_type=jnp.float32)
        return ((key_grad, value_grad), query_grad)
    start_state = (jnp.zeros(key_rows.shape, jnp.float32), jnp.zeros(key_rows.shape, jnp.float32))
    parts = (query_rows.reshape(count_blocks, block_rows, head_dim), grad_rows.reshape(count_blocks, block_rows, head_dim), log_total.reshape(count_blocks, block_rows), row_dots.reshape(count_blocks, block_rows))
    (key_grad, value_grad), query_grad = lax.scan(one_block, start_state, parts)
    return (query_grad.reshape(-1, head_dim), key_grad, value_grad)

def reference(inputs, cotangent, weights, gains, weight_moment, weight_second, gain_moment, gain_second):
    head_width = HEADS * HEAD_DIM // N_HEAD
    unit_width = FF // N_HEAD
    widths = [head_width] * 4 + [unit_width] * 3
    starts = [sum(widths[:kind_index]) for kind_index in range(7)]
    rounded = weights.astype(jnp.bfloat16)
    matrices = []
    for kind_index in range(7):
        matrices.append(jnp.concatenate([rounded[:, group * PW + starts[kind_index]:group * PW + starts[kind_index] + widths[kind_index]] for group in range(N_HEAD)], axis=1))
    query_proj, key_proj, value_proj, attn_out_proj, input_proj, gate_proj, ffn_out_proj = matrices
    gain_rows = lax.optimization_barrier(gains.astype(jnp.bfloat16)).astype(jnp.float32)
    attention_norm_gain = gain_rows[0]
    feedforward_norm_gain = gain_rows[1]
    score_scale = 1.0 / math.sqrt(HEAD_DIM)
    block_rows = min(SEQ_LEN, 4096)
    positions = jnp.arange(TOKENS, dtype=jnp.int32) % SEQ_LEN
    cosine_rows, sine_rows = rotary_tables(positions, HEAD_DIM)
    attention_normalized_input, attention_centered_scaled, attention_reciprocal_deviation = layer_norm_forward(inputs, attention_norm_gain)
    attn_in = attention_normalized_input.astype(jnp.bfloat16)
    query_rot = rotate(jnp.dot(attn_in, query_proj, preferred_element_type=jnp.float32).reshape(TOKENS, HEADS, HEAD_DIM), cosine_rows, sine_rows).astype(jnp.bfloat16)
    key_rot = rotate(jnp.dot(attn_in, key_proj, preferred_element_type=jnp.float32).reshape(TOKENS, HEADS, HEAD_DIM), cosine_rows, sine_rows).astype(jnp.bfloat16)
    value_rows = jnp.dot(attn_in, value_proj, preferred_element_type=jnp.float32).astype(jnp.bfloat16).reshape(TOKENS, HEADS, HEAD_DIM)
    query_heads = query_rot.transpose(1, 0, 2)
    key_heads = key_rot.transpose(1, 0, 2)
    value_heads = value_rows.transpose(1, 0, 2)
    attn_parts = []
    total_parts = []
    for sequence in range(SEQS):
        lower = sequence * SEQ_LEN
        upper = lower + SEQ_LEN
        part_attn, part_total = lax.map(lambda triple: head_forward(triple[0], triple[1], triple[2], block_rows, score_scale), (query_heads[:, lower:upper], key_heads[:, lower:upper], value_heads[:, lower:upper]))
        attn_parts.append(part_attn)
        total_parts.append(part_total)
    attn_heads = jnp.concatenate(attn_parts, axis=1)
    log_total = jnp.concatenate(total_parts, axis=1)
    attn_bf = attn_heads.astype(jnp.bfloat16)
    attn_rows = attn_bf.transpose(1, 0, 2).reshape(TOKENS, D)
    hidden_state = inputs + jnp.dot(attn_rows, attn_out_proj.T, preferred_element_type=jnp.float32)
    feedforward_normalized_input, feedforward_centered_scaled, feedforward_reciprocal_deviation = layer_norm_forward(hidden_state, feedforward_norm_gain)
    ffn_in = feedforward_normalized_input.astype(jnp.bfloat16)
    pre_act = jnp.dot(ffn_in, input_proj, preferred_element_type=jnp.float32)
    gate_val = jnp.dot(ffn_in, gate_proj, preferred_element_type=jnp.float32)
    activated, act_slope = gelu_parts(pre_act)
    mixed_rows = (activated * gate_val).astype(jnp.bfloat16)
    outputs = hidden_state + jnp.dot(mixed_rows, ffn_out_proj.T, preferred_element_type=jnp.float32)
    cot_rows = cotangent.astype(jnp.bfloat16)
    grad_ffn_out = jnp.dot(cot_rows.T, mixed_rows, preferred_element_type=jnp.float32)
    grad_mixed = jnp.dot(cot_rows, ffn_out_proj, preferred_element_type=jnp.float32)
    grad_pre = (grad_mixed * gate_val * act_slope).astype(jnp.bfloat16)
    grad_gate_val = (grad_mixed * activated).astype(jnp.bfloat16)
    grad_input_proj = jnp.dot(ffn_in.T, grad_pre, preferred_element_type=jnp.float32)
    grad_gate_proj = jnp.dot(ffn_in.T, grad_gate_val, preferred_element_type=jnp.float32)
    feedforward_normalized_gradient = jnp.dot(grad_pre, input_proj.T, preferred_element_type=jnp.float32) + jnp.dot(grad_gate_val, gate_proj.T, preferred_element_type=jnp.float32)
    second_norm_backward_cache, feedforward_norm_gain_gradient = layer_norm_backward(feedforward_normalized_gradient, feedforward_centered_scaled, feedforward_reciprocal_deviation, feedforward_norm_gain)
    grad_hidden = cotangent + second_norm_backward_cache
    hidden_rows = grad_hidden.astype(jnp.bfloat16)
    grad_attn_out = jnp.dot(hidden_rows.T, attn_rows, preferred_element_type=jnp.float32)
    grad_attn = jnp.dot(hidden_rows, attn_out_proj, preferred_element_type=jnp.float32).astype(jnp.bfloat16)
    grad_heads = grad_attn.reshape(TOKENS, HEADS, HEAD_DIM).transpose(1, 0, 2)
    row_dots = lax.optimization_barrier(jnp.sum(grad_heads.astype(jnp.float32) * attn_bf.astype(jnp.float32), axis=-1))
    query_parts = []
    key_parts = []
    value_parts = []
    for sequence in range(SEQS):
        lower = sequence * SEQ_LEN
        upper = lower + SEQ_LEN
        part_query, part_key, part_value = lax.map(lambda group_in: head_backward(group_in[0], group_in[1], group_in[2], group_in[3], group_in[4], group_in[5], block_rows, score_scale), (query_heads[:, lower:upper], key_heads[:, lower:upper], value_heads[:, lower:upper], grad_heads[:, lower:upper], log_total[:, lower:upper], row_dots[:, lower:upper]))
        query_parts.append(part_query)
        key_parts.append(part_key)
        value_parts.append(part_value)
    query_grad = jnp.concatenate(query_parts, axis=1)
    key_grad = jnp.concatenate(key_parts, axis=1)
    value_grad = jnp.concatenate(value_parts, axis=1)
    query_back = rotate_back(query_grad.transpose(1, 0, 2), cosine_rows, sine_rows).reshape(TOKENS, D).astype(jnp.bfloat16)
    key_back = rotate_back(key_grad.transpose(1, 0, 2), cosine_rows, sine_rows).reshape(TOKENS, D).astype(jnp.bfloat16)
    value_back = value_grad.transpose(1, 0, 2).reshape(TOKENS, D).astype(jnp.bfloat16)
    grad_query_proj = jnp.dot(attn_in.T, query_back, preferred_element_type=jnp.float32)
    grad_key_proj = jnp.dot(attn_in.T, key_back, preferred_element_type=jnp.float32)
    grad_value_proj = jnp.dot(attn_in.T, value_back, preferred_element_type=jnp.float32)
    attention_normalized_gradient = jnp.dot(query_back, query_proj.T, preferred_element_type=jnp.float32) + jnp.dot(key_back, key_proj.T, preferred_element_type=jnp.float32) + jnp.dot(value_back, value_proj.T, preferred_element_type=jnp.float32)
    first_norm_backward_cache, attention_norm_gain_gradient = layer_norm_backward(attention_normalized_gradient, attention_centered_scaled, attention_reciprocal_deviation, attention_norm_gain)
    input_grad = grad_hidden + first_norm_backward_cache
    grad_kinds = [grad_query_proj, grad_key_proj, grad_value_proj, grad_attn_out, grad_input_proj, grad_gate_proj, grad_ffn_out]
    grouped = []
    for group in range(N_HEAD):
        for kind_index in range(7):
            grouped.append(grad_kinds[kind_index][:, group * widths[kind_index]:(group + 1) * widths[kind_index]])
    weight_grad = jnp.concatenate(grouped, axis=1)
    gain_grad = jnp.stack([attention_norm_gain_gradient, feedforward_norm_gain_gradient])
    new_weights, new_weight_moment, new_weight_second = adam_update(weights, weight_grad, weight_moment, weight_second)
    new_gains, new_gain_moment, new_gain_second = adam_update(gains, gain_grad, gain_moment, gain_second)
    return (outputs, input_grad, weight_grad, gain_grad, new_weights, new_weight_moment, new_weight_second, new_gains, new_gain_moment, new_gain_second)
```

```python
from functools import partial
import math

import jax
import jax.numpy as jnp
from jax import lax
from jax.experimental import pallas as pl
from jax.experimental.pallas import tpu as pltpu
from jax.sharding import PartitionSpec as P

HEADS = 12
HEAD_DIM = 64
FF = 1152
STEP = 3

NORM_EPS = 1e-05
THETA = 160000.0
BETA_ONE = 0.9
BETA_TWO = 0.98
LEARN_RATE = 0.2
ADAM_EPS = 1e-06
DECAY = 0.01
NEG_LARGE = -1e30
SCALE = 1.0 / math.sqrt(HEAD_DIM)
TOKENS_AX = ("blk", "shard")
F32 = jnp.float32
BF16 = jnp.bfloat16
KEY_ROWS = 2048
SUB_ROWS = 512


VM = pl.BlockSpec(memory_space=pltpu.VMEM)
SM = pl.BlockSpec(memory_space=pltpu.SMEM)
ANY = pl.BlockSpec(memory_space=pl.ANY)


def sds(shape, dtype):
    return jax.ShapeDtypeStruct(shape, dtype)


def dot_nn(a, b):
    return lax.dot_general(a, b, (((1,), (0,)), ((), ())), preferred_element_type=F32)


def dot_nt(a, b):
    return lax.dot_general(a, b, (((1,), (1,)), ((), ())), preferred_element_type=F32)


def dot_tn(a, b):
    return lax.dot_general(a, b, (((0,), (0,)), ((), ())), preferred_element_type=F32)


def swap(x, axis, bits):
    size = lax.axis_size(axis)
    return lax.ppermute(x, axis, [(i, i ^ bits) for i in range(size)])


def staged():
    return lax.axis_size("blk") == 4 and lax.axis_size("shard") == 4


def chunk_order():
    return [z * 4 + x * 2 + c for c in range(2) for x in range(2) for z in range(4)]


def gather(x):
    if not staged():
        return [lax.all_gather(x, TOKENS_AX, axis=0, tiled=True)]
    got = {0: x}
    for z in range(1, 4):
        got[z * 4] = swap(x, "blk", z)
    for z in range(4):
        got[z * 4 + 2] = swap(got[z * 4], "shard", 2)
    for z in range(4):
        for h in (0, 2):
            got[z * 4 + h + 1] = swap(got[z * 4 + h], "shard", 1)
    return [got[j] for j in chunk_order()]


def add_kernel(*refs):
    keep, recv = refs[0], refs[1]
    for i, out in enumerate(refs[2:]):
        rows = out.shape[0]
        at = pl.ds(i * rows, rows)
        out[...] = (keep[at, :].astype(F32) + recv[at, :].astype(F32)).astype(BF16)


def scatter_sum(parts):
    if not staged():
        return [lax.psum_scatter(parts[0], TOKENS_AX, scatter_dimension=0, tiled=True)]
    keep, send = parts
    rows, cols = keep.shape[0] // 8, keep.shape[1]
    recv = swap(send, "shard", 1)
    s = pl.pallas_call(
        add_kernel,
        out_shape=[sds((rows, cols), BF16)] * 8,
        in_specs=[VM, VM],
        out_specs=[VM] * 8,
        name="pair_add",
    )(keep, recv)
    t = {}
    for z in (1, 2, 3, 0):
        got = swap(s[4 + z], "shard", 2)
        t[z] = (s[z].astype(F32) + got.astype(F32)).astype(BF16)
    return [t[0]] + [swap(t[z], "blk", z) for z in (1, 2, 3)]


def total(terms):
    out = terms[0].astype(F32)
    for term in terms[1:]:
        out = out + term.astype(F32)
    return out


def weight_copies(order_ref, chunks, dst, sems, cols=None):
    rows = chunks[0].shape[0]
    copies = []
    for i, chunk in enumerate(chunks):
        src = chunk if cols is None else chunk.at[:, pl.ds(cols[0], cols[1])]
        if len(chunks) == 1:
            at = pl.ds(0, rows)
        else:
            at = pl.ds(pl.multiple_of((order_ref[0] ^ chunk_order()[i]) * rows, 16), rows)
        copies.append(pltpu.make_async_copy(src, dst.at[at, :], sems.at[i]))
    for copy in copies:
        copy.start()
    return copies


def emit_blocks(order_ref, acc, outs):
    if len(outs) == 1:
        outs[0][...] = acc[...].astype(BF16)
        return
    rows = outs[0].shape[0] // 8
    for i, j in enumerate(chunk_order()):
        at = pl.ds(pl.multiple_of((order_ref[0] ^ j) * rows, 8), rows)
        outs[i // 8][pl.ds((i % 8) * rows, rows), :] = acc[at, :].astype(BF16)


def norm_parts(v):
    centre = v - jnp.mean(v, axis=-1, keepdims=True)
    inv = lax.rsqrt(jnp.mean(centre * centre, axis=-1, keepdims=True) + NORM_EPS)
    return centre * inv, inv


def norm_back(u, xhat, inv, g):
    s = u * g
    return inv * (
        s
        - jnp.mean(s, axis=-1, keepdims=True)
        - xhat * jnp.mean(s * xhat, axis=-1, keepdims=True)
    )


def low_half(shape):
    lane = lax.broadcasted_iota(jnp.int32, shape, 1)
    return (lane & (HEAD_DIM - 1)) < HEAD_DIM // 2


def turn(u):
    width = u.shape[1]
    half = HEAD_DIM // 2
    left = pltpu.roll(u, width - half, 1)
    right = pltpu.roll(u, half, 1)
    return left, right, low_half(u.shape)


def rope(u, cos, sin):
    left, right, low = turn(u)
    return u * cos + jnp.where(low, -left, right) * sin


def rope_back(w, cos, sin):
    left, right, low = turn(w * sin)
    return w * cos + jnp.where(low, left, -right)


def wide(table, width):
    return jnp.concatenate([table] * (width // table.shape[1]), axis=1)


def two_heads(pair):
    lane = lax.broadcasted_iota(jnp.int32, pair.shape, 1)
    zero = jnp.zeros_like(pair)
    first = lane < HEAD_DIM
    return jnp.concatenate(
        [jnp.where(first, pair, zero), jnp.where(first, zero, pair)], axis=0
    )


def join_heads(both):
    rows = both.shape[0] // 2
    lane = lax.broadcasted_iota(jnp.int32, (rows, both.shape[1]), 1)
    return jnp.where(lane < HEAD_DIM, both[:rows], both[rows:])


def as_row(col):
    return jnp.transpose(jnp.broadcast_to(col, (col.shape[0], 128)))[0:1, :]


def qkv_kernel(n, order_ref, x_ref, cos_ref, sin_ref, *rest):
    chunks = rest[:n]
    a_ref, q_ref, kv_ref, g_ref, w, sems = rest[n:]
    width = q_ref.shape[1]
    copies = weight_copies(order_ref, chunks, w, sems)
    xhat, _ = norm_parts(x_ref[...])
    for copy in copies:
        copy.wait()
    row = lax.broadcasted_iota(jnp.int32, (8, 128), 0)
    lane = lax.broadcasted_iota(jnp.int32, (8, 128), 1)
    pick = jnp.where(row == lane, 1.0, 0.0).astype(BF16)
    g = dot_nt(pick, w[:, 3 * width : 3 * width + 128])
    g_ref[...] = g
    a = (xhat * g[0:1, :]).astype(BF16)
    a_ref[...] = a
    cos = wide(cos_ref[...], width)
    sin = wide(sin_ref[...], width)
    q_ref[...] = rope(dot_nn(a, w[:, :width]), cos, sin).astype(BF16)
    kv_ref[:, :width] = rope(dot_nn(a, w[:, width : 2 * width]), cos, sin).astype(BF16)
    kv_ref[:, width:] = dot_nn(a, w[:, 2 * width : 3 * width]).astype(BF16)


def key_copies(chunks, dst, sems, block):
    if len(chunks) == 1:
        rows = dst.shape[0]
        at = pl.ds(pl.multiple_of(block * rows, rows), rows)
        copies = [pltpu.make_async_copy(chunks[0].at[at, :], dst, sems.at[0])]
    else:
        rows = chunks[0].shape[0]
        copies = [
            pltpu.make_async_copy(chunk, dst.at[pl.ds(i * rows, rows), :], sems.at[i])
            for i, chunk in enumerate(chunks)
        ]
    for copy in copies:
        copy.start()
    return copies


def each(count, body):
    if count == 1:
        body(0)
    else:
        lax.fori_loop(0, count, lambda i, c: (body(i), c)[1], 0)


def attend_kernel(n, nw, blocks, order_ref, q_ref, *rest):
    keys = rest[:n]
    wos = rest[n : n + nw]
    attn_ref, lse_ref, out_ref, kv, wo, m_s, l_s, acc_s, ksem, wsem = rest[n + nw :]
    width = q_ref.shape[1]
    pairs = width // 128
    wcopies = weight_copies(order_ref, wos, wo, wsem, (0, width))
    m_s[...] = jnp.full(m_s.shape, NEG_LARGE, F32)
    l_s[...] = jnp.zeros(l_s.shape, F32)
    acc_s[...] = jnp.zeros(acc_s.shape, F32)

    def block_work(block):
        for copy in key_copies(keys, kv, ksem, block):
            copy.wait()
        for p in range(pairs):
            at = slice(p * 128, p * 128 + 128)
            qm = two_heads(q_ref[:, at]) * jnp.asarray(SCALE, BF16)
            s = dot_nt(qm, kv[:, at])
            m_old = m_s[p]
            m_new = jnp.maximum(m_old, jnp.max(s, axis=1, keepdims=True))
            factor = jnp.exp(m_old - m_new)
            e = jnp.exp(s - m_new)
            l_s[p] = l_s[p] * factor + jnp.sum(e, axis=1, keepdims=True)
            m_s[p] = m_new
            acc_s[p] = acc_s[p] * factor + dot_nn(
                e.astype(BF16), kv[:, width + p * 128 : width + p * 128 + 128]
            )

    each(blocks, block_work)
    for p in range(pairs):
        attn_ref[:, p * 128 : p * 128 + 128] = join_heads(acc_s[p] / l_s[p]).astype(BF16)
        lse_ref[p : p + 1, :] = as_row(m_s[p] + jnp.log(l_s[p]))
    for copy in wcopies:
        copy.wait()
    out_ref[...] = dot_nt(attn_ref[...], wo[...]).astype(BF16)


def gelu_parts(z):
    cdf = 0.5 * (1.0 + lax.erf(z * 0.7071067811865476))
    density = jnp.exp(-0.5 * z * z) * 0.3989422804014327
    return z * cdf, cdf + z * density


def ffn_kernel(nw, width, order_ref, x_ref, pa_ref, pb_ref, cot_ref, g_ref, *rest):
    ws = rest[:nw]
    hid_ref, out_ref, db_ref, b_ref, dz_ref, mixed_ref, w, wsem = rest[nw:]
    units = mixed_ref.shape[1]
    copies = weight_copies(order_ref, ws, w, wsem, (width, w.shape[1]))
    hidden = x_ref[...] + (pa_ref[...].astype(F32) + pb_ref[...].astype(F32))
    hid_ref[...] = hidden
    xhat, _ = norm_parts(hidden)
    b = (xhat * g_ref[1:2, :]).astype(BF16)
    b_ref[...] = b
    cb = cot_ref[...].astype(BF16)
    for copy in copies:
        copy.wait()
    z = dot_nn(b, w[:, : 2 * units])
    gate = z[:, units:]
    act, slope = gelu_parts(z[:, :units])
    dmix = dot_nn(cb, w[:, 2 * units : 3 * units])
    dz = jnp.concatenate([dmix * gate * slope, dmix * act], axis=1).astype(BF16)
    dz_ref[...] = dz
    db_ref[...] = dot_nt(dz, w[:, : 2 * units]).astype(BF16)
    mixed = (act * gate).astype(BF16)
    mixed_ref[...] = mixed
    out_ref[...] = dot_nt(mixed, w[:, 2 * units : 3 * units]).astype(BF16)


def ffn_grad_kernel(no, order_ref, b_ref, dz_ref, cot_ref, mixed_ref, *rest):
    outs, acc = rest[:no], rest[no]
    two = dz_ref.shape[1]
    acc[:, :two] = dot_tn(b_ref[...], dz_ref[...])
    acc[:, two:] = dot_tn(cot_ref[...].astype(BF16), mixed_ref[...])
    emit_blocks(order_ref, acc, outs)


def attend_back_kernel(
    n, nw, no, blocks, order_ref, q_ref, attn_ref, lse_ref, hid_ref, cot_ref, g_ref,
    da_ref, db_ref, cos_ref, sin_ref, *rest
):
    keys = rest[:n]
    wos = rest[n : n + nw]
    outs = rest[n + nw : n + nw + no]
    dhid_ref, dqp_ref, kv, wo, dq_s, qm_s, dom_s, row_s, ksem, wsem = rest[n + nw + no :]
    width = q_ref.shape[1]
    pairs = width // 128
    wcopies = weight_copies(order_ref, wos, wo, wsem, (0, width))
    first = key_copies(keys, kv, ksem, 0) if blocks == 1 else None
    xhat, inv = norm_parts(hid_ref[...])
    db = da_ref[...].astype(F32) + db_ref[...].astype(F32)
    dhid = cot_ref[...] + norm_back(db, xhat, inv, g_ref[1:2, :])
    dhid_ref[...] = dhid
    for copy in wcopies:
        copy.wait()
    dattn = dot_nn(dhid.astype(BF16), wo[...]).astype(BF16)
    for p in range(pairs):
        at = slice(p * 128, p * 128 + 128)
        qm_s[p] = two_heads(q_ref[:, at]) * jnp.asarray(SCALE, BF16)
        dom = two_heads(dattn[:, at])
        dom_s[p] = dom
        both = jnp.concatenate([attn_ref[:, at]] * 2, axis=0)
        dots = jnp.sum(dom.astype(F32) * both.astype(F32), axis=1, keepdims=True)
        row_s[p : p + 1, :] = as_row(dots)
    dq_s[...] = jnp.zeros(dq_s.shape, F32)
    halves = len(outs)
    block_rows = kv.shape[0]

    def block_work(block):
        for copy in first or key_copies(keys, kv, ksem, block):
            copy.wait()
        for half in range(halves):
            count = block_rows // halves // SUB_ROWS

            def sub_work(sub):
                src = pl.ds(
                    pl.multiple_of(half * (block_rows // halves) + sub * SUB_ROWS, SUB_ROWS),
                    SUB_ROWS,
                )
                dst = pl.ds(
                    pl.multiple_of(block * block_rows + sub * SUB_ROWS, SUB_ROWS), SUB_ROWS
                )
                for p in range(pairs):
                    at = slice(p * 128, p * 128 + 128)
                    vat = slice(width + p * 128, width + p * 128 + 128)
                    k = kv[src, at]
                    prob = jnp.exp(dot_nt(k, qm_s[p]) - lse_ref[p : p + 1, :])
                    dprob = dot_nt(kv[src, vat], dom_s[p])
                    ds = (prob * (dprob - row_s[p : p + 1, :])).astype(BF16)
                    outs[half][dst, at] = dot_nn(ds, qm_s[p]).astype(BF16)
                    outs[half][dst, vat] = dot_nn(prob.astype(BF16), dom_s[p]).astype(BF16)
                    dq_s[p] += dot_tn(ds, k)

            each(count, sub_work)

    each(blocks, block_work)
    dq = jnp.concatenate([join_heads(dq_s[p]) for p in range(pairs)], axis=1) * SCALE
    dqp_ref[...] = rope_back(
        dq, wide(cos_ref[...], width), wide(sin_ref[...], width)
    ).astype(BF16)


def qkv_grad_kernel(
    n, nt, no, order_ref, a_ref, dqp_ref, dhid_ref, attn_ref, cos_ref, sin_ref, *rest
):
    terms = rest[:nt]
    chunks = rest[nt : nt + n]
    outs = rest[nt + n : nt + n + no]
    da_ref, w, acc, sems = rest[nt + n + no :]
    width = dqp_ref.shape[1]
    copies = weight_copies(order_ref, chunks, w, sems)
    dkv = terms[0][...].astype(F32)
    for term in terms[1:]:
        dkv = dkv + term[...].astype(F32)
    dkp = rope_back(
        dkv[:, :width], wide(cos_ref[...], width), wide(sin_ref[...], width)
    ).astype(BF16)
    d = jnp.concatenate([dqp_ref[...], dkp, dkv[:, width:].astype(BF16)], axis=1)
    for copy in copies:
        copy.wait()
    da_ref[...] = dot_nt(d, w[:, : 3 * width]).astype(BF16)
    acc[:, : 3 * width] = dot_tn(a_ref[...], d)
    acc[:, 3 * width :] = dot_tn(dhid_ref[...].astype(BF16), attn_ref[...])
    emit_blocks(order_ref, acc, outs)


def call(kernel, out_shape, specs, scratch, args, name):
    return pl.pallas_call(
        kernel,
        out_shape=out_shape,
        in_specs=specs,
        out_specs=jax.tree.map(lambda _: VM, out_shape),
        scratch_shapes=scratch,
        name=name,
    )(*args)


def rotary_tables(positions):
    half = HEAD_DIM // 2
    inverse = jnp.exp(jnp.arange(half, dtype=F32) * (-2.0 * math.log(THETA) / HEAD_DIM))
    angles = positions.astype(F32)[:, None] * inverse[None, :]
    angles = jnp.concatenate([angles] * 4, axis=-1)
    return jnp.cos(angles), jnp.sin(angles)


def adam_update(tensor, gradient, moment, second):
    moment = BETA_ONE * moment + (1.0 - BETA_ONE) * gradient
    second = BETA_TWO * second + (1.0 - BETA_TWO) * gradient * gradient
    first_hat = moment / (1.0 - BETA_ONE**STEP)
    second_hat = second / (1.0 - BETA_TWO**STEP)
    tensor = tensor - LEARN_RATE * (first_hat / (jnp.sqrt(second_hat) + ADAM_EPS) + DECAY * tensor)
    return tensor, moment, second


def head_swap(x):
    size = lax.axis_size("head")
    if size == 1:
        return jnp.zeros_like(x)
    return lax.ppermute(x, "head", [(i, i ^ 1) for i in range(size)])


def per_device(
    inputs, cotangent, weights, gains, weight_moment, weight_second, gain_moment, gain_second
):
    heads = lax.axis_size("head")
    width = HEADS // heads * HEAD_DIM
    units = FF // heads
    toks, d = inputs.shape
    rows = weights.shape[0]
    n = lax.axis_size(TOKENS_AX)
    seq = toks * n
    me = lax.axis_index(TOKENS_AX).astype(jnp.int32)
    order = me.reshape(1)
    pairs = width // 128

    wb = weights.astype(BF16)
    gb = gains.astype(BF16)
    wq_cols = 3 * width + 128
    rest_cols = width + 3 * units
    rest_pad = -rest_cols % 128
    w_first = jnp.concatenate([wb[:, : 3 * width], jnp.pad(gb.T, ((0, 0), (0, 126)))], axis=1)
    w_rest = jnp.pad(wb[:, 3 * width :], ((0, 0), (0, rest_pad)))
    rest_cols += rest_pad
    first_chunks = gather(w_first)
    cos, sin = rotary_tables(me * toks + jnp.arange(toks, dtype=jnp.int32))

    nw = len(first_chunks)
    wsem = pltpu.SemaphoreType.DMA((nw,))
    halves = 2 if staged() else 1

    a, q, kv, g = call(
        partial(qkv_kernel, nw),
        [sds((toks, d), BF16), sds((toks, width), BF16), sds((toks, 2 * width), BF16), sds((8, d), F32)],
        [SM, VM, VM, VM] + [ANY] * nw,
        [pltpu.VMEM((d, wq_cols), BF16), wsem],
        [order, inputs, cos, sin] + first_chunks,
        "qkv",
    )
    keys = gather(kv)
    w_rest, _ = lax.optimization_barrier((w_rest, kv))
    rest_chunks = gather(w_rest)
    nk = len(keys)
    block_rows = min(KEY_ROWS, seq)
    blocks = seq // block_rows
    ksem = pltpu.SemaphoreType.DMA((nk,))

    attn, lse, out_part = call(
        partial(attend_kernel, nk, nw, blocks),
        [sds((toks, width), BF16), sds((8, 2 * toks), F32), sds((toks, d), BF16)],
        [SM, VM] + [ANY] * (nk + nw),
        [
            pltpu.VMEM((block_rows, 2 * width), BF16),
            pltpu.VMEM((d, width), BF16),
            pltpu.VMEM((pairs, 2 * toks, 1), F32),
            pltpu.VMEM((pairs, 2 * toks, 1), F32),
            pltpu.VMEM((pairs, 2 * toks, 128), F32),
            ksem,
            wsem,
        ],
        [order, q] + keys + rest_chunks,
        "attend",
    )
    out_other = head_swap(out_part)

    hidden, ffn_part, db_part, b, dz, mixed = call(
        partial(ffn_kernel, nw, width),
        [
            sds((toks, d), F32),
            sds((toks, d), BF16),
            sds((toks, d), BF16),
            sds((toks, d), BF16),
            sds((toks, 2 * units), BF16),
            sds((toks, units), BF16),
        ],
        [SM] + [VM] * 5 + [ANY] * nw,
        [pltpu.VMEM((d, rest_cols - width), BF16), wsem],
        [order, inputs, out_part, out_other, cotangent, g] + rest_chunks,
        "ffn",
    )
    db_other = head_swap(db_part)
    ffn_other = head_swap(ffn_part)
    outputs = hidden + (ffn_part.astype(F32) + ffn_other.astype(F32))
    ffn_grads = call(
        partial(ffn_grad_kernel, halves),
        [sds((d // halves, 3 * units), BF16)] * halves,
        [SM] + [VM] * 4,
        [pltpu.VMEM((d, 3 * units), F32)],
        [order, b, dz, cotangent, mixed],
        "ffn_grad",
    )
    ffn_terms = scatter_sum(ffn_grads)

    back = call(
        partial(attend_back_kernel, nk, nw, halves, blocks),
        [sds((seq // halves, 2 * width), BF16)] * halves
        + [sds((toks, d), F32), sds((toks, width), BF16)],
        [SM] + [VM] * 10 + [ANY] * (nk + nw),
        [
            pltpu.VMEM((block_rows, 2 * width), BF16),
            pltpu.VMEM((d, width), BF16),
            pltpu.VMEM((pairs, 2 * toks, 128), F32),
            pltpu.VMEM((pairs, 2 * toks, 128), BF16),
            pltpu.VMEM((pairs, 2 * toks, 128), BF16),
            pltpu.VMEM((8, 2 * toks), F32),
            ksem,
            wsem,
        ],
        [order, q, attn, lse, hidden, cotangent, g, db_part, db_other, cos, sin] + keys + rest_chunks,
        "attend_back",
    )
    dhid, dqp = back[halves:]
    kv_terms = scatter_sum(back[:halves])
    nt = len(kv_terms)
    grads = call(
        partial(qkv_grad_kernel, nw, nt, halves),
        [sds((d // halves, 4 * width), BF16)] * halves + [sds((toks, d), BF16)],
        [SM] + [VM] * 6 + [VM] * nt + [ANY] * nw,
        [pltpu.VMEM((d, wq_cols), BF16), pltpu.VMEM((d, 4 * width), F32), wsem],
        [order, a, dqp, dhid, attn, cos, sin] + kv_terms + first_chunks,
        "qkv_grad",
    )
    da_part = grads[halves]
    da_other = head_swap(da_part)
    da = da_part.astype(F32) + da_other.astype(F32)
    xhat, inv = norm_parts(inputs)
    input_grad = dhid + norm_back(da, xhat, inv, g[0:1, :])

    first_grad = total(scatter_sum(grads[:halves]))
    ffn_grad = total(ffn_terms)
    weight_grad = jnp.concatenate([first_grad, ffn_grad], axis=1)
    wf = wb.astype(F32)
    gain_part = jnp.stack(
        [
            jnp.sum(wf[:, : 3 * width] * first_grad[:, : 3 * width], axis=1),
            jnp.sum(wf[:, 4 * width : 4 * width + 2 * units] * ffn_grad[:, : 2 * units], axis=1),
        ]
    )
    gain_grad = (gain_part + head_swap(gain_part)) / gb.astype(F32)
    new_weights, new_weight_moment, new_weight_second = adam_update(
        weights, weight_grad, weight_moment, weight_second
    )
    new_gains, new_gain_moment, new_gain_second = adam_update(
        gains, gain_grad, gain_moment, gain_second
    )
    return (
        outputs,
        input_grad,
        weight_grad,
        gain_grad,
        new_weights,
        new_weight_moment,
        new_weight_second,
        new_gains,
        new_gain_moment,
        new_gain_second,
    )


def solution(mesh):
    rows = P(("blk", "shard"), None)
    cells = P(("blk", "shard"), "head")
    lanes = P(None, ("blk", "shard"))
    return jax.shard_map(
        per_device,
        mesh=mesh,
        in_specs=(rows, rows, cells, lanes, cells, cells, lanes, lanes),
        out_specs=(rows, rows, cells, lanes, cells, cells, cells, lanes, lanes, lanes),
        check_vma=False,
    )
```

```python
from functools import partial
import math

import jax
import jax.numpy as jnp
from jax import lax
from jax.experimental import pallas as pl
from jax.experimental.pallas import tpu as pltpu
from jax.sharding import PartitionSpec as P


HEADS = 12
HEAD_DIM = 64
FF = 1152
STEP = 3

NORM_EPS = 1e-05
THETA = 160000.0
BETA_ONE = 0.9
BETA_TWO = 0.98
LEARN_RATE = 0.2
ADAM_EPS = 1e-06
DECAY = 0.01
NEG_LARGE = -1e30
SCALE = 1.0 / math.sqrt(HEAD_DIM)
TOKENS_AX = ("blk", "shard")
F32 = jnp.float32
BF16 = jnp.bfloat16
KEY_ROWS = 2048
SUB_ROWS = 512


VM = pl.BlockSpec(memory_space=pltpu.VMEM)
SM = pl.BlockSpec(memory_space=pltpu.SMEM)
ANY = pl.BlockSpec(memory_space=pl.ANY)


def sds(shape, dtype):
    return jax.ShapeDtypeStruct(shape, dtype)


def dot_nn(a, b):
    return lax.dot_general(a, b, (((1,), (0,)), ((), ())), preferred_element_type=F32)


def dot_nt(a, b):
    return lax.dot_general(a, b, (((1,), (1,)), ((), ())), preferred_element_type=F32)


def dot_tn(a, b):
    return lax.dot_general(a, b, (((0,), (0,)), ((), ())), preferred_element_type=F32)


def swap(x, axis, bits):
    size = lax.axis_size(axis)
    return lax.ppermute(x, axis, [(i, i ^ bits) for i in range(size)])


def staged():
    return lax.axis_size("blk") == 4 and lax.axis_size("shard") == 4


def chunk_order():
    return [z * 4 + x * 2 + c for c in range(2) for x in range(2) for z in range(4)]


def gather(x):
    if not staged():
        return [lax.all_gather(x, TOKENS_AX, axis=0, tiled=True)]
    got = {0: x}
    for z in range(1, 4):
        got[z * 4] = swap(x, "blk", z)
    for z in range(4):
        got[z * 4 + 2] = swap(got[z * 4], "shard", 2)
    for z in range(4):
        for h in (0, 2):
            got[z * 4 + h + 1] = swap(got[z * 4 + h], "shard", 1)
    return [got[j] for j in chunk_order()]


def add_kernel(*refs):
    keep, recv = refs[0], refs[1]
    for i, out in enumerate(refs[2:]):
        rows = out.shape[0]
        at = pl.ds(i * rows, rows)
        out[...] = (keep[at, :].astype(F32) + recv[at, :].astype(F32)).astype(BF16)


def scatter_sum(parts):
    if not staged():
        return [lax.psum_scatter(parts[0], TOKENS_AX, scatter_dimension=0, tiled=True)]
    keep, send = parts
    rows, cols = keep.shape[0] // 8, keep.shape[1]
    recv = swap(send, "shard", 1)
    s = pl.pallas_call(
        add_kernel,
        out_shape=[sds((rows, cols), BF16)] * 8,
        in_specs=[VM, VM],
        out_specs=[VM] * 8,
        name="pair_add",
    )(keep, recv)
    t = {}
    for z in (3, 2, 1, 0):
        got = swap(s[4 + z], "shard", 2)
        t[z] = (s[z].astype(F32) + got.astype(F32)).astype(BF16)
    return [t[0]] + [swap(t[z], "blk", z) for z in (3, 2, 1)]


def total(terms):
    out = terms[0].astype(F32)
    for term in terms[1:]:
        out = out + term.astype(F32)
    return out


def weight_copies(order_ref, chunks, dst, sems, cols=None):
    rows = chunks[0].shape[0]
    copies = []
    for i, chunk in enumerate(chunks):
        src = chunk if cols is None else chunk.at[:, pl.ds(cols[0], cols[1])]
        if len(chunks) == 1:
            at = pl.ds(0, rows)
        else:
            at = pl.ds(pl.multiple_of((order_ref[0] ^ chunk_order()[i]) * rows, 16), rows)
        copies.append(pltpu.make_async_copy(src, dst.at[at, :], sems.at[i]))
    for copy in copies:
        copy.start()
    return copies


def emit_blocks(order_ref, acc, outs):
    if len(outs) == 1:
        outs[0][...] = acc[...].astype(BF16)
        return
    rows = outs[0].shape[0] // 8
    for i, j in enumerate(chunk_order()):
        at = pl.ds(pl.multiple_of((order_ref[0] ^ j) * rows, 8), rows)
        outs[i // 8][pl.ds((i % 8) * rows, rows), :] = acc[at, :].astype(BF16)


def norm_parts(v):
    centre = v - jnp.mean(v, axis=-1, keepdims=True)
    inv = lax.rsqrt(jnp.mean(centre * centre, axis=-1, keepdims=True) + NORM_EPS)
    return centre * inv, inv


def norm_back(u, xhat, inv, g):
    s = u * g
    return inv * (
        s
        - jnp.mean(s, axis=-1, keepdims=True)
        - xhat * jnp.mean(s * xhat, axis=-1, keepdims=True)
    )


def low_half(shape):
    lane = lax.broadcasted_iota(jnp.int32, shape, 1)
    return (lane & (HEAD_DIM - 1)) < HEAD_DIM // 2


def turn(u):
    width = u.shape[1]
    half = HEAD_DIM // 2
    left = pltpu.roll(u, width - half, 1)
    right = pltpu.roll(u, half, 1)
    return left, right, low_half(u.shape)


def rope(u, cos, sin):
    left, right, low = turn(u)
    return u * cos + jnp.where(low, -left, right) * sin


def rope_back(w, cos, sin):
    left, right, low = turn(w * sin)
    return w * cos + jnp.where(low, left, -right)


def wide(table, width):
    return jnp.concatenate([table] * (width // table.shape[1]), axis=1)


def two_heads(pair):
    lane = lax.broadcasted_iota(jnp.int32, pair.shape, 1)
    zero = jnp.zeros_like(pair)
    first = lane < HEAD_DIM
    return jnp.concatenate(
        [jnp.where(first, pair, zero), jnp.where(first, zero, pair)], axis=0
    )


def join_heads(both):
    rows = both.shape[0] // 2
    lane = lax.broadcasted_iota(jnp.int32, (rows, both.shape[1]), 1)
    return jnp.where(lane < HEAD_DIM, both[:rows], both[rows:])


def as_row(col):
    return jnp.transpose(jnp.broadcast_to(col, (col.shape[0], 128)))[0:1, :]


def qkv_kernel(n, order_ref, x_ref, cos_ref, sin_ref, *rest):
    chunks = rest[:n]
    a_ref, q_ref, kv_ref, g_ref, w, sems = rest[n:]
    width = q_ref.shape[1]
    copies = weight_copies(order_ref, chunks, w, sems)
    xhat, _ = norm_parts(x_ref[...])
    for copy in copies:
        copy.wait()
    row = lax.broadcasted_iota(jnp.int32, (8, 128), 0)
    lane = lax.broadcasted_iota(jnp.int32, (8, 128), 1)
    pick = jnp.where(row == lane, 1.0, 0.0).astype(BF16)
    g = dot_nt(pick, w[:, 4 * width : 4 * width + 128])
    g_ref[...] = g
    a = (xhat * g[0:1, :]).astype(BF16)
    a_ref[...] = a
    cos = wide(cos_ref[...], width)
    sin = wide(sin_ref[...], width)
    q_ref[...] = rope(dot_nn(a, w[:, :width]), cos, sin).astype(BF16)
    kv_ref[:, :width] = rope(dot_nn(a, w[:, width : 2 * width]), cos, sin).astype(BF16)
    kv_ref[:, width:] = dot_nn(a, w[:, 2 * width : 3 * width]).astype(BF16)


def key_copies(chunks, dst, sems, block):
    if len(chunks) == 1:
        rows = dst.shape[0]
        at = pl.ds(pl.multiple_of(block * rows, rows), rows)
        copies = [pltpu.make_async_copy(chunks[0].at[at, :], dst, sems.at[0])]
    else:
        rows = chunks[0].shape[0]
        copies = [
            pltpu.make_async_copy(chunk, dst.at[pl.ds(i * rows, rows), :], sems.at[i])
            for i, chunk in enumerate(chunks)
        ]
    for copy in copies:
        copy.start()
    return copies


def each(count, body):
    if count == 1:
        body(0)
    else:
        lax.fori_loop(0, count, lambda i, c: (body(i), c)[1], 0)


def attend_kernel(n, nw, blocks, order_ref, q_ref, *rest):
    keys = rest[:n]
    wos = rest[n : n + nw]
    attn_ref, lse_ref, out_ref, kv, wo, m_s, l_s, acc_s, ksem, wsem = rest[n + nw :]
    width = q_ref.shape[1]
    pairs = width // 128
    wcopies = weight_copies(order_ref, wos, wo, wsem, (3 * width, width))
    m_s[...] = jnp.full(m_s.shape, NEG_LARGE, F32)
    l_s[...] = jnp.zeros(l_s.shape, F32)
    acc_s[...] = jnp.zeros(acc_s.shape, F32)

    def block_work(block):
        for copy in key_copies(keys, kv, ksem, block):
            copy.wait()
        for p in range(pairs):
            at = slice(p * 128, p * 128 + 128)
            qm = two_heads(q_ref[:, at]) * jnp.asarray(SCALE, BF16)
            s = dot_nt(qm, kv[:, at])
            m_old = m_s[p]
            m_new = jnp.maximum(m_old, jnp.max(s, axis=1, keepdims=True))
            factor = jnp.exp(m_old - m_new)
            e = jnp.exp(s - m_new)
            l_s[p] = l_s[p] * factor + jnp.sum(e, axis=1, keepdims=True)
            m_s[p] = m_new
            acc_s[p] = acc_s[p] * factor + dot_nn(
                e.astype(BF16), kv[:, width + p * 128 : width + p * 128 + 128]
            )

    each(blocks, block_work)
    for p in range(pairs):
        attn_ref[:, p * 128 : p * 128 + 128] = join_heads(acc_s[p] / l_s[p]).astype(BF16)
        lse_ref[p : p + 1, :] = as_row(m_s[p] + jnp.log(l_s[p]))
    for copy in wcopies:
        copy.wait()
    out_ref[...] = dot_nt(attn_ref[...], wo[...]).astype(BF16)


def gelu_parts(z):
    cdf = 0.5 * (1.0 + lax.erf(z * 0.7071067811865476))
    density = jnp.exp(-0.5 * z * z) * 0.3989422804014327
    return z * cdf, cdf + z * density


def ffn_kernel(nw, order_ref, x_ref, pa_ref, pb_ref, cot_ref, g_ref, *rest):
    ws = rest[:nw]
    hid_ref, out_ref, db_ref, b_ref, dz_ref, mixed_ref, w, wsem = rest[nw:]
    units = mixed_ref.shape[1]
    copies = weight_copies(order_ref, ws, w, wsem)
    hidden = x_ref[...] + (pa_ref[...].astype(F32) + pb_ref[...].astype(F32))
    hid_ref[...] = hidden
    xhat, _ = norm_parts(hidden)
    b = (xhat * g_ref[1:2, :]).astype(BF16)
    b_ref[...] = b
    cb = cot_ref[...].astype(BF16)
    for copy in copies:
        copy.wait()
    z = dot_nn(b, w[:, : 2 * units])
    gate = z[:, units:]
    act, slope = gelu_parts(z[:, :units])
    dmix = dot_nn(cb, w[:, 2 * units : 3 * units])
    dz = jnp.concatenate([dmix * gate * slope, dmix * act], axis=1).astype(BF16)
    dz_ref[...] = dz
    db_ref[...] = dot_nt(dz, w[:, : 2 * units]).astype(BF16)
    mixed = (act * gate).astype(BF16)
    mixed_ref[...] = mixed
    out_ref[...] = dot_nt(mixed, w[:, 2 * units : 3 * units]).astype(BF16)


def ffn_grad_kernel(no, order_ref, b_ref, dz_ref, cot_ref, mixed_ref, *rest):
    outs, acc = rest[:no], rest[no]
    two = dz_ref.shape[1]
    acc[:, :two] = dot_tn(b_ref[...], dz_ref[...])
    half = mixed_ref.shape[1]
    acc[:, two : two + half] = dot_tn(cot_ref[...].astype(BF16), mixed_ref[...])
    acc[:, two + half :] = jnp.zeros((acc.shape[0], acc.shape[1] - two - half), F32)
    emit_blocks(order_ref, acc, outs)


def attend_back_kernel(
    n, nw, no, blocks, order_ref, q_ref, attn_ref, lse_ref, hid_ref, cot_ref, g_ref,
    da_ref, db_ref, cos_ref, sin_ref, *rest
):
    keys = rest[:n]
    wos = rest[n : n + nw]
    outs = rest[n + nw : n + nw + no]
    dhid_ref, dqp_ref, kv, wo, dq_s, qm_s, dom_s, row_s, ksem, wsem = rest[n + nw + no :]
    width = q_ref.shape[1]
    pairs = width // 128
    wcopies = weight_copies(order_ref, wos, wo, wsem, (3 * width, width))
    first = key_copies(keys, kv, ksem, 0) if blocks == 1 else None
    xhat, inv = norm_parts(hid_ref[...])
    db = da_ref[...].astype(F32) + db_ref[...].astype(F32)
    dhid = cot_ref[...] + norm_back(db, xhat, inv, g_ref[1:2, :])
    dhid_ref[...] = dhid
    for copy in wcopies:
        copy.wait()
    dattn = dot_nn(dhid.astype(BF16), wo[...]).astype(BF16)
    for p in range(pairs):
        at = slice(p * 128, p * 128 + 128)
        qm_s[p] = two_heads(q_ref[:, at]) * jnp.asarray(SCALE, BF16)
        dom = two_heads(dattn[:, at])
        dom_s[p] = dom
        both = jnp.concatenate([attn_ref[:, at]] * 2, axis=0)
        dots = jnp.sum(dom.astype(F32) * both.astype(F32), axis=1, keepdims=True)
        row_s[p : p + 1, :] = as_row(dots)
    dq_s[...] = jnp.zeros(dq_s.shape, F32)
    halves = len(outs)
    block_rows = kv.shape[0]

    def block_work(block):
        for copy in first or key_copies(keys, kv, ksem, block):
            copy.wait()
        for half in range(halves):
            count = block_rows // halves // SUB_ROWS

            def sub_work(sub):
                src = pl.ds(
                    pl.multiple_of(half * (block_rows // halves) + sub * SUB_ROWS, SUB_ROWS),
                    SUB_ROWS,
                )
                dst = pl.ds(
                    pl.multiple_of(block * block_rows + sub * SUB_ROWS, SUB_ROWS), SUB_ROWS
                )
                for p in range(pairs):
                    at = slice(p * 128, p * 128 + 128)
                    vat = slice(width + p * 128, width + p * 128 + 128)
                    k = kv[src, at]
                    prob = jnp.exp(dot_nt(k, qm_s[p]) - lse_ref[p : p + 1, :])
                    dprob = dot_nt(kv[src, vat], dom_s[p])
                    ds = (prob * (dprob - row_s[p : p + 1, :])).astype(BF16)
                    outs[half][dst, at] = dot_nn(ds, qm_s[p]).astype(BF16)
                    outs[half][dst, vat] = dot_nn(prob.astype(BF16), dom_s[p]).astype(BF16)
                    dq_s[p] += dot_tn(ds, k)

            each(count, sub_work)

    each(blocks, block_work)
    dq = jnp.concatenate([join_heads(dq_s[p]) for p in range(pairs)], axis=1) * SCALE
    dqp_ref[...] = rope_back(
        dq, wide(cos_ref[...], width), wide(sin_ref[...], width)
    ).astype(BF16)


def qkv_grad_kernel(
    n, nt, no, order_ref, a_ref, dqp_ref, dhid_ref, attn_ref, cos_ref, sin_ref, *rest
):
    terms = rest[:nt]
    chunks = rest[nt : nt + n]
    outs = rest[nt + n : nt + n + no]
    da_ref, w, acc, sems = rest[nt + n + no :]
    width = dqp_ref.shape[1]
    copies = weight_copies(order_ref, chunks, w, sems)
    dkv = terms[0][...].astype(F32)
    for term in terms[1:]:
        dkv = dkv + term[...].astype(F32)
    dkp = rope_back(
        dkv[:, :width], wide(cos_ref[...], width), wide(sin_ref[...], width)
    ).astype(BF16)
    d = jnp.concatenate([dqp_ref[...], dkp, dkv[:, width:].astype(BF16)], axis=1)
    for copy in copies:
        copy.wait()
    da_ref[...] = dot_nt(d, w[:, : 3 * width]).astype(BF16)
    acc[:, : 3 * width] = dot_tn(a_ref[...], d)
    acc[:, 3 * width :] = dot_tn(dhid_ref[...].astype(BF16), attn_ref[...])
    emit_blocks(order_ref, acc, outs)


def call(kernel, out_shape, specs, scratch, args):
    return pl.pallas_call(
        kernel,
        out_shape=out_shape,
        in_specs=specs,
        out_specs=jax.tree.map(lambda _: VM, out_shape),
        scratch_shapes=scratch,
    )(*args)


def rotary_tables(positions):
    half = HEAD_DIM // 2
    inverse = jnp.exp(jnp.arange(half, dtype=F32) * (-2.0 * math.log(THETA) / HEAD_DIM))
    angles = positions.astype(F32)[:, None] * inverse[None, :]
    angles = jnp.concatenate([angles] * 4, axis=-1)
    return jnp.cos(angles), jnp.sin(angles)


def adam_update(tensor, gradient, moment, second):
    moment = BETA_ONE * moment + (1.0 - BETA_ONE) * gradient
    second = BETA_TWO * second + (1.0 - BETA_TWO) * gradient * gradient
    first_hat = moment / (1.0 - BETA_ONE**STEP)
    second_hat = second / (1.0 - BETA_TWO**STEP)
    tensor = tensor - LEARN_RATE * (first_hat / (jnp.sqrt(second_hat) + ADAM_EPS) + DECAY * tensor)
    return tensor, moment, second


def adam_kernel(nf, width, units, w_ref, m_ref, v_ref, *rest):
    firsts, lasts = rest[:nf], rest[nf : 2 * nf]
    g_ref, w_out, m_out, v_out, gain_ref = rest[2 * nf :]
    one = total([term[...] for term in firsts])
    two = total([term[...] for term in lasts])[:, : 3 * units]
    w = w_ref[...]
    wf = w.astype(BF16).astype(F32)
    cut = 4 * width
    sums = [
        jnp.sum(wf[:, : 3 * width] * one[:, : 3 * width], axis=1, keepdims=True),
        jnp.sum(wf[:, cut : cut + 2 * units] * two[:, : 2 * units], axis=1, keepdims=True),
    ]
    lane = lax.broadcasted_iota(jnp.int32, gain_ref.shape, 1)
    gain_ref[...] = jnp.where(lane == 0, sums[0], jnp.where(lane == 1, sums[1], 0.0))
    grad = jnp.concatenate([one, two], axis=1)
    g_ref[...] = grad
    w_out[...], m_out[...], v_out[...] = adam_update(w, grad, m_ref[...], v_ref[...])


def head_swap(x):
    if lax.axis_size("head") == 1:
        return jnp.zeros_like(x)
    return swap(x, "head", 1)


def layer(
    inputs, cotangent, weights, gains, weight_moment, weight_second, gain_moment, gain_second
):
    heads = lax.axis_size("head")
    width = HEADS // heads * HEAD_DIM
    units = FF // heads
    toks, d = inputs.shape
    rows = weights.shape[0]
    n = lax.axis_size(TOKENS_AX)
    seq = toks * n
    me = lax.axis_index(TOKENS_AX).astype(jnp.int32)
    order = me.reshape(1)
    pairs = width // 128

    wb = weights.astype(BF16)
    gb = gains.astype(BF16)
    wq_cols = 4 * width + 128
    rest_pad = -(3 * units) % 128
    rest_cols = 3 * units + rest_pad
    w_first = jnp.concatenate([wb[:, : 4 * width], jnp.pad(gb.T, ((0, 0), (0, 126)))], axis=1)
    w_rest = jnp.pad(wb[:, 4 * width :], ((0, 0), (0, rest_pad)))
    first_chunks = gather(w_first)
    cos, sin = rotary_tables(me * toks + jnp.arange(toks, dtype=jnp.int32))

    nw = len(first_chunks)
    wsem = pltpu.SemaphoreType.DMA((nw,))
    halves = 2 if staged() else 1

    a, q, kv, g = call(
        partial(qkv_kernel, nw),
        [sds((toks, d), BF16), sds((toks, width), BF16), sds((toks, 2 * width), BF16), sds((8, d), F32)],
        [SM, VM, VM, VM] + [ANY] * nw,
        [pltpu.VMEM((d, wq_cols), BF16), wsem],
        [order, inputs, cos, sin] + first_chunks,
    )
    keys = gather(kv)
    rest_chunks = gather(w_rest)
    nk = len(keys)
    block_rows = min(KEY_ROWS, seq)
    blocks = seq // block_rows
    ksem = pltpu.SemaphoreType.DMA((nk,))

    attn, lse, out_part = call(
        partial(attend_kernel, nk, nw, blocks),
        [sds((toks, width), BF16), sds((8, 2 * toks), F32), sds((toks, d), BF16)],
        [SM, VM] + [ANY] * (nk + nw),
        [
            pltpu.VMEM((block_rows, 2 * width), BF16),
            pltpu.VMEM((d, width), BF16),
            pltpu.VMEM((pairs, 2 * toks, 1), F32),
            pltpu.VMEM((pairs, 2 * toks, 1), F32),
            pltpu.VMEM((pairs, 2 * toks, 128), F32),
            ksem,
            wsem,
        ],
        [order, q] + keys + first_chunks,
    )
    out_other = head_swap(out_part)

    hidden, ffn_part, db_part, b, dz, mixed = call(
        partial(ffn_kernel, nw),
        [
            sds((toks, d), F32),
            sds((toks, d), BF16),
            sds((toks, d), BF16),
            sds((toks, d), BF16),
            sds((toks, 2 * units), BF16),
            sds((toks, units), BF16),
        ],
        [SM] + [VM] * 5 + [ANY] * nw,
        [pltpu.VMEM((d, rest_cols), BF16), wsem],
        [order, inputs, out_part, out_other, cotangent, g] + rest_chunks,
    )
    db_other = head_swap(db_part)
    ffn_other = head_swap(ffn_part)
    outputs = hidden + (ffn_part.astype(F32) + ffn_other.astype(F32))
    ffn_grads = call(
        partial(ffn_grad_kernel, halves),
        [sds((d // halves, rest_cols), BF16)] * halves,
        [SM] + [VM] * 4,
        [pltpu.VMEM((d, rest_cols), F32)],
        [order, b, dz, cotangent, mixed],
    )
    ffn_terms = scatter_sum(ffn_grads)

    back = call(
        partial(attend_back_kernel, nk, nw, halves, blocks),
        [sds((seq // halves, 2 * width), BF16)] * halves
        + [sds((toks, d), F32), sds((toks, width), BF16)],
        [SM] + [VM] * 10 + [ANY] * (nk + nw),
        [
            pltpu.VMEM((block_rows, 2 * width), BF16),
            pltpu.VMEM((d, width), BF16),
            pltpu.VMEM((pairs, 2 * toks, 128), F32),
            pltpu.VMEM((pairs, 2 * toks, 128), BF16),
            pltpu.VMEM((pairs, 2 * toks, 128), BF16),
            pltpu.VMEM((8, 2 * toks), F32),
            ksem,
            wsem,
        ],
        [order, q, attn, lse, hidden, cotangent, g, db_part, db_other, cos, sin] + keys + first_chunks,
    )
    dhid, dqp = back[halves:]
    kv_terms = scatter_sum(back[:halves])
    nt = len(kv_terms)
    grads = call(
        partial(qkv_grad_kernel, nw, nt, halves),
        [sds((d // halves, 4 * width), BF16)] * halves + [sds((toks, d), BF16)],
        [SM] + [VM] * 6 + [VM] * nt + [ANY] * nw,
        [pltpu.VMEM((d, wq_cols), BF16), pltpu.VMEM((d, 4 * width), F32), wsem],
        [order, a, dqp, dhid, attn, cos, sin] + kv_terms + first_chunks,
    )
    da_part = grads[halves]
    da_other = head_swap(da_part)
    da = da_part.astype(F32) + da_other.astype(F32)
    xhat, inv = norm_parts(inputs)
    input_grad = dhid + norm_back(da, xhat, inv, g[0:1, :])

    first_terms = scatter_sum(grads[:halves])
    full = weights.shape
    weight_grad, new_weights, new_weight_moment, new_weight_second, gain_part = call(
        partial(adam_kernel, nt, width, units),
        [sds(full, F32)] * 4 + [sds((rows, 128), F32)],
        [VM] * (3 + 2 * nt),
        [],
        [weights, weight_moment, weight_second] + first_terms + ffn_terms,
    )
    gain_part = gain_part[:, :2].T
    gain_grad = (gain_part + head_swap(gain_part)) / gb.astype(F32)
    new_gains, new_gain_moment, new_gain_second = adam_update(
        gains, gain_grad, gain_moment, gain_second
    )
    return (
        outputs,
        input_grad,
        weight_grad,
        gain_grad,
        new_weights,
        new_weight_moment,
        new_weight_second,
        new_gains,
        new_gain_moment,
        new_gain_second,
    )


def solution(mesh):
    rows = P(("blk", "shard"), None)
    cells = P(("blk", "shard"), "head")
    lanes = P(None, ("blk", "shard"))
    return jax.shard_map(
        layer,
        mesh=mesh,
        in_specs=(rows, rows, cells, lanes, cells, cells, lanes, lanes),
        out_specs=(rows, rows, cells, lanes, cells, cells, cells, lanes, lanes, lanes),
        check_vma=False,
    )
```

```python
from functools import partial
import math

import jax
import jax.numpy as jnp
from jax import lax
from jax.experimental import pallas as pl
from jax.experimental.pallas import tpu as pltpu
from jax.sharding import PartitionSpec as P


HEADS = 12
HEAD_DIM = 64
FF = 1152
STEP = 3

NORM_EPS = 1e-05
THETA = 160000.0
BETA_ONE = 0.9
BETA_TWO = 0.98
LEARN_RATE = 0.2
ADAM_EPS = 1e-06
DECAY = 0.01
NEG_LARGE = -1e30
SCALE = 1.0 / math.sqrt(HEAD_DIM)
TOKENS_AX = ("blk", "shard")
F32 = jnp.float32
BF16 = jnp.bfloat16
KEY_ROWS = 2048
SUB_ROWS = 512


VM = pl.BlockSpec(memory_space=pltpu.VMEM)
SM = pl.BlockSpec(memory_space=pltpu.SMEM)
ANY = pl.BlockSpec(memory_space=pl.ANY)


def sds(shape, dtype):
    return jax.ShapeDtypeStruct(shape, dtype)


def dot_nn(a, b):
    return lax.dot_general(a, b, (((1,), (0,)), ((), ())), preferred_element_type=F32)


def dot_nt(a, b):
    return lax.dot_general(a, b, (((1,), (1,)), ((), ())), preferred_element_type=F32)


def dot_tn(a, b):
    return lax.dot_general(a, b, (((0,), (0,)), ((), ())), preferred_element_type=F32)


def swap(x, axis, bits):
    size = lax.axis_size(axis)
    return lax.ppermute(x, axis, [(i, i ^ bits) for i in range(size)])


def staged():
    return lax.axis_size("blk") == 4 and lax.axis_size("shard") == 4


def chunk_order():
    return [z * 4 + x * 2 + c for c in range(2) for x in range(2) for z in range(4)]


def gather(x):
    if not staged():
        return [lax.all_gather(x, TOKENS_AX, axis=0, tiled=True)]
    got = {0: x}
    got[8] = swap(x, "blk", 2)
    got[4] = swap(x, "blk", 1)
    got[12] = swap(got[8], "blk", 1)
    for z in range(4):
        got[z * 4 + 2] = swap(got[z * 4], "shard", 2)
    for z in range(4):
        for h in (0, 2):
            got[z * 4 + h + 1] = swap(got[z * 4 + h], "shard", 1)
    return [got[j] for j in chunk_order()]


def add_kernel(*refs):
    keep, recv = refs[0], refs[1]
    for i, out in enumerate(refs[2:]):
        rows = out.shape[0]
        at = pl.ds(i * rows, rows)
        out[...] = (keep[at, :].astype(F32) + recv[at, :].astype(F32)).astype(BF16)


def scatter_sum(parts):
    if not staged():
        return [lax.psum_scatter(parts[0], TOKENS_AX, scatter_dimension=0, tiled=True)]
    keep, send = parts
    rows, cols = keep.shape[0] // 8, keep.shape[1]
    recv = swap(send, "shard", 1)
    s = pl.pallas_call(
        add_kernel,
        out_shape=[sds((rows, cols), BF16)] * 8,
        in_specs=[VM, VM],
        out_specs=[VM] * 8,
        name="pair_add",
    )(keep, recv)
    got = {z: swap(s[4 + z], "shard", 2) for z in (3, 2, 1, 0)}

    def block(z, *more):
        return total([s[z], got[z], *more]).astype(BF16)

    far = swap(block(3), "blk", 1)
    two = swap(block(2, far), "blk", 2)
    one = swap(block(1), "blk", 1)
    return [s[0], got[0], one, two]


def total(terms):
    out = terms[0].astype(F32)
    for term in terms[1:]:
        out = out + term.astype(F32)
    return out


def weight_copies(order_ref, chunks, dst, sems, cols=None):
    rows = chunks[0].shape[0]
    copies = []
    for i, chunk in enumerate(chunks):
        src = chunk if cols is None else chunk.at[:, pl.ds(cols[0], cols[1])]
        if len(chunks) == 1:
            at = pl.ds(0, rows)
        else:
            at = pl.ds(pl.multiple_of((order_ref[0] ^ chunk_order()[i]) * rows, 16), rows)
        copies.append(pltpu.make_async_copy(src, dst.at[at, :], sems.at[i]))
    for copy in copies:
        copy.start()
    return copies


def emit_blocks(order_ref, acc, outs):
    if len(outs) == 1:
        outs[0][...] = acc[...].astype(BF16)
        return
    rows = outs[0].shape[0] // 8
    for i, j in enumerate(chunk_order()):
        at = pl.ds(pl.multiple_of((order_ref[0] ^ j) * rows, 8), rows)
        outs[i // 8][pl.ds((i % 8) * rows, rows), :] = acc[at, :].astype(BF16)


def norm_parts(v):
    centre = v - jnp.mean(v, axis=-1, keepdims=True)
    inv = lax.rsqrt(jnp.mean(centre * centre, axis=-1, keepdims=True) + NORM_EPS)
    return centre * inv, inv


def norm_back(u, xhat, inv, g):
    s = u * g
    return inv * (
        s
        - jnp.mean(s, axis=-1, keepdims=True)
        - xhat * jnp.mean(s * xhat, axis=-1, keepdims=True)
    )


def low_half(shape):
    lane = lax.broadcasted_iota(jnp.int32, shape, 1)
    return (lane & (HEAD_DIM - 1)) < HEAD_DIM // 2


def turn(u):
    width = u.shape[1]
    half = HEAD_DIM // 2
    left = pltpu.roll(u, width - half, 1)
    right = pltpu.roll(u, half, 1)
    return left, right, low_half(u.shape)


def rope(u, cos, sin):
    left, right, low = turn(u)
    return u * cos + jnp.where(low, -left, right) * sin


def rope_back(w, cos, sin):
    left, right, low = turn(w * sin)
    return w * cos + jnp.where(low, left, -right)


def wide(table, width):
    return jnp.concatenate([table] * (width // table.shape[1]), axis=1)


def two_heads(pair):
    lane = lax.broadcasted_iota(jnp.int32, pair.shape, 1)
    zero = jnp.zeros_like(pair)
    first = lane < HEAD_DIM
    return jnp.concatenate(
        [jnp.where(first, pair, zero), jnp.where(first, zero, pair)], axis=0
    )


def join_heads(both):
    rows = both.shape[0] // 2
    lane = lax.broadcasted_iota(jnp.int32, (rows, both.shape[1]), 1)
    return jnp.where(lane < HEAD_DIM, both[:rows], both[rows:])


def as_row(col):
    return jnp.transpose(jnp.broadcast_to(col, (col.shape[0], 128)))[0:1, :]


def qkv_kernel(n, order_ref, x_ref, cos_ref, sin_ref, *rest):
    chunks = rest[:n]
    a_ref, q_ref, kv_ref, g_ref, w, sems = rest[n:]
    width = q_ref.shape[1]
    copies = weight_copies(order_ref, chunks, w, sems)
    xhat, _ = norm_parts(x_ref[...])
    for copy in copies:
        copy.wait()
    row = lax.broadcasted_iota(jnp.int32, (8, 128), 0)
    lane = lax.broadcasted_iota(jnp.int32, (8, 128), 1)
    pick = jnp.where(row == lane, 1.0, 0.0).astype(BF16)
    g = dot_nt(pick, w[:, 4 * width : 4 * width + 128])
    g_ref[...] = g
    a = (xhat * g[0:1, :]).astype(BF16)
    a_ref[...] = a
    cos = wide(cos_ref[...], width)
    sin = wide(sin_ref[...], width)
    q_ref[...] = rope(dot_nn(a, w[:, :width]), cos, sin).astype(BF16)
    kv_ref[:, :width] = rope(dot_nn(a, w[:, width : 2 * width]), cos, sin).astype(BF16)
    kv_ref[:, width:] = dot_nn(a, w[:, 2 * width : 3 * width]).astype(BF16)


def key_copies(chunks, dst, sems, block):
    if len(chunks) == 1:
        rows = dst.shape[0]
        at = pl.ds(pl.multiple_of(block * rows, rows), rows)
        copies = [pltpu.make_async_copy(chunks[0].at[at, :], dst, sems.at[0])]
    else:
        rows = chunks[0].shape[0]
        copies = [
            pltpu.make_async_copy(chunk, dst.at[pl.ds(i * rows, rows), :], sems.at[i])
            for i, chunk in enumerate(chunks)
        ]
    for copy in copies:
        copy.start()
    return copies


def each(count, body):
    if count == 1:
        body(0)
    else:
        lax.fori_loop(0, count, lambda i, c: (body(i), c)[1], 0)


def attend_kernel(n, nw, blocks, order_ref, q_ref, *rest):
    keys = rest[:n]
    wos = rest[n : n + nw]
    attn_ref, lse_ref, out_ref, kv, wo, m_s, l_s, acc_s, ksem, wsem = rest[n + nw :]
    width = q_ref.shape[1]
    pairs = width // 128
    wcopies = weight_copies(order_ref, wos, wo, wsem, (3 * width, width))
    m_s[...] = jnp.full(m_s.shape, NEG_LARGE, F32)
    l_s[...] = jnp.zeros(l_s.shape, F32)
    acc_s[...] = jnp.zeros(acc_s.shape, F32)

    def block_work(block):
        for copy in key_copies(keys, kv, ksem, block):
            copy.wait()
        for p in range(pairs):
            at = slice(p * 128, p * 128 + 128)
            qm = two_heads(q_ref[:, at]) * jnp.asarray(SCALE, BF16)
            s = dot_nt(qm, kv[:, at])
            m_old = m_s[p]
            m_new = jnp.maximum(m_old, jnp.max(s, axis=1, keepdims=True))
            factor = jnp.exp(m_old - m_new)
            e = jnp.exp(s - m_new)
            l_s[p] = l_s[p] * factor + jnp.sum(e, axis=1, keepdims=True)
            m_s[p] = m_new
            acc_s[p] = acc_s[p] * factor + dot_nn(
                e.astype(BF16), kv[:, width + p * 128 : width + p * 128 + 128]
            )

    each(blocks, block_work)
    for p in range(pairs):
        attn_ref[:, p * 128 : p * 128 + 128] = join_heads(acc_s[p] / l_s[p]).astype(BF16)
        lse_ref[p : p + 1, :] = as_row(m_s[p] + jnp.log(l_s[p]))
    for copy in wcopies:
        copy.wait()
    out_ref[...] = dot_nt(attn_ref[...], wo[...]).astype(BF16)


def gelu_parts(z):
    cdf = 0.5 * (1.0 + lax.erf(z * 0.7071067811865476))
    density = jnp.exp(-0.5 * z * z) * 0.3989422804014327
    return z * cdf, cdf + z * density


def ffn_kernel(nw, order_ref, x_ref, pa_ref, pb_ref, cot_ref, g_ref, *rest):
    ws = rest[:nw]
    hid_ref, out_ref, db_ref, b_ref, dz_ref, mixed_ref, w, wsem = rest[nw:]
    units = mixed_ref.shape[1]
    copies = weight_copies(order_ref, ws, w, wsem)
    hidden = x_ref[...] + (pa_ref[...].astype(F32) + pb_ref[...].astype(F32))
    hid_ref[...] = hidden
    xhat, _ = norm_parts(hidden)
    b = (xhat * g_ref[1:2, :]).astype(BF16)
    b_ref[...] = b
    cb = cot_ref[...].astype(BF16)
    for copy in copies:
        copy.wait()
    z = dot_nn(b, w[:, : 2 * units])
    gate = z[:, units:]
    act, slope = gelu_parts(z[:, :units])
    dmix = dot_nn(cb, w[:, 2 * units : 3 * units])
    dz = jnp.concatenate([dmix * gate * slope, dmix * act], axis=1).astype(BF16)
    dz_ref[...] = dz
    db_ref[...] = dot_nt(dz, w[:, : 2 * units]).astype(BF16)
    mixed = (act * gate).astype(BF16)
    mixed_ref[...] = mixed
    out_ref[...] = dot_nt(mixed, w[:, 2 * units : 3 * units]).astype(BF16)


def ffn_grad_kernel(no, order_ref, b_ref, dz_ref, cot_ref, mixed_ref, *rest):
    outs, acc = rest[:no], rest[no]
    two = dz_ref.shape[1]
    acc[:, :two] = dot_tn(b_ref[...], dz_ref[...])
    half = mixed_ref.shape[1]
    acc[:, two : two + half] = dot_tn(cot_ref[...].astype(BF16), mixed_ref[...])
    acc[:, two + half :] = jnp.zeros((acc.shape[0], acc.shape[1] - two - half), F32)
    emit_blocks(order_ref, acc, outs)


def attend_back_kernel(
    n, nw, no, blocks, order_ref, q_ref, attn_ref, lse_ref, hid_ref, cot_ref, g_ref,
    da_ref, db_ref, cos_ref, sin_ref, *rest
):
    keys = rest[:n]
    wos = rest[n : n + nw]
    outs = rest[n + nw : n + nw + no]
    dhid_ref, dqp_ref, kv, wo, dq_s, qm_s, dom_s, row_s, ksem, wsem = rest[n + nw + no :]
    width = q_ref.shape[1]
    pairs = width // 128
    wcopies = weight_copies(order_ref, wos, wo, wsem, (3 * width, width))
    first = key_copies(keys, kv, ksem, 0) if blocks == 1 else None
    xhat, inv = norm_parts(hid_ref[...])
    db = da_ref[...].astype(F32) + db_ref[...].astype(F32)
    dhid = cot_ref[...] + norm_back(db, xhat, inv, g_ref[1:2, :])
    dhid_ref[...] = dhid
    for copy in wcopies:
        copy.wait()
    dattn = dot_nn(dhid.astype(BF16), wo[...]).astype(BF16)
    for p in range(pairs):
        at = slice(p * 128, p * 128 + 128)
        qm_s[p] = two_heads(q_ref[:, at]) * jnp.asarray(SCALE, BF16)
        dom = two_heads(dattn[:, at])
        dom_s[p] = dom
        both = jnp.concatenate([attn_ref[:, at]] * 2, axis=0)
        dots = jnp.sum(dom.astype(F32) * both.astype(F32), axis=1, keepdims=True)
        row_s[p : p + 1, :] = as_row(dots)
    dq_s[...] = jnp.zeros(dq_s.shape, F32)
    halves = len(outs)
    block_rows = kv.shape[0]

    def block_work(block):
        for copy in first or key_copies(keys, kv, ksem, block):
            copy.wait()
        for half in range(halves):
            count = block_rows // halves // SUB_ROWS

            def sub_work(sub):
                src = pl.ds(
                    pl.multiple_of(half * (block_rows // halves) + sub * SUB_ROWS, SUB_ROWS),
                    SUB_ROWS,
                )
                dst = pl.ds(
                    pl.multiple_of(block * block_rows + sub * SUB_ROWS, SUB_ROWS), SUB_ROWS
                )
                for p in range(pairs):
                    at = slice(p * 128, p * 128 + 128)
                    vat = slice(width + p * 128, width + p * 128 + 128)
                    k = kv[src, at]
                    prob = jnp.exp(dot_nt(k, qm_s[p]) - lse_ref[p : p + 1, :])
                    dprob = dot_nt(kv[src, vat], dom_s[p])
                    ds = (prob * (dprob - row_s[p : p + 1, :])).astype(BF16)
                    outs[half][dst, at] = dot_nn(ds, qm_s[p]).astype(BF16)
                    outs[half][dst, vat] = dot_nn(prob.astype(BF16), dom_s[p]).astype(BF16)
                    dq_s[p] += dot_tn(ds, k)

            each(count, sub_work)

    each(blocks, block_work)
    dq = jnp.concatenate([join_heads(dq_s[p]) for p in range(pairs)], axis=1) * SCALE
    dqp_ref[...] = rope_back(
        dq, wide(cos_ref[...], width), wide(sin_ref[...], width)
    ).astype(BF16)


def qkv_grad_kernel(
    n, nt, no, order_ref, a_ref, dqp_ref, dhid_ref, attn_ref, cos_ref, sin_ref, *rest
):
    terms = rest[:nt]
    chunks = rest[nt : nt + n]
    outs = rest[nt + n : nt + n + no]
    da_ref, w, acc, sems = rest[nt + n + no :]
    width = dqp_ref.shape[1]
    copies = weight_copies(order_ref, chunks, w, sems)
    dkv = terms[0][...].astype(F32)
    for term in terms[1:]:
        dkv = dkv + term[...].astype(F32)
    dkp = rope_back(
        dkv[:, :width], wide(cos_ref[...], width), wide(sin_ref[...], width)
    ).astype(BF16)
    d = jnp.concatenate([dqp_ref[...], dkp, dkv[:, width:].astype(BF16)], axis=1)
    for copy in copies:
        copy.wait()
    da_ref[...] = dot_nt(d, w[:, : 3 * width]).astype(BF16)
    acc[:, : 3 * width] = dot_tn(a_ref[...], d)
    acc[:, 3 * width :] = dot_tn(dhid_ref[...].astype(BF16), attn_ref[...])
    emit_blocks(order_ref, acc, outs)


def call(kernel, out_shape, specs, scratch, args):
    return pl.pallas_call(
        kernel,
        out_shape=out_shape,
        in_specs=specs,
        out_specs=jax.tree.map(lambda _: VM, out_shape),
        scratch_shapes=scratch,
    )(*args)


def rotary_tables(positions):
    half = HEAD_DIM // 2
    inverse = jnp.exp(jnp.arange(half, dtype=F32) * (-2.0 * math.log(THETA) / HEAD_DIM))
    angles = positions.astype(F32)[:, None] * inverse[None, :]
    angles = jnp.concatenate([angles] * 4, axis=-1)
    return jnp.cos(angles), jnp.sin(angles)


def adam_update(tensor, gradient, moment, second):
    moment = BETA_ONE * moment + (1.0 - BETA_ONE) * gradient
    second = BETA_TWO * second + (1.0 - BETA_TWO) * gradient * gradient
    first_hat = moment / (1.0 - BETA_ONE**STEP)
    second_hat = second / (1.0 - BETA_TWO**STEP)
    tensor = tensor - LEARN_RATE * (first_hat / (jnp.sqrt(second_hat) + ADAM_EPS) + DECAY * tensor)
    return tensor, moment, second


def gsum_kernel(nf, width, units, w_ref, *rest):
    firsts, lasts = rest[:nf], rest[nf : 2 * nf]
    g_ref, gain_ref = rest[2 * nf :]
    one = total([term[...] for term in firsts])
    two = total([term[...] for term in lasts])[:, : 3 * units]
    wf = w_ref[...].astype(BF16).astype(F32)
    cut = 4 * width
    sums = [
        jnp.sum(wf[:, : 3 * width] * one[:, : 3 * width], axis=1, keepdims=True),
        jnp.sum(wf[:, cut : cut + 2 * units] * two[:, : 2 * units], axis=1, keepdims=True),
    ]
    lane = lax.broadcasted_iota(jnp.int32, gain_ref.shape, 1)
    gain_ref[...] = jnp.where(lane == 0, sums[0], jnp.where(lane == 1, sums[1], 0.0))
    g_ref[:, :cut] = one
    g_ref[:, cut:] = two


def adam_kernel(w_ref, g_ref, m_ref, v_ref, w_out, m_out, v_out):
    w_out[...], m_out[...], v_out[...] = adam_update(
        w_ref[...], g_ref[...], m_ref[...], v_ref[...]
    )


def head_swap(x):
    if lax.axis_size("head") == 1:
        return jnp.zeros_like(x)
    return swap(x, "head", 1)


def layer(
    inputs, cotangent, weights, gains, weight_moment, weight_second, gain_moment, gain_second
):
    heads = lax.axis_size("head")
    width = HEADS // heads * HEAD_DIM
    units = FF // heads
    toks, d = inputs.shape
    rows = weights.shape[0]
    n = lax.axis_size(TOKENS_AX)
    seq = toks * n
    me = lax.axis_index(TOKENS_AX).astype(jnp.int32)
    order = me.reshape(1)
    pairs = width // 128

    wb = weights.astype(BF16)
    gb = gains.astype(BF16)
    wq_cols = 4 * width + 128
    rest_pad = -(3 * units) % 128
    rest_cols = 3 * units + rest_pad
    w_first = jnp.concatenate([wb[:, : 4 * width], jnp.pad(gb.T, ((0, 0), (0, 126)))], axis=1)
    w_rest = jnp.pad(wb[:, 4 * width :], ((0, 0), (0, rest_pad)))
    first_chunks = gather(w_first)
    cos, sin = rotary_tables(me * toks + jnp.arange(toks, dtype=jnp.int32))

    nw = len(first_chunks)
    wsem = pltpu.SemaphoreType.DMA((nw,))
    halves = 2 if staged() else 1

    a, q, kv, g = call(
        partial(qkv_kernel, nw),
        [sds((toks, d), BF16), sds((toks, width), BF16), sds((toks, 2 * width), BF16), sds((8, d), F32)],
        [SM, VM, VM, VM] + [ANY] * nw,
        [pltpu.VMEM((d, wq_cols), BF16), wsem],
        [order, inputs, cos, sin] + first_chunks,
    )
    keys = gather(kv)
    rest_chunks = gather(w_rest)
    nk = len(keys)
    block_rows = min(KEY_ROWS, seq)
    blocks = seq // block_rows
    ksem = pltpu.SemaphoreType.DMA((nk,))

    attn, lse, out_part = call(
        partial(attend_kernel, nk, nw, blocks),
        [sds((toks, width), BF16), sds((8, 2 * toks), F32), sds((toks, d), BF16)],
        [SM, VM] + [ANY] * (nk + nw),
        [
            pltpu.VMEM((block_rows, 2 * width), BF16),
            pltpu.VMEM((d, width), BF16),
            pltpu.VMEM((pairs, 2 * toks, 1), F32),
            pltpu.VMEM((pairs, 2 * toks, 1), F32),
            pltpu.VMEM((pairs, 2 * toks, 128), F32),
            ksem,
            wsem,
        ],
        [order, q] + keys + first_chunks,
    )
    out_other = head_swap(out_part)

    hidden, ffn_part, db_part, b, dz, mixed = call(
        partial(ffn_kernel, nw),
        [
            sds((toks, d), F32),
            sds((toks, d), BF16),
            sds((toks, d), BF16),
            sds((toks, d), BF16),
            sds((toks, 2 * units), BF16),
            sds((toks, units), BF16),
        ],
        [SM] + [VM] * 5 + [ANY] * nw,
        [pltpu.VMEM((d, rest_cols), BF16), wsem],
        [order, inputs, out_part, out_other, cotangent, g] + rest_chunks,
    )
    db_other = head_swap(db_part)
    ffn_other = head_swap(ffn_part)
    outputs = hidden + (ffn_part.astype(F32) + ffn_other.astype(F32))
    ffn_grads = call(
        partial(ffn_grad_kernel, halves),
        [sds((d // halves, rest_cols), BF16)] * halves,
        [SM] + [VM] * 4,
        [pltpu.VMEM((d, rest_cols), F32)],
        [order, b, dz, cotangent, mixed],
    )
    ffn_terms = scatter_sum(ffn_grads)

    back = call(
        partial(attend_back_kernel, nk, nw, halves, blocks),
        [sds((seq // halves, 2 * width), BF16)] * halves
        + [sds((toks, d), F32), sds((toks, width), BF16)],
        [SM] + [VM] * 10 + [ANY] * (nk + nw),
        [
            pltpu.VMEM((block_rows, 2 * width), BF16),
            pltpu.VMEM((d, width), BF16),
            pltpu.VMEM((pairs, 2 * toks, 128), F32),
            pltpu.VMEM((pairs, 2 * toks, 128), BF16),
            pltpu.VMEM((pairs, 2 * toks, 128), BF16),
            pltpu.VMEM((8, 2 * toks), F32),
            ksem,
            wsem,
        ],
        [order, q, attn, lse, hidden, cotangent, g, db_part, db_other, cos, sin] + keys + first_chunks,
    )
    dhid, dqp = back[halves:]
    kv_terms = scatter_sum(back[:halves])
    nt = len(kv_terms)
    grads = call(
        partial(qkv_grad_kernel, nw, nt, halves),
        [sds((d // halves, 4 * width), BF16)] * halves + [sds((toks, d), BF16)],
        [SM] + [VM] * 6 + [VM] * nt + [ANY] * nw,
        [pltpu.VMEM((d, wq_cols), BF16), pltpu.VMEM((d, 4 * width), F32), wsem],
        [order, a, dqp, dhid, attn, cos, sin] + kv_terms + first_chunks,
    )
    da_part = grads[halves]
    da_other = head_swap(da_part)
    da = da_part.astype(F32) + da_other.astype(F32)
    xhat, inv = norm_parts(inputs)
    input_grad = dhid + norm_back(da, xhat, inv, g[0:1, :])

    first_terms = scatter_sum(grads[:halves])
    full = weights.shape
    weight_grad, gain_part = call(
        partial(gsum_kernel, nt, width, units),
        [sds(full, F32), sds((rows, 128), F32)],
        [VM] * (1 + 2 * nt),
        [],
        [weights] + first_terms + ffn_terms,
    )
    gain_part = gain_part[:, :2].T
    gain_grad = (gain_part + head_swap(gain_part)) / gb.astype(F32)
    step_rows = 8 if rows % 8 == 0 else rows
    cells = pl.BlockSpec((step_rows, full[1]), lambda i: (i, 0))
    new_weights, new_weight_moment, new_weight_second = pl.pallas_call(
        adam_kernel,
        grid=(rows // step_rows,),
        out_shape=[sds(full, F32)] * 3,
        in_specs=[cells] * 4,
        out_specs=[cells] * 3,
        name="adam",
    )(weights, weight_grad, weight_moment, weight_second)
    new_gains, new_gain_moment, new_gain_second = adam_update(
        gains, gain_grad, gain_moment, gain_second
    )
    return (
        outputs,
        input_grad,
        weight_grad,
        gain_grad,
        new_weights,
        new_weight_moment,
        new_weight_second,
        new_gains,
        new_gain_moment,
        new_gain_second,
    )


def solution(mesh):
    rows = P(("blk", "shard"), None)
    cells = P(("blk", "shard"), "head")
    lanes = P(None, ("blk", "shard"))
    return jax.shard_map(
        layer,
        mesh=mesh,
        in_specs=(rows, rows, cells, lanes, cells, cells, lanes, lanes),
        out_specs=(rows, rows, cells, lanes, cells, cells, cells, lanes, lanes, lanes),
        check_vma=False,
    )
```

```python
from functools import partial
import math

import jax
import jax.numpy as jnp
from jax import lax
from jax.experimental import pallas as pl
from jax.experimental.pallas import tpu as pltpu
from jax.sharding import PartitionSpec as P


HEADS = 12
HEAD_DIM = 64
FF = 1152
STEP = 3

NORM_EPS = 1e-05
THETA = 160000.0
BETA_ONE = 0.9
BETA_TWO = 0.98
LEARN_RATE = 0.2
ADAM_EPS = 1e-06
DECAY = 0.01
NEG_LARGE = -1e30
SCALE = 1.0 / math.sqrt(HEAD_DIM)
TOKENS_AX = ("blk", "shard")
F32 = jnp.float32
BF16 = jnp.bfloat16
KEY_ROWS = 2048
SUB_ROWS = 512


VM = pl.BlockSpec(memory_space=pltpu.VMEM)
SM = pl.BlockSpec(memory_space=pltpu.SMEM)
ANY = pl.BlockSpec(memory_space=pl.ANY)


def sds(shape, dtype):
    return jax.ShapeDtypeStruct(shape, dtype)


def dot_nn(a, b):
    return lax.dot_general(a, b, (((1,), (0,)), ((), ())), preferred_element_type=F32)


def dot_nt(a, b):
    return lax.dot_general(a, b, (((1,), (1,)), ((), ())), preferred_element_type=F32)


def dot_tn(a, b):
    return lax.dot_general(a, b, (((0,), (0,)), ((), ())), preferred_element_type=F32)


def swap(x, axis, bits):
    size = lax.axis_size(axis)
    return lax.ppermute(x, axis, [(i, i ^ bits) for i in range(size)])


def staged():
    return lax.axis_size("blk") == 4 and lax.axis_size("shard") == 4


def chunk_order():
    return [z * 4 + x * 2 + c for c in range(2) for x in range(2) for z in range(4)]


def gather(x):
    if not staged():
        return [lax.all_gather(x, TOKENS_AX, axis=0, tiled=True)]
    got = {0: x}
    got[8] = swap(x, "blk", 2)
    got[4] = swap(x, "blk", 1)
    got[12] = swap(got[8], "blk", 1)
    for z in range(4):
        got[z * 4 + 2] = swap(got[z * 4], "shard", 2)
    for z in range(4):
        for h in (0, 2):
            got[z * 4 + h + 1] = swap(got[z * 4 + h], "shard", 1)
    return [got[j] for j in chunk_order()]


def add_kernel(*refs):
    keep, recv = refs[0], refs[1]
    for i, out in enumerate(refs[2:]):
        rows = out.shape[0]
        at = pl.ds(i * rows, rows)
        out[...] = (keep[at, :].astype(F32) + recv[at, :].astype(F32)).astype(BF16)


def scatter_sum(parts):
    if not staged():
        return [lax.psum_scatter(parts[0], TOKENS_AX, scatter_dimension=0, tiled=True)]
    keep, send = parts
    rows, cols = keep.shape[0] // 8, keep.shape[1]
    recv = swap(send, "shard", 1)
    s = pl.pallas_call(
        add_kernel,
        out_shape=[sds((rows, cols), BF16)] * 8,
        in_specs=[VM, VM],
        out_specs=[VM] * 8,
        name="pair_add",
    )(keep, recv)
    got = {z: swap(s[4 + z], "shard", 2) for z in (3, 2, 1, 0)}

    def block(z, *more):
        return total([s[z], got[z], *more]).astype(BF16)

    far = swap(block(3), "blk", 1)
    two = swap(block(2, far), "blk", 2)
    one = swap(block(1), "blk", 1)
    return [s[0], got[0], one, two]


def total(terms):
    out = terms[0].astype(F32)
    for term in terms[1:]:
        out = out + term.astype(F32)
    return out


def weight_copies(order_ref, chunks, dst, sems, cols=None):
    rows = chunks[0].shape[0]
    copies = []
    for i, chunk in enumerate(chunks):
        src = chunk if cols is None else chunk.at[:, pl.ds(cols[0], cols[1])]
        if len(chunks) == 1:
            at = pl.ds(0, rows)
        else:
            at = pl.ds(pl.multiple_of((order_ref[0] ^ chunk_order()[i]) * rows, 16), rows)
        copies.append(pltpu.make_async_copy(src, dst.at[at, :], sems.at[i]))
    for copy in copies:
        copy.start()
    return copies


def emit_blocks(order_ref, acc, outs):
    if len(outs) == 1:
        outs[0][...] = acc[...].astype(BF16)
        return
    rows = outs[0].shape[0] // 8
    for i, j in enumerate(chunk_order()):
        at = pl.ds(pl.multiple_of((order_ref[0] ^ j) * rows, 8), rows)
        outs[i // 8][pl.ds((i % 8) * rows, rows), :] = acc[at, :].astype(BF16)


def norm_parts(v):
    centre = v - jnp.mean(v, axis=-1, keepdims=True)
    inv = lax.rsqrt(jnp.mean(centre * centre, axis=-1, keepdims=True) + NORM_EPS)
    return centre * inv, inv


def norm_back(u, xhat, inv, g):
    s = u * g
    return inv * (
        s
        - jnp.mean(s, axis=-1, keepdims=True)
        - xhat * jnp.mean(s * xhat, axis=-1, keepdims=True)
    )


def low_half(shape):
    lane = lax.broadcasted_iota(jnp.int32, shape, 1)
    return (lane & (HEAD_DIM - 1)) < HEAD_DIM // 2


def turn(u):
    width = u.shape[1]
    half = HEAD_DIM // 2
    left = pltpu.roll(u, width - half, 1)
    right = pltpu.roll(u, half, 1)
    return left, right, low_half(u.shape)


def rope(u, cos, sin):
    left, right, low = turn(u)
    return u * cos + jnp.where(low, -left, right) * sin


def rope_back(w, cos, sin):
    left, right, low = turn(w * sin)
    return w * cos + jnp.where(low, left, -right)


def wide(table, width):
    return jnp.concatenate([table] * (width // table.shape[1]), axis=1)


def two_heads(pair):
    lane = lax.broadcasted_iota(jnp.int32, pair.shape, 1)
    zero = jnp.zeros_like(pair)
    first = lane < HEAD_DIM
    return jnp.concatenate(
        [jnp.where(first, pair, zero), jnp.where(first, zero, pair)], axis=0
    )


def join_heads(both):
    rows = both.shape[0] // 2
    lane = lax.broadcasted_iota(jnp.int32, (rows, both.shape[1]), 1)
    return jnp.where(lane < HEAD_DIM, both[:rows], both[rows:])


def as_row(col):
    return jnp.transpose(jnp.broadcast_to(col, (col.shape[0], 128)))[0:1, :]


def qkv_kernel(n, order_ref, x_ref, cos_ref, sin_ref, *rest):
    chunks = rest[:n]
    a_ref, q_ref, kv_ref, g_ref, w, sems = rest[n:]
    width = q_ref.shape[1]
    copies = weight_copies(order_ref, chunks, w, sems)
    xhat, _ = norm_parts(x_ref[...])
    for copy in copies:
        copy.wait()
    row = lax.broadcasted_iota(jnp.int32, (8, 128), 0)
    lane = lax.broadcasted_iota(jnp.int32, (8, 128), 1)
    pick = jnp.where(row == lane, 1.0, 0.0).astype(BF16)
    g = dot_nt(pick, w[:, 4 * width : 4 * width + 128])
    g_ref[...] = g
    a = (xhat * g[0:1, :]).astype(BF16)
    a_ref[...] = a
    cos = wide(cos_ref[...], width)
    sin = wide(sin_ref[...], width)
    q_ref[...] = rope(dot_nn(a, w[:, :width]), cos, sin).astype(BF16)
    kv_ref[:, :width] = rope(dot_nn(a, w[:, width : 2 * width]), cos, sin).astype(BF16)
    kv_ref[:, width:] = dot_nn(a, w[:, 2 * width : 3 * width]).astype(BF16)


def key_copies(chunks, dst, sems, block):
    if len(chunks) == 1:
        rows = dst.shape[0]
        at = pl.ds(pl.multiple_of(block * rows, rows), rows)
        copies = [pltpu.make_async_copy(chunks[0].at[at, :], dst, sems.at[0])]
    else:
        rows = chunks[0].shape[0]
        copies = [
            pltpu.make_async_copy(chunk, dst.at[pl.ds(i * rows, rows), :], sems.at[i])
            for i, chunk in enumerate(chunks)
        ]
    for copy in copies:
        copy.start()
    return copies


def each(count, body):
    if count == 1:
        body(0)
    else:
        lax.fori_loop(0, count, lambda i, c: (body(i), c)[1], 0)


def attend_kernel(n, nw, blocks, order_ref, q_ref, *rest):
    keys = rest[:n]
    wos = rest[n : n + nw]
    attn_ref, lse_ref, out_ref, kv, wo, m_s, l_s, acc_s, ksem, wsem = rest[n + nw :]
    width = q_ref.shape[1]
    pairs = width // 128
    wcopies = weight_copies(order_ref, wos, wo, wsem, (3 * width, width))
    m_s[...] = jnp.full(m_s.shape, NEG_LARGE, F32)
    l_s[...] = jnp.zeros(l_s.shape, F32)
    acc_s[...] = jnp.zeros(acc_s.shape, F32)

    def block_work(block):
        for copy in key_copies(keys, kv, ksem, block):
            copy.wait()
        for p in range(pairs):
            at = slice(p * 128, p * 128 + 128)
            qm = two_heads(q_ref[:, at]) * jnp.asarray(SCALE, BF16)
            s = dot_nt(qm, kv[:, at])
            m_old = m_s[p]
            m_new = jnp.maximum(m_old, jnp.max(s, axis=1, keepdims=True))
            factor = jnp.exp(m_old - m_new)
            e = jnp.exp(s - m_new)
            l_s[p] = l_s[p] * factor + jnp.sum(e, axis=1, keepdims=True)
            m_s[p] = m_new
            acc_s[p] = acc_s[p] * factor + dot_nn(
                e.astype(BF16), kv[:, width + p * 128 : width + p * 128 + 128]
            )

    each(blocks, block_work)
    for p in range(pairs):
        attn_ref[:, p * 128 : p * 128 + 128] = join_heads(acc_s[p] / l_s[p]).astype(BF16)
        lse_ref[p : p + 1, :] = as_row(m_s[p] + jnp.log(l_s[p]))
    for copy in wcopies:
        copy.wait()
    out_ref[...] = dot_nt(attn_ref[...], wo[...]).astype(BF16)


def gelu_parts(z):
    cdf = 0.5 * (1.0 + lax.erf(z * 0.7071067811865476))
    density = jnp.exp(-0.5 * z * z) * 0.3989422804014327
    return z * cdf, cdf + z * density


def ffn_kernel(nw, order_ref, x_ref, pa_ref, pb_ref, cot_ref, g_ref, *rest):
    ws = rest[:nw]
    hid_ref, out_ref, db_ref, b_ref, dz_ref, mixed_ref, w, wsem = rest[nw:]
    units = mixed_ref.shape[1]
    copies = weight_copies(order_ref, ws, w, wsem)
    hidden = x_ref[...] + (pa_ref[...].astype(F32) + pb_ref[...].astype(F32))
    hid_ref[...] = hidden
    xhat, _ = norm_parts(hidden)
    b = (xhat * g_ref[1:2, :]).astype(BF16)
    b_ref[...] = b
    cb = cot_ref[...].astype(BF16)
    for copy in copies:
        copy.wait()
    z = dot_nn(b, w[:, : 2 * units])
    gate = z[:, units:]
    act, slope = gelu_parts(z[:, :units])
    dmix = dot_nn(cb, w[:, 2 * units : 3 * units])
    dz = jnp.concatenate([dmix * gate * slope, dmix * act], axis=1).astype(BF16)
    dz_ref[...] = dz
    db_ref[...] = dot_nt(dz, w[:, : 2 * units]).astype(BF16)
    mixed = (act * gate).astype(BF16)
    mixed_ref[...] = mixed
    out_ref[...] = dot_nt(mixed, w[:, 2 * units : 3 * units]).astype(BF16)


def ffn_grad_kernel(no, order_ref, b_ref, dz_ref, cot_ref, mixed_ref, *rest):
    outs, acc = rest[:no], rest[no]
    two = dz_ref.shape[1]
    acc[:, :two] = dot_tn(b_ref[...], dz_ref[...])
    half = mixed_ref.shape[1]
    acc[:, two : two + half] = dot_tn(cot_ref[...].astype(BF16), mixed_ref[...])
    acc[:, two + half :] = jnp.zeros((acc.shape[0], acc.shape[1] - two - half), F32)
    emit_blocks(order_ref, acc, outs)


def attend_back_kernel(
    n, nw, no, blocks, order_ref, q_ref, attn_ref, lse_ref, hid_ref, cot_ref, g_ref,
    da_ref, db_ref, cos_ref, sin_ref, *rest
):
    keys = rest[:n]
    wos = rest[n : n + nw]
    outs = rest[n + nw : n + nw + no]
    dhid_ref, dqp_ref, kv, wo, dq_s, qm_s, dom_s, row_s, ksem, wsem = rest[n + nw + no :]
    width = q_ref.shape[1]
    pairs = width // 128
    wcopies = weight_copies(order_ref, wos, wo, wsem, (3 * width, width))
    first = key_copies(keys, kv, ksem, 0) if blocks == 1 else None
    xhat, inv = norm_parts(hid_ref[...])
    db = da_ref[...].astype(F32) + db_ref[...].astype(F32)
    dhid = cot_ref[...] + norm_back(db, xhat, inv, g_ref[1:2, :])
    dhid_ref[...] = dhid
    for copy in wcopies:
        copy.wait()
    dattn = dot_nn(dhid.astype(BF16), wo[...]).astype(BF16)
    for p in range(pairs):
        at = slice(p * 128, p * 128 + 128)
        qm_s[p] = two_heads(q_ref[:, at]) * jnp.asarray(SCALE, BF16)
        dom = two_heads(dattn[:, at])
        dom_s[p] = dom
        both = jnp.concatenate([attn_ref[:, at]] * 2, axis=0)
        dots = jnp.sum(dom.astype(F32) * both.astype(F32), axis=1, keepdims=True)
        row_s[p : p + 1, :] = as_row(dots)
    dq_s[...] = jnp.zeros(dq_s.shape, F32)
    halves = len(outs)
    block_rows = kv.shape[0]

    def block_work(block):
        for copy in first or key_copies(keys, kv, ksem, block):
            copy.wait()
        for half in range(halves):
            count = block_rows // halves // SUB_ROWS

            def sub_work(sub):
                src = pl.ds(
                    pl.multiple_of(half * (block_rows // halves) + sub * SUB_ROWS, SUB_ROWS),
                    SUB_ROWS,
                )
                dst = pl.ds(
                    pl.multiple_of(block * block_rows + sub * SUB_ROWS, SUB_ROWS), SUB_ROWS
                )
                for p in range(pairs):
                    at = slice(p * 128, p * 128 + 128)
                    vat = slice(width + p * 128, width + p * 128 + 128)
                    k = kv[src, at]
                    prob = jnp.exp(dot_nt(k, qm_s[p]) - lse_ref[p : p + 1, :])
                    dprob = dot_nt(kv[src, vat], dom_s[p])
                    ds = (prob * (dprob - row_s[p : p + 1, :])).astype(BF16)
                    outs[half][dst, at] = dot_nn(ds, qm_s[p]).astype(BF16)
                    outs[half][dst, vat] = dot_nn(prob.astype(BF16), dom_s[p]).astype(BF16)
                    dq_s[p] += dot_tn(ds, k)

            each(count, sub_work)

    each(blocks, block_work)
    dq = jnp.concatenate([join_heads(dq_s[p]) for p in range(pairs)], axis=1) * SCALE
    dqp_ref[...] = rope_back(
        dq, wide(cos_ref[...], width), wide(sin_ref[...], width)
    ).astype(BF16)


def qkv_grad_kernel(
    n, nt, no, order_ref, a_ref, dqp_ref, dhid_ref, attn_ref, cos_ref, sin_ref, *rest
):
    terms = rest[:nt]
    chunks = rest[nt : nt + n]
    outs = rest[nt + n : nt + n + no]
    da_ref, w, acc, sems = rest[nt + n + no :]
    width = dqp_ref.shape[1]
    copies = weight_copies(order_ref, chunks, w, sems)
    dkv = terms[0][...].astype(F32)
    for term in terms[1:]:
        dkv = dkv + term[...].astype(F32)
    dkp = rope_back(
        dkv[:, :width], wide(cos_ref[...], width), wide(sin_ref[...], width)
    ).astype(BF16)
    d = jnp.concatenate([dqp_ref[...], dkp, dkv[:, width:].astype(BF16)], axis=1)
    for copy in copies:
        copy.wait()
    da_ref[...] = dot_nt(d, w[:, : 3 * width]).astype(BF16)
    acc[:, : 3 * width] = dot_tn(a_ref[...], d)
    acc[:, 3 * width :] = dot_tn(dhid_ref[...].astype(BF16), attn_ref[...])
    emit_blocks(order_ref, acc, outs)


def call(kernel, out_shape, specs, scratch, args):
    return pl.pallas_call(
        kernel,
        out_shape=out_shape,
        in_specs=specs,
        out_specs=jax.tree.map(lambda _: VM, out_shape),
        scratch_shapes=scratch,
    )(*args)


def rotary_tables(positions):
    half = HEAD_DIM // 2
    inverse = jnp.exp(jnp.arange(half, dtype=F32) * (-2.0 * math.log(THETA) / HEAD_DIM))
    angles = positions.astype(F32)[:, None] * inverse[None, :]
    angles = jnp.concatenate([angles] * 4, axis=-1)
    return jnp.cos(angles), jnp.sin(angles)


def adam_update(tensor, gradient, moment, second):
    moment = BETA_ONE * moment + (1.0 - BETA_ONE) * gradient
    second = BETA_TWO * second + (1.0 - BETA_TWO) * gradient * gradient
    first_hat = moment / (1.0 - BETA_ONE**STEP)
    second_hat = second / (1.0 - BETA_TWO**STEP)
    tensor = tensor - LEARN_RATE * (first_hat / (jnp.sqrt(second_hat) + ADAM_EPS) + DECAY * tensor)
    return tensor, moment, second


def gsum_kernel(nf, width, units, w_ref, *rest):
    firsts, lasts = rest[:nf], rest[nf : 2 * nf]
    g_ref, gain_ref = rest[2 * nf :]
    one = total([term[...] for term in firsts])
    two = total([term[...] for term in lasts])[:, : 3 * units]
    wf = w_ref[...].astype(BF16).astype(F32)
    cut = 4 * width
    sums = [
        jnp.sum(wf[:, : 3 * width] * one[:, : 3 * width], axis=1, keepdims=True),
        jnp.sum(wf[:, cut : cut + 2 * units] * two[:, : 2 * units], axis=1, keepdims=True),
    ]
    lane = lax.broadcasted_iota(jnp.int32, (wf.shape[0], 128), 1)
    cols = jnp.where(lane == 0, sums[0], jnp.where(lane == 1, sums[1], 0.0))
    gain_ref[...] = jnp.transpose(cols)[:2, :]
    g_ref[:, :cut] = one
    g_ref[:, cut:] = two


def adam_kernel(w_ref, g_ref, m_ref, v_ref, w_out, m_out, v_out):
    w_out[...], m_out[...], v_out[...] = adam_update(
        w_ref[...], g_ref[...], m_ref[...], v_ref[...]
    )


def gadam_kernel(a_ref, b_ref, w_ref, m_ref, v_ref, g_out, w_out, m_out, v_out):
    w = w_ref[...]
    grad = (a_ref[...] + b_ref[...]) / w.astype(BF16).astype(F32)
    g_out[...] = grad
    w_out[...], m_out[...], v_out[...] = adam_update(w, grad, m_ref[...], v_ref[...])


def lnback_kernel(x_ref, da_ref, db_ref, dhid_ref, g_ref, out_ref):
    xhat, inv = norm_parts(x_ref[...])
    da = da_ref[...].astype(F32) + db_ref[...].astype(F32)
    out_ref[...] = dhid_ref[...] + norm_back(da, xhat, inv, g_ref[0:1, :])


def head_swap(x):
    if lax.axis_size("head") == 1:
        return jnp.zeros_like(x)
    return swap(x, "head", 1)


def layer(
    inputs, cotangent, weights, gains, weight_moment, weight_second, gain_moment, gain_second
):
    heads = lax.axis_size("head")
    width = HEADS // heads * HEAD_DIM
    units = FF // heads
    toks, d = inputs.shape
    rows = weights.shape[0]
    n = lax.axis_size(TOKENS_AX)
    seq = toks * n
    me = lax.axis_index(TOKENS_AX).astype(jnp.int32)
    order = me.reshape(1)
    pairs = width // 128

    wb = weights.astype(BF16)
    gb = gains.astype(BF16)
    wq_cols = 4 * width + 128
    rest_pad = -(3 * units) % 128
    rest_cols = 3 * units + rest_pad
    w_first = jnp.concatenate([wb[:, : 4 * width], jnp.pad(gb.T, ((0, 0), (0, 126)))], axis=1)
    w_rest = jnp.pad(wb[:, 4 * width :], ((0, 0), (0, rest_pad)))
    first_chunks = gather(w_first)
    cos, sin = rotary_tables(me * toks + jnp.arange(toks, dtype=jnp.int32))

    nw = len(first_chunks)
    wsem = pltpu.SemaphoreType.DMA((nw,))
    halves = 2 if staged() else 1

    a, q, kv, g = call(
        partial(qkv_kernel, nw),
        [sds((toks, d), BF16), sds((toks, width), BF16), sds((toks, 2 * width), BF16), sds((8, d), F32)],
        [SM, VM, VM, VM] + [ANY] * nw,
        [pltpu.VMEM((d, wq_cols), BF16), wsem],
        [order, inputs, cos, sin] + first_chunks,
    )
    keys = gather(kv)
    rest_chunks = gather(w_rest)
    nk = len(keys)
    block_rows = min(KEY_ROWS, seq)
    blocks = seq // block_rows
    ksem = pltpu.SemaphoreType.DMA((nk,))

    attn, lse, out_part = call(
        partial(attend_kernel, nk, nw, blocks),
        [sds((toks, width), BF16), sds((8, 2 * toks), F32), sds((toks, d), BF16)],
        [SM, VM] + [ANY] * (nk + nw),
        [
            pltpu.VMEM((block_rows, 2 * width), BF16),
            pltpu.VMEM((d, width), BF16),
            pltpu.VMEM((pairs, 2 * toks, 1), F32),
            pltpu.VMEM((pairs, 2 * toks, 1), F32),
            pltpu.VMEM((pairs, 2 * toks, 128), F32),
            ksem,
            wsem,
        ],
        [order, q] + keys + first_chunks,
    )
    out_other = head_swap(out_part)

    hidden, ffn_part, db_part, b, dz, mixed = call(
        partial(ffn_kernel, nw),
        [
            sds((toks, d), F32),
            sds((toks, d), BF16),
            sds((toks, d), BF16),
            sds((toks, d), BF16),
            sds((toks, 2 * units), BF16),
            sds((toks, units), BF16),
        ],
        [SM] + [VM] * 5 + [ANY] * nw,
        [pltpu.VMEM((d, rest_cols), BF16), wsem],
        [order, inputs, out_part, out_other, cotangent, g] + rest_chunks,
    )
    db_other = head_swap(db_part)
    ffn_other = head_swap(ffn_part)
    outputs = hidden + (ffn_part.astype(F32) + ffn_other.astype(F32))
    ffn_grads = call(
        partial(ffn_grad_kernel, halves),
        [sds((d // halves, rest_cols), BF16)] * halves,
        [SM] + [VM] * 4,
        [pltpu.VMEM((d, rest_cols), F32)],
        [order, b, dz, cotangent, mixed],
    )
    ffn_terms = scatter_sum(ffn_grads)

    back = call(
        partial(attend_back_kernel, nk, nw, halves, blocks),
        [sds((seq // halves, 2 * width), BF16)] * halves
        + [sds((toks, d), F32), sds((toks, width), BF16)],
        [SM] + [VM] * 10 + [ANY] * (nk + nw),
        [
            pltpu.VMEM((block_rows, 2 * width), BF16),
            pltpu.VMEM((d, width), BF16),
            pltpu.VMEM((pairs, 2 * toks, 128), F32),
            pltpu.VMEM((pairs, 2 * toks, 128), BF16),
            pltpu.VMEM((pairs, 2 * toks, 128), BF16),
            pltpu.VMEM((8, 2 * toks), F32),
            ksem,
            wsem,
        ],
        [order, q, attn, lse, hidden, cotangent, g, db_part, db_other, cos, sin] + keys + first_chunks,
    )
    dhid, dqp = back[halves:]
    kv_terms = scatter_sum(back[:halves])
    nt = len(kv_terms)
    grads = call(
        partial(qkv_grad_kernel, nw, nt, halves),
        [sds((d // halves, 4 * width), BF16)] * halves + [sds((toks, d), BF16)],
        [SM] + [VM] * 6 + [VM] * nt + [ANY] * nw,
        [pltpu.VMEM((d, wq_cols), BF16), pltpu.VMEM((d, 4 * width), F32), wsem],
        [order, a, dqp, dhid, attn, cos, sin] + kv_terms + first_chunks,
    )
    da_part = grads[halves]
    da_other = head_swap(da_part)
    (input_grad,) = call(
        lnback_kernel, [sds((toks, d), F32)], [VM] * 5, [], [inputs, da_part, da_other, dhid, g]
    )

    first_terms = scatter_sum(grads[:halves])
    full = weights.shape
    weight_grad, gain_part = call(
        partial(gsum_kernel, nt, width, units),
        [sds(full, F32), sds(gains.shape, F32)],
        [VM] * (1 + 2 * nt),
        [],
        [weights] + first_terms + ffn_terms,
    )
    gain_other = head_swap(gain_part)
    step_rows = rows // 2 if rows % 16 == 0 else rows
    cells = pl.BlockSpec((step_rows, full[1]), lambda i: (i, 0))
    new_weights, new_weight_moment, new_weight_second = pl.pallas_call(
        adam_kernel,
        grid=(rows // step_rows,),
        out_shape=[sds(full, F32)] * 3,
        in_specs=[cells] * 4,
        out_specs=[cells] * 3,
        name="adam",
    )(weights, weight_grad, weight_moment, weight_second)
    gain_grad, new_gains, new_gain_moment, new_gain_second = call(
        gadam_kernel,
        [sds(gains.shape, F32)] * 4,
        [VM] * 5,
        [],
        [gain_part, gain_other, gains, gain_moment, gain_second],
    )
    return (
        outputs,
        input_grad,
        weight_grad,
        gain_grad,
        new_weights,
        new_weight_moment,
        new_weight_second,
        new_gains,
        new_gain_moment,
        new_gain_second,
    )


def solution(mesh):
    rows = P(("blk", "shard"), None)
    cells = P(("blk", "shard"), "head")
    lanes = P(None, ("blk", "shard"))
    return jax.shard_map(
        layer,
        mesh=mesh,
        in_specs=(rows, rows, cells, lanes, cells, cells, lanes, lanes),
        out_specs=(rows, rows, cells, lanes, cells, cells, cells, lanes, lanes, lanes),
        check_vma=False,
    )
```

```python
from functools import partial
import math

import jax
import jax.numpy as jnp
from jax import lax
from jax.experimental import pallas as pl
from jax.experimental.pallas import tpu as pltpu
from jax.sharding import PartitionSpec as P


HEADS = 12
HEAD_DIM = 64
FF = 1152
STEP = 3

NORM_EPS = 1e-05
THETA = 160000.0
BETA_ONE = 0.9
BETA_TWO = 0.98
LEARN_RATE = 0.2
ADAM_EPS = 1e-06
DECAY = 0.01
NEG_LARGE = -1e30
SCALE = 1.0 / math.sqrt(HEAD_DIM)
TOKENS_AX = ("blk", "shard")
F32 = jnp.float32
BF16 = jnp.bfloat16
KEY_ROWS = 2048
SUB_ROWS = 512


VM = pl.BlockSpec(memory_space=pltpu.VMEM)
SM = pl.BlockSpec(memory_space=pltpu.SMEM)
ANY = pl.BlockSpec(memory_space=pl.ANY)


def sds(shape, dtype):
    return jax.ShapeDtypeStruct(shape, dtype)


def dot_nn(a, b):
    return lax.dot_general(a, b, (((1,), (0,)), ((), ())), preferred_element_type=F32)


def dot_nt(a, b):
    return lax.dot_general(a, b, (((1,), (1,)), ((), ())), preferred_element_type=F32)


def dot_tn(a, b):
    return lax.dot_general(a, b, (((0,), (0,)), ((), ())), preferred_element_type=F32)


def swap(x, axis, bits):
    size = lax.axis_size(axis)
    return lax.ppermute(x, axis, [(i, i ^ bits) for i in range(size)])


def staged():
    return lax.axis_size("blk") == 4 and lax.axis_size("shard") == 4


def chunk_order():
    return [z * 4 + x * 2 + c for c in range(2) for x in range(2) for z in range(4)]


def gather(x):
    if not staged():
        return [lax.all_gather(x, TOKENS_AX, axis=0, tiled=True)]
    got = {0: x}
    got[8] = swap(x, "blk", 2)
    got[4] = swap(x, "blk", 1)
    got[12] = swap(got[8], "blk", 1)
    for z in range(4):
        got[z * 4 + 2] = swap(got[z * 4], "shard", 2)
    for z in range(4):
        for h in (0, 2):
            got[z * 4 + h + 1] = swap(got[z * 4 + h], "shard", 1)
    return [got[j] for j in chunk_order()]


def add_kernel(*refs):
    keep, recv = refs[0], refs[1]
    for i, out in enumerate(refs[2:]):
        rows = out.shape[0]
        at = pl.ds(i * rows, rows)
        out[...] = (keep[at, :].astype(F32) + recv[at, :].astype(F32)).astype(BF16)


def pair_sum(keep, send):
    rows, cols = keep.shape[0] // 8, keep.shape[1]
    recv = swap(send, "shard", 1)
    return pl.pallas_call(
        add_kernel,
        out_shape=[sds((rows, cols), BF16)] * 8,
        in_specs=[VM, VM],
        out_specs=[VM] * 8,
        name="pair_add",
    )(keep, recv)


def native_sum(part):
    return [lax.psum_scatter(part, TOKENS_AX, scatter_dimension=0, tiled=True)]


def scatter_sum(s):
    got = {z: swap(s[4 + z], "shard", 2) for z in (3, 2, 1, 0)}

    def block(z, *more):
        return total([s[z], got[z], *more]).astype(BF16)

    far = swap(block(3), "blk", 1)
    two = swap(block(2, far), "blk", 2)
    one = swap(block(1), "blk", 1)
    return [s[0], got[0], one, two]


def total(terms):
    out = terms[0].astype(F32)
    for term in terms[1:]:
        out = out + term.astype(F32)
    return out


def weight_copies(order_ref, chunks, dst, sems, cols=None):
    rows = chunks[0].shape[0]
    copies = []
    for i, chunk in enumerate(chunks):
        src = chunk if cols is None else chunk.at[:, pl.ds(cols[0], cols[1])]
        if len(chunks) == 1:
            at = pl.ds(0, rows)
        else:
            at = pl.ds(pl.multiple_of((order_ref[0] ^ chunk_order()[i]) * rows, 16), rows)
        copies.append(pltpu.make_async_copy(src, dst.at[at, :], sems.at[i]))
    for copy in copies:
        copy.start()
    return copies


def emit_blocks(order_ref, acc, outs):
    if len(outs) == 1:
        outs[0][...] = acc[...].astype(BF16)
        return
    rows = outs[0].shape[0] // 8
    for i, j in enumerate(chunk_order()):
        at = pl.ds(pl.multiple_of((order_ref[0] ^ j) * rows, 8), rows)
        outs[i // 8][pl.ds((i % 8) * rows, rows), :] = acc[at, :].astype(BF16)


def norm_parts(v):
    centre = v - jnp.mean(v, axis=-1, keepdims=True)
    inv = lax.rsqrt(jnp.mean(centre * centre, axis=-1, keepdims=True) + NORM_EPS)
    return centre * inv, inv


def norm_back(u, xhat, inv, g):
    s = u * g
    return inv * (
        s
        - jnp.mean(s, axis=-1, keepdims=True)
        - xhat * jnp.mean(s * xhat, axis=-1, keepdims=True)
    )


def low_half(shape):
    lane = lax.broadcasted_iota(jnp.int32, shape, 1)
    return (lane & (HEAD_DIM - 1)) < HEAD_DIM // 2


def turn(u):
    width = u.shape[1]
    half = HEAD_DIM // 2
    left = pltpu.roll(u, width - half, 1)
    right = pltpu.roll(u, half, 1)
    return left, right, low_half(u.shape)


def rope(u, cos, sin):
    left, right, low = turn(u)
    return u * cos + jnp.where(low, -left, right) * sin


def rope_back(w, cos, sin):
    left, right, low = turn(w * sin)
    return w * cos + jnp.where(low, left, -right)


def wide(table, width):
    return jnp.concatenate([table] * (width // table.shape[1]), axis=1)


def two_heads(pair):
    lane = lax.broadcasted_iota(jnp.int32, pair.shape, 1)
    zero = jnp.zeros_like(pair)
    first = lane < HEAD_DIM
    return jnp.concatenate(
        [jnp.where(first, pair, zero), jnp.where(first, zero, pair)], axis=0
    )


def join_heads(both):
    rows = both.shape[0] // 2
    lane = lax.broadcasted_iota(jnp.int32, (rows, both.shape[1]), 1)
    return jnp.where(lane < HEAD_DIM, both[:rows], both[rows:])


def as_row(col):
    return jnp.transpose(jnp.broadcast_to(col, (col.shape[0], 128)))[0:1, :]


def qkv_kernel(n, order_ref, x_ref, cos_ref, sin_ref, *rest):
    chunks = rest[:n]
    at_ref, q_ref, kv_ref, g_ref, w, sems = rest[n:]
    width = q_ref.shape[1]
    copies = weight_copies(order_ref, chunks, w, sems)
    xhat, _ = norm_parts(x_ref[...])
    for copy in copies:
        copy.wait()
    row = lax.broadcasted_iota(jnp.int32, (8, 128), 0)
    lane = lax.broadcasted_iota(jnp.int32, (8, 128), 1)
    pick = jnp.where(row == lane, 1.0, 0.0).astype(BF16)
    g = dot_nt(pick, w[:, 4 * width : 4 * width + 128])
    g_ref[...] = g
    a = (xhat * g[0:1, :]).astype(BF16)
    at_ref[...] = jnp.transpose(a)
    cos = wide(cos_ref[...], width)
    sin = wide(sin_ref[...], width)
    q_ref[...] = rope(dot_nn(a, w[:, :width]), cos, sin).astype(BF16)
    kv_ref[:, :width] = rope(dot_nn(a, w[:, width : 2 * width]), cos, sin).astype(BF16)
    kv_ref[:, width:] = dot_nn(a, w[:, 2 * width : 3 * width]).astype(BF16)


def key_copies(chunks, dst, sems, block):
    if len(chunks) == 1:
        rows = dst.shape[0]
        at = pl.ds(pl.multiple_of(block * rows, rows), rows)
        copies = [pltpu.make_async_copy(chunks[0].at[at, :], dst, sems.at[0])]
    else:
        rows = chunks[0].shape[0]
        copies = [
            pltpu.make_async_copy(chunk, dst.at[pl.ds(i * rows, rows), :], sems.at[i])
            for i, chunk in enumerate(chunks)
        ]
    for copy in copies:
        copy.start()
    return copies


def each(count, body):
    if count == 1:
        body(0)
    else:
        lax.fori_loop(0, count, lambda i, c: (body(i), c)[1], 0)


def attend_kernel(n, nw, blocks, order_ref, q_ref, *rest):
    keys = rest[:n]
    wos = rest[n : n + nw]
    attn_ref, lse_ref, out_ref, kv, wo, m_s, l_s, acc_s, ksem, wsem = rest[n + nw :]
    width = q_ref.shape[1]
    pairs = width // 128
    wcopies = weight_copies(order_ref, wos, wo, wsem, (3 * width, width))
    m_s[...] = jnp.full(m_s.shape, NEG_LARGE, F32)
    l_s[...] = jnp.zeros(l_s.shape, F32)
    acc_s[...] = jnp.zeros(acc_s.shape, F32)

    def block_work(block):
        for copy in key_copies(keys, kv, ksem, block):
            copy.wait()
        for p in range(pairs):
            at = slice(p * 128, p * 128 + 128)
            qm = two_heads(q_ref[:, at]) * jnp.asarray(SCALE, BF16)
            s = dot_nt(qm, kv[:, at])
            m_old = m_s[p]
            m_new = jnp.maximum(m_old, jnp.max(s, axis=1, keepdims=True))
            factor = jnp.exp(m_old - m_new)
            e = jnp.exp(s - m_new)
            l_s[p] = l_s[p] * factor + jnp.sum(e, axis=1, keepdims=True)
            m_s[p] = m_new
            acc_s[p] = acc_s[p] * factor + dot_nn(
                e.astype(BF16), kv[:, width + p * 128 : width + p * 128 + 128]
            )

    each(blocks, block_work)
    for p in range(pairs):
        attn_ref[:, p * 128 : p * 128 + 128] = join_heads(acc_s[p] / l_s[p]).astype(BF16)
        lse_ref[p : p + 1, :] = as_row(m_s[p] + jnp.log(l_s[p]))
    for copy in wcopies:
        copy.wait()
    out_ref[...] = dot_nt(attn_ref[...], wo[...]).astype(BF16)


def gelu_parts(z):
    cdf = 0.5 * (1.0 + lax.erf(z * 0.7071067811865476))
    density = jnp.exp(-0.5 * z * z) * 0.3989422804014327
    return z * cdf, cdf + z * density


def ffn_kernel(nw, order_ref, x_ref, pa_ref, pb_ref, cot_ref, g_ref, *rest):
    ws = rest[:nw]
    hid_ref, out_ref, db_ref, b_ref, dz_ref, mixed_ref, w, wsem = rest[nw:]
    units = mixed_ref.shape[1]
    copies = weight_copies(order_ref, ws, w, wsem)
    hidden = x_ref[...] + (pa_ref[...].astype(F32) + pb_ref[...].astype(F32))
    hid_ref[...] = hidden
    xhat, _ = norm_parts(hidden)
    b = (xhat * g_ref[1:2, :]).astype(BF16)
    b_ref[...] = b
    cb = cot_ref[...].astype(BF16)
    for copy in copies:
        copy.wait()
    z = dot_nn(b, w[:, : 2 * units])
    gate = z[:, units:]
    act, slope = gelu_parts(z[:, :units])
    dmix = dot_nn(cb, w[:, 2 * units : 3 * units])
    dz = jnp.concatenate([dmix * gate * slope, dmix * act], axis=1).astype(BF16)
    dz_ref[...] = dz
    db_ref[...] = dot_nt(dz, w[:, : 2 * units]).astype(BF16)
    mixed = (act * gate).astype(BF16)
    mixed_ref[...] = mixed
    out_ref[...] = dot_nt(mixed, w[:, 2 * units : 3 * units]).astype(BF16)


def ffn_grad_kernel(no, order_ref, b_ref, dz_ref, cot_ref, mixed_ref, *rest):
    outs, acc = rest[:no], rest[no]
    two = dz_ref.shape[1]
    acc[:, :two] = dot_tn(b_ref[...], dz_ref[...])
    half = mixed_ref.shape[1]
    acc[:, two : two + half] = dot_tn(cot_ref[...].astype(BF16), mixed_ref[...])
    acc[:, two + half :] = jnp.zeros((acc.shape[0], acc.shape[1] - two - half), F32)
    emit_blocks(order_ref, acc, outs)


def back_tile(k, v, qm, dom, lse_row, dot_row):
    prob = jnp.exp(dot_nt(k, qm) - lse_row)
    ds = (prob * (dot_nt(v, dom) - dot_row)).astype(BF16)
    return dot_nn(ds, qm), dot_nn(prob.astype(BF16), dom), dot_tn(ds, k)


def back_kernel(
    n, nw, blocks, order_ref, q_ref, attn_ref, lse_ref, hid_ref, cot_ref, g_ref,
    da_ref, db_ref, *rest
):
    keys = rest[:n]
    wos = rest[n : n + nw]
    out_ref, dhid_ref, dq_ref, qm_ref, dom_ref, row_ref, kv, wo, ksem, wsem = rest[n + nw :]
    width = q_ref.shape[1]
    pairs = width // 128
    wcopies = weight_copies(order_ref, wos, wo, wsem, (3 * width, width))
    first = key_copies(keys, kv, ksem, 0) if blocks == 1 else None
    xhat, inv = norm_parts(hid_ref[...])
    db = da_ref[...].astype(F32) + db_ref[...].astype(F32)
    dhid = cot_ref[...] + norm_back(db, xhat, inv, g_ref[1:2, :])
    dhid_ref[...] = dhid
    for copy in wcopies:
        copy.wait()
    dattn = dot_nn(dhid.astype(BF16), wo[...]).astype(BF16)
    for p in range(pairs):
        at = slice(p * 128, p * 128 + 128)
        qm_ref[p] = two_heads(q_ref[:, at]) * jnp.asarray(SCALE, BF16)
        dom = two_heads(dattn[:, at])
        dom_ref[p] = dom
        both = jnp.concatenate([attn_ref[:, at]] * 2, axis=0)
        dots = jnp.sum(dom.astype(F32) * both.astype(F32), axis=1, keepdims=True)
        row_ref[p : p + 1, :] = as_row(dots)
    dq_ref[...] = jnp.zeros(dq_ref.shape, F32)
    block_rows = kv.shape[0]

    def block_work(block):
        for copy in first or key_copies(keys, kv, ksem, block):
            copy.wait()

        def sub_work(sub):
            src = pl.ds(pl.multiple_of(sub * SUB_ROWS, SUB_ROWS), SUB_ROWS)
            dst = pl.ds(pl.multiple_of(block * block_rows + sub * SUB_ROWS, SUB_ROWS), SUB_ROWS)
            for p in range(pairs):
                at = slice(p * 128, p * 128 + 128)
                vat = slice(width + p * 128, width + p * 128 + 128)
                dk, dv, dq = back_tile(
                    kv[src, at], kv[src, vat], qm_ref[p], dom_ref[p],
                    lse_ref[p : p + 1, :], row_ref[p : p + 1, :],
                )
                out_ref[dst, at] = dk.astype(BF16)
                out_ref[dst, vat] = dv.astype(BF16)
                dq_ref[p] += dq

        each(block_rows // SUB_ROWS, sub_work)

    each(blocks, block_work)


def back_rest_kernel(n, lse_ref, dq_ref, qm_ref, dom_ref, row_ref, cos_ref, sin_ref, *rest):
    if n:
        keys, recv = rest[:n], rest[n]
        sums = rest[n + 1 : 2 * n + 1]
        dqp_ref, kv, ksem = rest[2 * n + 1 :]
        copies = key_copies(keys, kv, ksem, 0)
        each_rows = sums[0].shape[0]
    else:
        (dqp_ref,) = rest
    width = dqp_ref.shape[1]
    pairs = width // 128
    dq = [dq_ref[p] for p in range(pairs)]
    if n:
        for copy in copies:
            copy.wait()
        per = SUB_ROWS // each_rows
        for sub in range(kv.shape[0] // SUB_ROWS):
            src = pl.ds(sub * SUB_ROWS, SUB_ROWS)
            for p in range(pairs):
                at = slice(p * 128, p * 128 + 128)
                vat = slice(width + p * 128, width + p * 128 + 128)
                dk, dv, more = back_tile(
                    kv[src, at], kv[src, vat], qm_ref[p], dom_ref[p],
                    lse_ref[p : p + 1, :], row_ref[p : p + 1, :],
                )
                dq[p] += more
                dk = dk + recv[src, at].astype(F32)
                dv = dv + recv[src, vat].astype(F32)
                for i in range(per):
                    part = slice(i * each_rows, (i + 1) * each_rows)
                    sums[sub * per + i][:, at] = dk[part].astype(BF16)
                    sums[sub * per + i][:, vat] = dv[part].astype(BF16)
    dq = jnp.concatenate([join_heads(x) for x in dq], axis=1) * SCALE
    dqp_ref[...] = rope_back(
        dq, wide(cos_ref[...], width), wide(sin_ref[...], width)
    ).astype(BF16)


def pick_rows(order_ref, ref, blocks, rows):
    return jnp.concatenate(
        [ref[pl.ds(pl.multiple_of((order_ref[0] ^ j) * rows, 16), rows), :] for j in blocks], axis=0
    )


def qkv_grad_kernel(
    n, nt, order_ref, at_ref, dqp_ref, dhid_ref, attn_ref, cos_ref, sin_ref, *rest
):
    terms = rest[:nt]
    chunks = rest[nt : nt + n]
    out_ref, da_ref, d_ref, ht_ref, w, sems = rest[nt + n :]
    width = dqp_ref.shape[1]
    copies = weight_copies(order_ref, chunks, w, sems, (0, 3 * width))
    dkv = total([term[...] for term in terms])
    dkp = rope_back(
        dkv[:, :width], wide(cos_ref[...], width), wide(sin_ref[...], width)
    ).astype(BF16)
    d = jnp.concatenate([dqp_ref[...], dkp, dkv[:, width:].astype(BF16)], axis=1)
    d_ref[...] = d
    ht_ref[...] = jnp.transpose(dhid_ref[...].astype(BF16))
    if n == 1:
        a_t, h_t = at_ref[...], ht_ref[...]
    else:
        rows = at_ref.shape[0] // 16
        a_t = pick_rows(order_ref, at_ref, chunk_order()[8:], rows)
        h_t = pick_rows(order_ref, ht_ref, chunk_order()[8:], rows)
    out_ref[:, : 3 * width] = dot_nn(a_t, d).astype(BF16)
    out_ref[:, 3 * width :] = dot_nn(h_t, attn_ref[...]).astype(BF16)
    for copy in copies:
        copy.wait()
    da_ref[...] = dot_nt(d, w[...]).astype(BF16)


def qkv_grad_rest_kernel(order_ref, at_ref, ht_ref, d_ref, attn_ref, recv, *sums):
    cut = d_ref.shape[1]
    rows = at_ref.shape[0] // 16
    a_t = pick_rows(order_ref, at_ref, chunk_order()[:8], rows)
    h_t = pick_rows(order_ref, ht_ref, chunk_order()[:8], rows)
    one = dot_nn(a_t, d_ref[...]) + recv[:, :cut].astype(F32)
    two = dot_nn(h_t, attn_ref[...]) + recv[:, cut:].astype(F32)
    for i, out in enumerate(sums):
        part = slice(i * rows, (i + 1) * rows)
        out[:, :cut] = one[part].astype(BF16)
        out[:, cut:] = two[part].astype(BF16)


def call(kernel, out_shape, specs, scratch, args):
    return pl.pallas_call(
        kernel,
        out_shape=out_shape,
        in_specs=specs,
        out_specs=jax.tree.map(lambda _: VM, out_shape),
        scratch_shapes=scratch,
    )(*args)


def rotary_tables(positions):
    half = HEAD_DIM // 2
    inverse = jnp.exp(jnp.arange(half, dtype=F32) * (-2.0 * math.log(THETA) / HEAD_DIM))
    angles = positions.astype(F32)[:, None] * inverse[None, :]
    angles = jnp.concatenate([angles] * 4, axis=-1)
    return jnp.cos(angles), jnp.sin(angles)


def adam_update(tensor, gradient, moment, second):
    moment = BETA_ONE * moment + (1.0 - BETA_ONE) * gradient
    second = BETA_TWO * second + (1.0 - BETA_TWO) * gradient * gradient
    first_hat = moment / (1.0 - BETA_ONE**STEP)
    second_hat = second / (1.0 - BETA_TWO**STEP)
    tensor = tensor - LEARN_RATE * (first_hat / (jnp.sqrt(second_hat) + ADAM_EPS) + DECAY * tensor)
    return tensor, moment, second


def gsum_kernel(nf, width, units, w_ref, *rest):
    firsts, lasts = rest[:nf], rest[nf : 2 * nf]
    g_ref, gain_ref = rest[2 * nf :]
    one = total([term[...] for term in firsts])
    two = total([term[...] for term in lasts])[:, : 3 * units]
    wf = w_ref[...].astype(BF16).astype(F32)
    cut = 4 * width
    sums = [
        jnp.sum(wf[:, : 3 * width] * one[:, : 3 * width], axis=1, keepdims=True),
        jnp.sum(wf[:, cut : cut + 2 * units] * two[:, : 2 * units], axis=1, keepdims=True),
    ]
    lane = lax.broadcasted_iota(jnp.int32, (wf.shape[0], 128), 1)
    cols = jnp.where(lane == 0, sums[0], jnp.where(lane == 1, sums[1], 0.0))
    gain_ref[...] = jnp.transpose(cols)[:2, :]
    g_ref[:, :cut] = one
    g_ref[:, cut:] = two


def adam_kernel(w_ref, g_ref, m_ref, v_ref, w_out, m_out, v_out):
    w_out[...], m_out[...], v_out[...] = adam_update(
        w_ref[...], g_ref[...], m_ref[...], v_ref[...]
    )


def gadam_kernel(a_ref, b_ref, w_ref, m_ref, v_ref, g_out, w_out, m_out, v_out):
    w = w_ref[...]
    grad = (a_ref[...] + b_ref[...]) / w.astype(BF16).astype(F32)
    g_out[...] = grad
    w_out[...], m_out[...], v_out[...] = adam_update(w, grad, m_ref[...], v_ref[...])


def lnback_kernel(x_ref, da_ref, db_ref, dhid_ref, g_ref, out_ref):
    xhat, inv = norm_parts(x_ref[...])
    da = da_ref[...].astype(F32) + db_ref[...].astype(F32)
    out_ref[...] = dhid_ref[...] + norm_back(da, xhat, inv, g_ref[0:1, :])


def head_swap(x):
    if lax.axis_size("head") == 1:
        return jnp.zeros_like(x)
    return swap(x, "head", 1)


def layer(
    inputs, cotangent, weights, gains, weight_moment, weight_second, gain_moment, gain_second
):
    heads = lax.axis_size("head")
    width = HEADS // heads * HEAD_DIM
    units = FF // heads
    toks, d = inputs.shape
    rows = weights.shape[0]
    n = lax.axis_size(TOKENS_AX)
    seq = toks * n
    me = lax.axis_index(TOKENS_AX).astype(jnp.int32)
    order = me.reshape(1)
    pairs = width // 128

    wb = weights.astype(BF16)
    gb = gains.astype(BF16)
    wq_cols = 4 * width + 128
    rest_pad = -(3 * units) % 128
    rest_cols = 3 * units + rest_pad
    w_first = jnp.concatenate([wb[:, : 4 * width], jnp.pad(gb.T, ((0, 0), (0, 126)))], axis=1)
    w_rest = jnp.pad(wb[:, 4 * width :], ((0, 0), (0, rest_pad)))
    first_chunks = gather(w_first)
    cos, sin = rotary_tables(me * toks + jnp.arange(toks, dtype=jnp.int32))

    nw = len(first_chunks)
    wsem = pltpu.SemaphoreType.DMA((nw,))
    halves = 2 if staged() else 1

    a_t, q, kv, g = call(
        partial(qkv_kernel, nw),
        [sds((d, toks), BF16), sds((toks, width), BF16), sds((toks, 2 * width), BF16), sds((8, d), F32)],
        [SM, VM, VM, VM] + [ANY] * nw,
        [pltpu.VMEM((d, wq_cols), BF16), wsem],
        [order, inputs, cos, sin] + first_chunks,
    )
    keys = gather(kv)
    rest_chunks = gather(w_rest)
    nk = len(keys)
    block_rows = min(KEY_ROWS, seq)
    blocks = seq // block_rows
    ksem = pltpu.SemaphoreType.DMA((nk,))

    attn, lse, out_part = call(
        partial(attend_kernel, nk, nw, blocks),
        [sds((toks, width), BF16), sds((8, 2 * toks), F32), sds((toks, d), BF16)],
        [SM, VM] + [ANY] * (nk + nw),
        [
            pltpu.VMEM((block_rows, 2 * width), BF16),
            pltpu.VMEM((d, width), BF16),
            pltpu.VMEM((pairs, 2 * toks, 1), F32),
            pltpu.VMEM((pairs, 2 * toks, 1), F32),
            pltpu.VMEM((pairs, 2 * toks, 128), F32),
            ksem,
            wsem,
        ],
        [order, q] + keys + first_chunks,
    )
    out_other = head_swap(out_part)

    hidden, ffn_part, db_part, b, dz, mixed = call(
        partial(ffn_kernel, nw),
        [
            sds((toks, d), F32),
            sds((toks, d), BF16),
            sds((toks, d), BF16),
            sds((toks, d), BF16),
            sds((toks, 2 * units), BF16),
            sds((toks, units), BF16),
        ],
        [SM] + [VM] * 5 + [ANY] * nw,
        [pltpu.VMEM((d, rest_cols), BF16), wsem],
        [order, inputs, out_part, out_other, cotangent, g] + rest_chunks,
    )
    db_other = head_swap(db_part)
    ffn_other = head_swap(ffn_part)
    outputs = hidden + (ffn_part.astype(F32) + ffn_other.astype(F32))
    ffn_grads = call(
        partial(ffn_grad_kernel, halves),
        [sds((d // halves, rest_cols), BF16)] * halves,
        [SM] + [VM] * 4,
        [pltpu.VMEM((d, rest_cols), F32)],
        [order, b, dz, cotangent, mixed],
    )
    if staged():
        ffn_sums = pair_sum(*ffn_grads)
    else:
        ffn_terms = native_sum(*ffn_grads)

    first_half = nk // 2 if staged() else 0
    part_rows = block_rows // halves
    part_sem = pltpu.SemaphoreType.DMA((nk - first_half,))
    both = (pairs, 2 * toks, 128)
    kv_part, dhid, dq, qm, dom, dots = call(
        partial(back_kernel, nk - first_half, nw, blocks),
        [
            sds((seq // halves, 2 * width), BF16),
            sds((toks, d), F32),
            sds(both, F32),
            sds(both, BF16),
            sds(both, BF16),
            sds((8, 2 * toks), F32),
        ],
        [SM] + [VM] * 8 + [ANY] * (nk - first_half + nw),
        [
            pltpu.VMEM((part_rows, 2 * width), BF16),
            pltpu.VMEM((d, width), BF16),
            part_sem,
            wsem,
        ],
        [order, q, attn, lse, hidden, cotangent, g, db_part, db_other]
        + keys[first_half:]
        + first_chunks,
    )
    rest_args = [lse, dq, qm, dom, dots, cos, sin]
    if staged():
        *kv_sums, dqp = call(
            partial(back_rest_kernel, first_half),
            [sds((toks, 2 * width), BF16)] * first_half + [sds((toks, width), BF16)],
            [VM] * 7 + [ANY] * first_half + [VM],
            [pltpu.VMEM((part_rows, 2 * width), BF16), part_sem],
            rest_args + keys[:first_half] + [swap(kv_part, "shard", 1)],
        )
        kv_terms = scatter_sum(kv_sums)
        ffn_terms = scatter_sum(ffn_sums)
    else:
        (dqp,) = call(
            partial(back_rest_kernel, 0), [sds((toks, width), BF16)], [VM] * 7, [], rest_args
        )
        kv_terms = native_sum(kv_part)
    nt = len(kv_terms)
    w_part, da_part, d_qkv, h_t = call(
        partial(qkv_grad_kernel, nw, nt),
        [
            sds((d // halves, 4 * width), BF16),
            sds((toks, d), BF16),
            sds((toks, 3 * width), BF16),
            sds((d, toks), BF16),
        ],
        [SM] + [VM] * 6 + [VM] * nt + [ANY] * nw,
        [pltpu.VMEM((d, 3 * width), BF16), wsem],
        [order, a_t, dqp, dhid, attn, cos, sin] + kv_terms + first_chunks,
    )
    da_other = head_swap(da_part)
    (input_grad,) = call(
        lnback_kernel,
        [sds((toks, d), F32)],
        [VM] * 5,
        [],
        [inputs, da_part, da_other, dhid, g],
    )

    if staged():
        first_sums = call(
            qkv_grad_rest_kernel,
            [sds((rows, 4 * width), BF16)] * 8,
            [SM] + [VM] * 5,
            [],
            [order, a_t, h_t, d_qkv, attn, swap(w_part, "shard", 1)],
        )
        first_terms = scatter_sum(first_sums)
    else:
        first_terms = native_sum(w_part)
    full = weights.shape
    weight_grad, gain_part = call(
        partial(gsum_kernel, nt, width, units),
        [sds(full, F32), sds(gains.shape, F32)],
        [VM] * (1 + 2 * nt),
        [],
        [weights] + first_terms + ffn_terms,
    )
    gain_other = head_swap(gain_part)
    step_rows = rows // 2 if rows % 16 == 0 else rows
    cells = pl.BlockSpec((step_rows, full[1]), lambda i: (i, 0))
    new_weights, new_weight_moment, new_weight_second = pl.pallas_call(
        adam_kernel,
        grid=(rows // step_rows,),
        out_shape=[sds(full, F32)] * 3,
        in_specs=[cells] * 4,
        out_specs=[cells] * 3,
        name="adam",
    )(weights, weight_grad, weight_moment, weight_second)
    gain_grad, new_gains, new_gain_moment, new_gain_second = call(
        gadam_kernel,
        [sds(gains.shape, F32)] * 4,
        [VM] * 5,
        [],
        [gain_part, gain_other, gains, gain_moment, gain_second],
    )
    return (
        outputs,
        input_grad,
        weight_grad,
        gain_grad,
        new_weights,
        new_weight_moment,
        new_weight_second,
        new_gains,
        new_gain_moment,
        new_gain_second,
    )


def solution(mesh):
    rows = P(("blk", "shard"), None)
    cells = P(("blk", "shard"), "head")
    lanes = P(None, ("blk", "shard"))
    return jax.shard_map(
        layer,
        mesh=mesh,
        in_specs=(rows, rows, cells, lanes, cells, cells, lanes, lanes),
        out_specs=(rows, rows, cells, lanes, cells, cells, cells, lanes, lanes, lanes),
        check_vma=False,
    )
```

```python
from functools import partial
import math

import jax
import jax.numpy as jnp
from jax import lax
from jax.experimental import pallas as pl
from jax.experimental.pallas import tpu as pltpu
from jax.sharding import PartitionSpec as P


HEADS = 12
HEAD_DIM = 64
FF = 1152
STEP = 3

NORM_EPS = 1e-05
THETA = 160000.0
BETA_ONE = 0.9
BETA_TWO = 0.98
LEARN_RATE = 0.2
ADAM_EPS = 1e-06
DECAY = 0.01
NEG_LARGE = -1e30
SCALE = 1.0 / math.sqrt(HEAD_DIM)
TOKENS_AX = ("blk", "shard")
F32 = jnp.float32
BF16 = jnp.bfloat16
KEY_ROWS = 2048
SUB_ROWS = 512


VM = pl.BlockSpec(memory_space=pltpu.VMEM)
SM = pl.BlockSpec(memory_space=pltpu.SMEM)
ANY = pl.BlockSpec(memory_space=pl.ANY)


def sds(shape, dtype):
    return jax.ShapeDtypeStruct(shape, dtype)


def dot_nn(a, b):
    return lax.dot_general(a, b, (((1,), (0,)), ((), ())), preferred_element_type=F32)


def dot_nt(a, b):
    return lax.dot_general(a, b, (((1,), (1,)), ((), ())), preferred_element_type=F32)


def dot_tn(a, b):
    return lax.dot_general(a, b, (((0,), (0,)), ((), ())), preferred_element_type=F32)


def swap(x, axis, bits):
    size = lax.axis_size(axis)
    return lax.ppermute(x, axis, [(i, i ^ bits) for i in range(size)])


def staged():
    return lax.axis_size("blk") == 4 and lax.axis_size("shard") == 4


def chunk_order():
    return [z * 4 + x * 2 + c for c in range(2) for x in range(2) for z in range(4)]


def gather(x):
    if not staged():
        return [lax.all_gather(x, TOKENS_AX, axis=0, tiled=True)]
    got = {0: x}
    got[8] = swap(x, "blk", 2)
    got[4] = swap(x, "blk", 1)
    got[12] = swap(got[8], "blk", 1)
    for z in range(4):
        got[z * 4 + 2] = swap(got[z * 4], "shard", 2)
    for z in range(4):
        for h in (0, 2):
            got[z * 4 + h + 1] = swap(got[z * 4 + h], "shard", 1)
    return [got[j] for j in chunk_order()]


def add_kernel(*refs):
    keep, recv = refs[0], refs[1]
    for i, out in enumerate(refs[2:]):
        rows = out.shape[0]
        at = pl.ds(i * rows, rows)
        out[...] = (keep[at, :].astype(F32) + recv[at, :].astype(F32)).astype(BF16)


def block_kernel(*refs):
    refs[-1][...] = total([ref[...] for ref in refs[:-1]]).astype(BF16)


def native_sum(part):
    return [lax.psum_scatter(part, TOKENS_AX, scatter_dimension=0, tiled=True)]


def pair_swap(groups):
    return [swap(groups[2 + x], "shard", 1) for x in (1, 0)][::-1]


def scatter_sum(groups, recv):
    keep = groups[0]
    rows, cols = keep.shape[0] // 4, keep.shape[1]
    s = pl.pallas_call(
        add_kernel,
        out_shape=[sds((rows, cols), BF16)] * 4,
        in_specs=[VM, VM],
        out_specs=[VM] * 4,
        name="pair_add",
    )(groups[1], recv[1])
    got = {z: swap(s[z], "shard", 2) for z in (3, 2, 1, 0)}

    def block(z, *more):
        head = pl.BlockSpec((rows, cols), lambda i: (z, 0))
        return call(
            block_kernel,
            [sds((rows, cols), BF16)],
            [head, head] + [VM] * (1 + len(more)),
            [],
            [keep, recv[0], got[z], *more],
        )[0]

    far = swap(block(3), "blk", 1)
    two = swap(block(2, far), "blk", 2)
    one = swap(block(1), "blk", 1)
    return [keep, recv[0], got[0], one, two]


def term_specs(terms):
    shape = terms[-1].shape
    head = pl.BlockSpec(shape, lambda i: (0, 0))
    return [VM if term.shape == shape else head for term in terms]


def total(terms):
    out = terms[0].astype(F32)
    for term in terms[1:]:
        out = out + term.astype(F32)
    return out


def weight_copies(order_ref, chunks, dst, sems, cols=None):
    rows = chunks[0].shape[0]
    copies = []
    for i, chunk in enumerate(chunks):
        src = chunk if cols is None else chunk.at[:, pl.ds(cols[0], cols[1])]
        if len(chunks) == 1:
            at = pl.ds(0, rows)
        else:
            at = pl.ds(pl.multiple_of((order_ref[0] ^ chunk_order()[i]) * rows, 16), rows)
        copies.append(pltpu.make_async_copy(src, dst.at[at, :], sems.at[i]))
    for copy in copies:
        copy.start()
    return copies


def emit_blocks(order_ref, acc, outs):
    if len(outs) == 1:
        outs[0][...] = acc[...].astype(BF16)
        return
    rows = outs[0].shape[0] // 4
    for i, j in enumerate(chunk_order()):
        at = pl.ds(pl.multiple_of((order_ref[0] ^ j) * rows, 8), rows)
        outs[i // 4][pl.ds((i % 4) * rows, rows), :] = acc[at, :].astype(BF16)


def norm_parts(v):
    centre = v - jnp.mean(v, axis=-1, keepdims=True)
    inv = lax.rsqrt(jnp.mean(centre * centre, axis=-1, keepdims=True) + NORM_EPS)
    return centre * inv, inv


def norm_back(u, xhat, inv, g):
    s = u * g
    return inv * (
        s
        - jnp.mean(s, axis=-1, keepdims=True)
        - xhat * jnp.mean(s * xhat, axis=-1, keepdims=True)
    )


def low_half(shape):
    lane = lax.broadcasted_iota(jnp.int32, shape, 1)
    return (lane & (HEAD_DIM - 1)) < HEAD_DIM // 2


def turn(u):
    width = u.shape[1]
    half = HEAD_DIM // 2
    left = pltpu.roll(u, width - half, 1)
    right = pltpu.roll(u, half, 1)
    return left, right, low_half(u.shape)


def rope(u, cos, sin):
    left, right, low = turn(u)
    return u * cos + jnp.where(low, -left, right) * sin


def rope_back(w, cos, sin):
    left, right, low = turn(w * sin)
    return w * cos + jnp.where(low, left, -right)


def wide(table, width):
    return jnp.concatenate([table] * (width // table.shape[1]), axis=1)


def two_heads(pair):
    lane = lax.broadcasted_iota(jnp.int32, pair.shape, 1)
    zero = jnp.zeros_like(pair)
    first = lane < HEAD_DIM
    return jnp.concatenate(
        [jnp.where(first, pair, zero), jnp.where(first, zero, pair)], axis=0
    )


def join_heads(both):
    rows = both.shape[0] // 2
    lane = lax.broadcasted_iota(jnp.int32, (rows, both.shape[1]), 1)
    return jnp.where(lane < HEAD_DIM, both[:rows], both[rows:])


def as_row(col):
    return jnp.transpose(jnp.broadcast_to(col, (col.shape[0], 128)))[0:1, :]


def qkv_kernel(n, order_ref, x_ref, cos_ref, sin_ref, *rest):
    chunks = rest[:n]
    at_ref, q_ref, kv_ref, g_ref, w, sems = rest[n:]
    width = q_ref.shape[1]
    copies = weight_copies(order_ref, chunks, w, sems)
    xhat, _ = norm_parts(x_ref[...])
    for copy in copies:
        copy.wait()
    row = lax.broadcasted_iota(jnp.int32, (8, 128), 0)
    lane = lax.broadcasted_iota(jnp.int32, (8, 128), 1)
    pick = jnp.where(row == lane, 1.0, 0.0).astype(BF16)
    g = dot_nt(pick, w[:, 4 * width : 4 * width + 128])
    g_ref[...] = g
    a = (xhat * g[0:1, :]).astype(BF16)
    at_ref[...] = jnp.transpose(a)
    cos = wide(cos_ref[...], width)
    sin = wide(sin_ref[...], width)
    q_ref[...] = rope(dot_nn(a, w[:, :width]), cos, sin).astype(BF16)
    kv_ref[:, :width] = rope(dot_nn(a, w[:, width : 2 * width]), cos, sin).astype(BF16)
    kv_ref[:, width:] = dot_nn(a, w[:, 2 * width : 3 * width]).astype(BF16)


def key_copies(chunks, dst, sems, block):
    if len(chunks) == 1:
        rows = dst.shape[0]
        at = pl.ds(pl.multiple_of(block * rows, rows), rows)
        copies = [pltpu.make_async_copy(chunks[0].at[at, :], dst, sems.at[0])]
    else:
        rows = chunks[0].shape[0]
        copies = [
            pltpu.make_async_copy(chunk, dst.at[pl.ds(i * rows, rows), :], sems.at[i])
            for i, chunk in enumerate(chunks)
        ]
    for copy in copies:
        copy.start()
    return copies


def each(count, body):
    if count == 1:
        body(0)
    else:
        lax.fori_loop(0, count, lambda i, c: (body(i), c)[1], 0)


def attend_kernel(n, nw, blocks, order_ref, q_ref, *rest):
    keys = rest[:n]
    wos = rest[n : n + nw]
    attn_ref, lse_ref, out_ref, kv, wo, m_s, l_s, acc_s, ksem, wsem = rest[n + nw :]
    width = q_ref.shape[1]
    pairs = width // 128
    wcopies = weight_copies(order_ref, wos, wo, wsem, (3 * width, width))
    m_s[...] = jnp.full(m_s.shape, NEG_LARGE, F32)
    l_s[...] = jnp.zeros(l_s.shape, F32)
    acc_s[...] = jnp.zeros(acc_s.shape, F32)

    def block_work(block):
        for copy in key_copies(keys, kv, ksem, block):
            copy.wait()
        for p in range(pairs):
            at = slice(p * 128, p * 128 + 128)
            qm = two_heads(q_ref[:, at]) * jnp.asarray(SCALE, BF16)
            s = dot_nt(qm, kv[:, at])
            m_old = m_s[p]
            m_new = jnp.maximum(m_old, jnp.max(s, axis=1, keepdims=True))
            factor = jnp.exp(m_old - m_new)
            e = jnp.exp(s - m_new)
            l_s[p] = l_s[p] * factor + jnp.sum(e, axis=1, keepdims=True)
            m_s[p] = m_new
            acc_s[p] = acc_s[p] * factor + dot_nn(
                e.astype(BF16), kv[:, width + p * 128 : width + p * 128 + 128]
            )

    each(blocks, block_work)
    for p in range(pairs):
        attn_ref[:, p * 128 : p * 128 + 128] = join_heads(acc_s[p] / l_s[p]).astype(BF16)
        lse_ref[p : p + 1, :] = as_row(m_s[p] + jnp.log(l_s[p]))
    for copy in wcopies:
        copy.wait()
    out_ref[...] = dot_nt(attn_ref[...], wo[...]).astype(BF16)


def gelu_parts(z):
    cdf = 0.5 * (1.0 + lax.erf(z * 0.7071067811865476))
    density = jnp.exp(-0.5 * z * z) * 0.3989422804014327
    return z * cdf, cdf + z * density


def ffn_kernel(nw, order_ref, x_ref, pa_ref, pb_ref, cot_ref, g_ref, *rest):
    ws = rest[:nw]
    hid_ref, out_ref, db_ref, b_ref, dz_ref, mixed_ref, w, wsem = rest[nw:]
    units = mixed_ref.shape[1]
    copies = weight_copies(order_ref, ws, w, wsem)
    hidden = x_ref[...] + (pa_ref[...].astype(F32) + pb_ref[...].astype(F32))
    hid_ref[...] = hidden
    xhat, _ = norm_parts(hidden)
    b = (xhat * g_ref[1:2, :]).astype(BF16)
    b_ref[...] = b
    cb = cot_ref[...].astype(BF16)
    for copy in copies:
        copy.wait()
    z = dot_nn(b, w[:, : 2 * units])
    gate = z[:, units:]
    act, slope = gelu_parts(z[:, :units])
    dmix = dot_nn(cb, w[:, 2 * units : 3 * units])
    dz = jnp.concatenate([dmix * gate * slope, dmix * act], axis=1).astype(BF16)
    dz_ref[...] = dz
    db_ref[...] = dot_nt(dz, w[:, : 2 * units]).astype(BF16)
    mixed = (act * gate).astype(BF16)
    mixed_ref[...] = mixed
    out_ref[...] = dot_nt(mixed, w[:, 2 * units : 3 * units]).astype(BF16)


def ffn_grad_kernel(no, order_ref, b_ref, dz_ref, cot_ref, mixed_ref, *rest):
    outs, acc = rest[:no], rest[no]
    two = dz_ref.shape[1]
    acc[:, :two] = dot_tn(b_ref[...], dz_ref[...])
    half = mixed_ref.shape[1]
    acc[:, two : two + half] = dot_tn(cot_ref[...].astype(BF16), mixed_ref[...])
    acc[:, two + half :] = jnp.zeros((acc.shape[0], acc.shape[1] - two - half), F32)
    emit_blocks(order_ref, acc, outs)


def back_tile(k, v, qm, dom, lse_row, dot_row):
    prob = jnp.exp(dot_nt(k, qm) - lse_row)
    ds = (prob * (dot_nt(v, dom) - dot_row)).astype(BF16)
    return dot_nn(ds, qm), dot_nn(prob.astype(BF16), dom), dot_tn(ds, k)


def back_kernel(
    n, nw, no, blocks, order_ref, q_ref, attn_ref, lse_ref, hid_ref, cot_ref, g_ref,
    da_ref, db_ref, cos_ref, sin_ref, *rest
):
    keys = rest[:n]
    wos = rest[n : n + nw]
    outs = rest[n + nw : n + nw + no]
    dhid_ref, dqp_ref, kv, wo, dq_s, qm_s, dom_s, row_s, ksem, wsem = rest[n + nw + no :]
    width = q_ref.shape[1]
    pairs = width // 128
    wcopies = weight_copies(order_ref, wos, wo, wsem, (3 * width, width))
    first = key_copies(keys, kv, ksem, 0) if blocks == 1 else None
    xhat, inv = norm_parts(hid_ref[...])
    db = da_ref[...].astype(F32) + db_ref[...].astype(F32)
    dhid = cot_ref[...] + norm_back(db, xhat, inv, g_ref[1:2, :])
    dhid_ref[...] = dhid
    for copy in wcopies:
        copy.wait()
    dattn = dot_nn(dhid.astype(BF16), wo[...]).astype(BF16)
    for p in range(pairs):
        at = slice(p * 128, p * 128 + 128)
        qm_s[p] = two_heads(q_ref[:, at]) * jnp.asarray(SCALE, BF16)
        dom = two_heads(dattn[:, at])
        dom_s[p] = dom
        both = jnp.concatenate([attn_ref[:, at]] * 2, axis=0)
        dots = jnp.sum(dom.astype(F32) * both.astype(F32), axis=1, keepdims=True)
        row_s[p : p + 1, :] = as_row(dots)
    dq_s[...] = jnp.zeros(dq_s.shape, F32)
    block_rows = kv.shape[0]

    def block_work(block):
        for copy in first or key_copies(keys, kv, ksem, block):
            copy.wait()
        for group, out_ref in enumerate(outs):
            size = block_rows // no

            def sub_work(sub):
                start = group * size + sub * SUB_ROWS
                src = pl.ds(pl.multiple_of(start, SUB_ROWS), SUB_ROWS)
                dst = pl.ds(
                    pl.multiple_of(block * block_rows + sub * SUB_ROWS, SUB_ROWS), SUB_ROWS
                )
                for p in range(pairs):
                    at = slice(p * 128, p * 128 + 128)
                    vat = slice(width + p * 128, width + p * 128 + 128)
                    dk, dv, dq = back_tile(
                        kv[src, at], kv[src, vat], qm_s[p], dom_s[p],
                        lse_ref[p : p + 1, :], row_s[p : p + 1, :],
                    )
                    out_ref[dst, at] = dk.astype(BF16)
                    out_ref[dst, vat] = dv.astype(BF16)
                    dq_s[p] += dq

            each(size // SUB_ROWS, sub_work)

    each(blocks, block_work)
    dq = jnp.concatenate([join_heads(dq_s[p]) for p in range(pairs)], axis=1) * SCALE
    dqp_ref[...] = rope_back(
        dq, wide(cos_ref[...], width), wide(sin_ref[...], width)
    ).astype(BF16)


def pick_rows(order_ref, ref, blocks, rows):
    return jnp.concatenate(
        [ref[pl.ds(pl.multiple_of((order_ref[0] ^ j) * rows, 16), rows), :] for j in blocks], axis=0
    )


def qkv_grad_kernel(
    n, nt, no, order_ref, at_ref, dqp_ref, dhid_ref, attn_ref, cos_ref, sin_ref, *rest
):
    terms = rest[:nt]
    chunks = rest[nt : nt + n]
    outs = rest[nt + n : nt + n + no]
    da_ref, w, ht, sems = rest[nt + n + no :]
    width = dqp_ref.shape[1]
    copies = weight_copies(order_ref, chunks, w, sems, (0, 3 * width))
    dkv = total([term[...] for term in terms])
    dkp = rope_back(
        dkv[:, :width], wide(cos_ref[...], width), wide(sin_ref[...], width)
    ).astype(BF16)
    d = jnp.concatenate([dqp_ref[...], dkp, dkv[:, width:].astype(BF16)], axis=1)
    ht[...] = jnp.transpose(dhid_ref[...].astype(BF16))
    if no == 1:
        a_t, h_t = at_ref[...], ht[...]
    else:
        rows = at_ref.shape[0] // 16
        a_t = pick_rows(order_ref, at_ref, chunk_order(), rows)
        h_t = pick_rows(order_ref, ht, chunk_order(), rows)
    one = dot_nn(a_t, d).astype(BF16)
    two = dot_nn(h_t, attn_ref[...]).astype(BF16)
    size = one.shape[0] // no
    for i, out in enumerate(outs):
        out[:, : 3 * width] = one[i * size : (i + 1) * size]
        out[:, 3 * width :] = two[i * size : (i + 1) * size]
    for copy in copies:
        copy.wait()
    da_ref[...] = dot_nt(d, w[...]).astype(BF16)


def call(kernel, out_shape, specs, scratch, args):
    return pl.pallas_call(
        kernel,
        out_shape=out_shape,
        in_specs=specs,
        out_specs=jax.tree.map(lambda _: VM, out_shape),
        scratch_shapes=scratch,
        grid=(1,) if any(spec.block_shape for spec in specs) else (),
    )(*args)


def rotary_tables(positions):
    half = HEAD_DIM // 2
    inverse = jnp.exp(jnp.arange(half, dtype=F32) * (-2.0 * math.log(THETA) / HEAD_DIM))
    angles = positions.astype(F32)[:, None] * inverse[None, :]
    angles = jnp.concatenate([angles] * 4, axis=-1)
    return jnp.cos(angles), jnp.sin(angles)


def adam_update(tensor, gradient, moment, second):
    moment = BETA_ONE * moment + (1.0 - BETA_ONE) * gradient
    second = BETA_TWO * second + (1.0 - BETA_TWO) * gradient * gradient
    first_hat = moment / (1.0 - BETA_ONE**STEP)
    second_hat = second / (1.0 - BETA_TWO**STEP)
    tensor = tensor - LEARN_RATE * (first_hat / (jnp.sqrt(second_hat) + ADAM_EPS) + DECAY * tensor)
    return tensor, moment, second


def gsum_kernel(nf, width, units, w_ref, *rest):
    firsts, lasts = rest[:nf], rest[nf : 2 * nf]
    g_ref, gain_ref = rest[2 * nf :]
    one = total([term[...] for term in firsts])
    two = total([term[...] for term in lasts])[:, : 3 * units]
    wf = w_ref[...].astype(BF16).astype(F32)
    cut = 4 * width
    sums = [
        jnp.sum(wf[:, : 3 * width] * one[:, : 3 * width], axis=1, keepdims=True),
        jnp.sum(wf[:, cut : cut + 2 * units] * two[:, : 2 * units], axis=1, keepdims=True),
    ]
    lane = lax.broadcasted_iota(jnp.int32, (wf.shape[0], 128), 1)
    cols = jnp.where(lane == 0, sums[0], jnp.where(lane == 1, sums[1], 0.0))
    gain_ref[...] = jnp.transpose(cols)[:2, :]
    g_ref[:, :cut] = one
    g_ref[:, cut:] = two


def adam_kernel(w_ref, g_ref, m_ref, v_ref, w_out, m_out, v_out):
    w_out[...], m_out[...], v_out[...] = adam_update(
        w_ref[...], g_ref[...], m_ref[...], v_ref[...]
    )


def gadam_kernel(a_ref, b_ref, w_ref, m_ref, v_ref, g_out, w_out, m_out, v_out):
    w = w_ref[...]
    grad = (a_ref[...] + b_ref[...]) / w.astype(BF16).astype(F32)
    g_out[...] = grad
    w_out[...], m_out[...], v_out[...] = adam_update(w, grad, m_ref[...], v_ref[...])


def lnback_kernel(
    x_ref, da_ref, db_ref, dhid_ref, g_ref, hid_ref, fa_ref, fb_ref, grad_ref, out_ref
):
    xhat, inv = norm_parts(x_ref[...])
    da = da_ref[...].astype(F32) + db_ref[...].astype(F32)
    grad_ref[...] = dhid_ref[...] + norm_back(da, xhat, inv, g_ref[0:1, :])
    out_ref[...] = hid_ref[...] + (fa_ref[...].astype(F32) + fb_ref[...].astype(F32))


def head_swap(x):
    if lax.axis_size("head") == 1:
        return jnp.zeros_like(x)
    return swap(x, "head", 1)


def layer(
    inputs, cotangent, weights, gains, weight_moment, weight_second, gain_moment, gain_second
):
    heads = lax.axis_size("head")
    width = HEADS // heads * HEAD_DIM
    units = FF // heads
    toks, d = inputs.shape
    rows = weights.shape[0]
    n = lax.axis_size(TOKENS_AX)
    seq = toks * n
    me = lax.axis_index(TOKENS_AX).astype(jnp.int32)
    order = me.reshape(1)
    pairs = width // 128

    wb = weights.astype(BF16)
    gb = gains.astype(BF16)
    wq_cols = 4 * width + 128
    rest_pad = -(3 * units) % 128
    rest_cols = 3 * units + rest_pad
    w_first = jnp.concatenate([wb[:, : 4 * width], jnp.pad(gb.T, ((0, 0), (0, 126)))], axis=1)
    w_rest = jnp.pad(wb[:, 4 * width :], ((0, 0), (0, rest_pad)))
    first_chunks = gather(w_first)
    cos, sin = rotary_tables(me * toks + jnp.arange(toks, dtype=jnp.int32))

    nw = len(first_chunks)
    wsem = pltpu.SemaphoreType.DMA((nw,))
    parts = 4 if staged() else 1

    a_t, q, kv, g = call(
        partial(qkv_kernel, nw),
        [sds((d, toks), BF16), sds((toks, width), BF16), sds((toks, 2 * width), BF16), sds((8, d), F32)],
        [SM, VM, VM, VM] + [ANY] * nw,
        [pltpu.VMEM((d, wq_cols), BF16), wsem],
        [order, inputs, cos, sin] + first_chunks,
    )
    keys = gather(kv)
    rest_chunks = gather(w_rest)
    nk = len(keys)
    block_rows = min(KEY_ROWS, seq)
    blocks = seq // block_rows
    ksem = pltpu.SemaphoreType.DMA((nk,))

    attn, lse, out_part = call(
        partial(attend_kernel, nk, nw, blocks),
        [sds((toks, width), BF16), sds((8, 2 * toks), F32), sds((toks, d), BF16)],
        [SM, VM] + [ANY] * (nk + nw),
        [
            pltpu.VMEM((block_rows, 2 * width), BF16),
            pltpu.VMEM((d, width), BF16),
            pltpu.VMEM((pairs, 2 * toks, 1), F32),
            pltpu.VMEM((pairs, 2 * toks, 1), F32),
            pltpu.VMEM((pairs, 2 * toks, 128), F32),
            ksem,
            wsem,
        ],
        [order, q] + keys + first_chunks,
    )
    out_other = head_swap(out_part)

    hidden, ffn_part, db_part, b, dz, mixed = call(
        partial(ffn_kernel, nw),
        [
            sds((toks, d), F32),
            sds((toks, d), BF16),
            sds((toks, d), BF16),
            sds((toks, d), BF16),
            sds((toks, 2 * units), BF16),
            sds((toks, units), BF16),
        ],
        [SM] + [VM] * 5 + [ANY] * nw,
        [pltpu.VMEM((d, rest_cols), BF16), wsem],
        [order, inputs, out_part, out_other, cotangent, g] + rest_chunks,
    )
    db_other = head_swap(db_part)
    ffn_other = head_swap(ffn_part)
    ffn_grads = call(
        partial(ffn_grad_kernel, parts),
        [sds((d // parts, rest_cols), BF16)] * parts,
        [SM] + [VM] * 4,
        [pltpu.VMEM((d, rest_cols), F32)],
        [order, b, dz, cotangent, mixed],
    )
    if staged():
        ffn_recv = pair_swap(ffn_grads)
    else:
        ffn_terms = native_sum(*ffn_grads)

    both = (pairs, 2 * toks, 128)
    *kv_groups, dhid, dqp = call(
        partial(back_kernel, nk, nw, parts, blocks),
        [sds((seq // parts, 2 * width), BF16)] * parts
        + [sds((toks, d), F32), sds((toks, width), BF16)],
        [SM] + [VM] * 10 + [ANY] * (nk + nw),
        [
            pltpu.VMEM((block_rows, 2 * width), BF16),
            pltpu.VMEM((d, width), BF16),
            pltpu.VMEM(both, F32),
            pltpu.VMEM(both, BF16),
            pltpu.VMEM(both, BF16),
            pltpu.VMEM((8, 2 * toks), F32),
            ksem,
            wsem,
        ],
        [order, q, attn, lse, hidden, cotangent, g, db_part, db_other, cos, sin]
        + keys
        + first_chunks,
    )
    if staged():
        kv_terms = scatter_sum(kv_groups, pair_swap(kv_groups))
        ffn_terms = scatter_sum(ffn_grads, ffn_recv)
    else:
        kv_terms = native_sum(*kv_groups)
    nt = len(kv_terms)
    *w_groups, da_part = call(
        partial(qkv_grad_kernel, nw, nt, parts),
        [sds((d // parts, 4 * width), BF16)] * parts + [sds((toks, d), BF16)],
        [SM] + [VM] * 6 + term_specs(kv_terms) + [ANY] * nw,
        [pltpu.VMEM((d, 3 * width), BF16), pltpu.VMEM((d, toks), BF16), wsem],
        [order, a_t, dqp, dhid, attn, cos, sin] + kv_terms + first_chunks,
    )
    da_other = head_swap(da_part)
    input_grad, outputs = call(
        lnback_kernel,
        [sds((toks, d), F32)] * 2,
        [VM] * 8,
        [],
        [inputs, da_part, da_other, dhid, g, hidden, ffn_part, ffn_other],
    )
    if staged():
        first_terms = scatter_sum(w_groups, pair_swap(w_groups))
    else:
        first_terms = native_sum(*w_groups)
    full = weights.shape
    weight_grad, gain_part = call(
        partial(gsum_kernel, nt, width, units),
        [sds(full, F32), sds(gains.shape, F32)],
        [VM] + term_specs(first_terms) + term_specs(ffn_terms),
        [],
        [weights] + first_terms + ffn_terms,
    )
    gain_other = head_swap(gain_part)
    step_rows = rows // 2 if rows % 16 == 0 else rows
    cells = pl.BlockSpec((step_rows, full[1]), lambda i: (i, 0))
    new_weights, new_weight_moment, new_weight_second = pl.pallas_call(
        adam_kernel,
        grid=(rows // step_rows,),
        out_shape=[sds(full, F32)] * 3,
        in_specs=[cells] * 4,
        out_specs=[cells] * 3,
        name="adam",
    )(weights, weight_grad, weight_moment, weight_second)
    gain_grad, new_gains, new_gain_moment, new_gain_second = call(
        gadam_kernel,
        [sds(gains.shape, F32)] * 4,
        [VM] * 5,
        [],
        [gain_part, gain_other, gains, gain_moment, gain_second],
    )
    return (
        outputs,
        input_grad,
        weight_grad,
        gain_grad,
        new_weights,
        new_weight_moment,
        new_weight_second,
        new_gains,
        new_gain_moment,
        new_gain_second,
    )


def solution(mesh):
    rows = P(("blk", "shard"), None)
    cells = P(("blk", "shard"), "head")
    lanes = P(None, ("blk", "shard"))
    return jax.shard_map(
        layer,
        mesh=mesh,
        in_specs=(rows, rows, cells, lanes, cells, cells, lanes, lanes),
        out_specs=(rows, rows, cells, lanes, cells, cells, cells, lanes, lanes, lanes),
        check_vma=False,
    )
```

```python
from functools import partial
import math

import jax
import jax.numpy as jnp
from jax import lax
from jax.experimental import pallas as pl
from jax.experimental.pallas import tpu as pltpu
from jax.sharding import PartitionSpec as P


HEADS = 12
HEAD_DIM = 64
FF = 1152
STEP = 3

NORM_EPS = 1e-05
THETA = 160000.0
BETA_ONE = 0.9
BETA_TWO = 0.98
LEARN_RATE = 0.2
ADAM_EPS = 1e-06
DECAY = 0.01
NEG_LARGE = -1e30
SCALE = 1.0 / math.sqrt(HEAD_DIM)
TOKENS_AX = ("blk", "shard")
F32 = jnp.float32
BF16 = jnp.bfloat16
KEY_ROWS = 2048
SUB_ROWS = 512


VM = pl.BlockSpec(memory_space=pltpu.VMEM)
SM = pl.BlockSpec(memory_space=pltpu.SMEM)
ANY = pl.BlockSpec(memory_space=pl.ANY)


def sds(shape, dtype):
    return jax.ShapeDtypeStruct(shape, dtype)


def dot_nn(a, b):
    return lax.dot_general(a, b, (((1,), (0,)), ((), ())), preferred_element_type=F32)


def dot_nt(a, b):
    return lax.dot_general(a, b, (((1,), (1,)), ((), ())), preferred_element_type=F32)


def dot_tn(a, b):
    return lax.dot_general(a, b, (((0,), (0,)), ((), ())), preferred_element_type=F32)


def swap(x, axis, bits):
    size = lax.axis_size(axis)
    return lax.ppermute(x, axis, [(i, i ^ bits) for i in range(size)])


def staged():
    return lax.axis_size("blk") == 4 and lax.axis_size("shard") == 4


def chunk_order():
    return [z * 4 + x * 2 + c for c in range(2) for x in range(2) for z in range(4)]


def gather(x):
    if not staged():
        return [lax.all_gather(x, TOKENS_AX, axis=0, tiled=True)]
    got = {0: x}
    got[8] = swap(x, "blk", 2)
    got[4] = swap(x, "blk", 1)
    got[12] = swap(got[8], "blk", 1)
    for z in range(4):
        got[z * 4 + 2] = swap(got[z * 4], "shard", 2)
    for z in range(4):
        for h in (0, 2):
            got[z * 4 + h + 1] = swap(got[z * 4 + h], "shard", 1)
    return [got[j] for j in chunk_order()]


def add_kernel(keep, recv, *rest):
    outs = rest[:4]
    kept, got, done, sems = rest[4:]
    rows = outs[0].shape[0]
    at = [pl.ds(i * rows, rows) for i in range(4)]
    loads = [
        [
            pltpu.make_async_copy(src.at[at[i], :], dst.at[at[i], :], sems.at[k, i])
            for k, (src, dst) in enumerate(((keep, kept), (recv, got)))
        ]
        for i in range(4)
    ]
    stores = [pltpu.make_async_copy(done.at[at[i], :], outs[i], sems.at[2, i]) for i in range(4)]
    for pair in loads:
        for copy in pair:
            copy.start()
    for i in range(4):
        for copy in loads[i]:
            copy.wait()
        done[at[i], :] = (kept[at[i], :].astype(F32) + got[at[i], :].astype(F32)).astype(BF16)
        stores[i].start()
    for copy in stores:
        copy.wait()


def pair_add(keep, recv):
    rows, cols = keep.shape[0] // 4, keep.shape[1]
    return pl.pallas_call(
        add_kernel,
        out_shape=[sds((rows, cols), BF16)] * 4,
        in_specs=[ANY, ANY],
        out_specs=[ANY] * 4,
        scratch_shapes=[pltpu.VMEM(keep.shape, BF16)] * 3 + [pltpu.SemaphoreType.DMA((3, 4))],
        name="pair_add",
    )(keep, recv)


def native_sum(part):
    return [lax.psum_scatter(part, TOKENS_AX, scatter_dimension=0, tiled=True)]


def pair_swap(groups):
    return [swap(groups[2 + x], "shard", 1) for x in (1, 0)][::-1]


def scatter_sum(groups, recv):
    s = pair_add(groups[1], recv[1])
    got = {z: swap(s[z], "shard", 2) for z in (3, 2, 1, 0)}
    keep = pair_add(groups[0], recv[0])

    def block(z, *more):
        return total([keep[z], got[z], *more]).astype(BF16)

    far = swap(block(3), "blk", 1)
    two = swap(block(2, far), "blk", 2)
    one = swap(block(1), "blk", 1)
    return [keep[0], got[0], one, two]


def total(terms):
    out = terms[0].astype(F32)
    for term in terms[1:]:
        out = out + term.astype(F32)
    return out


def weight_copies(order_ref, chunks, dst, sems, cols=None):
    rows = chunks[0].shape[0]
    copies = []
    for i, chunk in enumerate(chunks):
        src = chunk if cols is None else chunk.at[:, pl.ds(cols[0], cols[1])]
        if len(chunks) == 1:
            at = pl.ds(0, rows)
        else:
            at = pl.ds(pl.multiple_of((order_ref[0] ^ chunk_order()[i]) * rows, 16), rows)
        copies.append(pltpu.make_async_copy(src, dst.at[at, :], sems.at[i]))
    for copy in copies:
        copy.start()
    return copies


def emit_blocks(order_ref, acc, outs):
    if len(outs) == 1:
        outs[0][...] = acc[...].astype(BF16)
        return
    rows = outs[0].shape[0] // 4
    for i, j in enumerate(chunk_order()):
        at = pl.ds(pl.multiple_of((order_ref[0] ^ j) * rows, 8), rows)
        outs[i // 4][pl.ds((i % 4) * rows, rows), :] = acc[at, :].astype(BF16)


def norm_parts(v):
    centre = v - jnp.mean(v, axis=-1, keepdims=True)
    inv = lax.rsqrt(jnp.mean(centre * centre, axis=-1, keepdims=True) + NORM_EPS)
    return centre * inv, inv


def norm_back(u, xhat, inv, g):
    s = u * g
    return inv * (
        s
        - jnp.mean(s, axis=-1, keepdims=True)
        - xhat * jnp.mean(s * xhat, axis=-1, keepdims=True)
    )


def low_half(shape):
    lane = lax.broadcasted_iota(jnp.int32, shape, 1)
    return (lane & (HEAD_DIM - 1)) < HEAD_DIM // 2


def turn(u):
    width = u.shape[1]
    half = HEAD_DIM // 2
    left = pltpu.roll(u, width - half, 1)
    right = pltpu.roll(u, half, 1)
    return left, right, low_half(u.shape)


def rope(u, cos, sin):
    left, right, low = turn(u)
    return u * cos + jnp.where(low, -left, right) * sin


def rope_back(w, cos, sin):
    left, right, low = turn(w * sin)
    return w * cos + jnp.where(low, left, -right)


def wide(table, width):
    return jnp.concatenate([table] * (width // table.shape[1]), axis=1)


def two_heads(pair):
    lane = lax.broadcasted_iota(jnp.int32, pair.shape, 1)
    zero = jnp.zeros_like(pair)
    first = lane < HEAD_DIM
    return jnp.concatenate(
        [jnp.where(first, pair, zero), jnp.where(first, zero, pair)], axis=0
    )


def join_heads(both):
    rows = both.shape[0] // 2
    lane = lax.broadcasted_iota(jnp.int32, (rows, both.shape[1]), 1)
    return jnp.where(lane < HEAD_DIM, both[:rows], both[rows:])


def as_row(col):
    return jnp.transpose(jnp.broadcast_to(col, (col.shape[0], 128)))[0:1, :]


def qkv_kernel(n, order_ref, x_ref, cos_ref, sin_ref, *rest):
    chunks = rest[:n]
    at_ref, q_ref, kv_ref, g_ref, w, sems = rest[n:]
    width = q_ref.shape[1]
    copies = weight_copies(order_ref, chunks, w, sems)
    xhat, _ = norm_parts(x_ref[...])
    for copy in copies:
        copy.wait()
    row = lax.broadcasted_iota(jnp.int32, (8, 128), 0)
    lane = lax.broadcasted_iota(jnp.int32, (8, 128), 1)
    pick = jnp.where(row == lane, 1.0, 0.0).astype(BF16)
    g = dot_nt(pick, w[:, 4 * width : 4 * width + 128])
    g_ref[...] = g
    a = (xhat * g[0:1, :]).astype(BF16)
    at_ref[...] = jnp.transpose(a)
    cos = wide(cos_ref[...], width)
    sin = wide(sin_ref[...], width)
    q_ref[...] = rope(dot_nn(a, w[:, :width]), cos, sin).astype(BF16)
    kv_ref[:, :width] = rope(dot_nn(a, w[:, width : 2 * width]), cos, sin).astype(BF16)
    kv_ref[:, width:] = dot_nn(a, w[:, 2 * width : 3 * width]).astype(BF16)


def key_copies(chunks, dst, sems, block):
    if len(chunks) == 1:
        rows = dst.shape[0]
        at = pl.ds(pl.multiple_of(block * rows, rows), rows)
        copies = [pltpu.make_async_copy(chunks[0].at[at, :], dst, sems.at[0])]
    else:
        rows = chunks[0].shape[0]
        copies = [
            pltpu.make_async_copy(chunk, dst.at[pl.ds(i * rows, rows), :], sems.at[i])
            for i, chunk in enumerate(chunks)
        ]
    for copy in copies:
        copy.start()
    return copies


def each(count, body):
    if count == 1:
        body(0)
    else:
        lax.fori_loop(0, count, lambda i, c: (body(i), c)[1], 0)


def attend_kernel(n, nw, blocks, order_ref, q_ref, *rest):
    keys = rest[:n]
    wos = rest[n : n + nw]
    attn_ref, lse_ref, out_ref, kv, wo, m_s, l_s, acc_s, ksem, wsem = rest[n + nw :]
    width = q_ref.shape[1]
    pairs = width // 128
    wcopies = weight_copies(order_ref, wos, wo, wsem, (3 * width, width))
    m_s[...] = jnp.full(m_s.shape, NEG_LARGE, F32)
    l_s[...] = jnp.zeros(l_s.shape, F32)
    acc_s[...] = jnp.zeros(acc_s.shape, F32)

    def block_work(block):
        for copy in key_copies(keys, kv, ksem, block):
            copy.wait()
        for p in range(pairs):
            at = slice(p * 128, p * 128 + 128)
            qm = two_heads(q_ref[:, at]) * jnp.asarray(SCALE, BF16)
            s = dot_nt(qm, kv[:, at])
            m_old = m_s[p]
            m_new = jnp.maximum(m_old, jnp.max(s, axis=1, keepdims=True))
            factor = jnp.exp(m_old - m_new)
            e = jnp.exp(s - m_new)
            l_s[p] = l_s[p] * factor + jnp.sum(e, axis=1, keepdims=True)
            m_s[p] = m_new
            acc_s[p] = acc_s[p] * factor + dot_nn(
                e.astype(BF16), kv[:, width + p * 128 : width + p * 128 + 128]
            )

    each(blocks, block_work)
    for p in range(pairs):
        attn_ref[:, p * 128 : p * 128 + 128] = join_heads(acc_s[p] / l_s[p]).astype(BF16)
        lse_ref[p : p + 1, :] = as_row(m_s[p] + jnp.log(l_s[p]))
    for copy in wcopies:
        copy.wait()
    out_ref[...] = dot_nt(attn_ref[...], wo[...]).astype(BF16)


def gelu_parts(z):
    cdf = 0.5 * (1.0 + lax.erf(z * 0.7071067811865476))
    density = jnp.exp(-0.5 * z * z) * 0.3989422804014327
    return z * cdf, cdf + z * density


def ffn_kernel(nw, order_ref, x_ref, pa_ref, pb_ref, cot_ref, g_ref, *rest):
    ws = rest[:nw]
    hid_ref, out_ref, db_ref, b_ref, dz_ref, mixed_ref, w, wsem = rest[nw:]
    units = mixed_ref.shape[1]
    copies = weight_copies(order_ref, ws, w, wsem)
    hidden = x_ref[...] + (pa_ref[...].astype(F32) + pb_ref[...].astype(F32))
    hid_ref[...] = hidden
    xhat, _ = norm_parts(hidden)
    b = (xhat * g_ref[1:2, :]).astype(BF16)
    b_ref[...] = b
    cb = cot_ref[...].astype(BF16)
    for copy in copies:
        copy.wait()
    z = dot_nn(b, w[:, : 2 * units])
    gate = z[:, units:]
    act, slope = gelu_parts(z[:, :units])
    dmix = dot_nn(cb, w[:, 2 * units : 3 * units])
    dz = jnp.concatenate([dmix * gate * slope, dmix * act], axis=1).astype(BF16)
    dz_ref[...] = dz
    db_ref[...] = dot_nt(dz, w[:, : 2 * units]).astype(BF16)
    mixed = (act * gate).astype(BF16)
    mixed_ref[...] = mixed
    out_ref[...] = dot_nt(mixed, w[:, 2 * units : 3 * units]).astype(BF16)


def ffn_grad_kernel(no, order_ref, b_ref, dz_ref, cot_ref, mixed_ref, *rest):
    outs, acc = rest[:no], rest[no]
    two = dz_ref.shape[1]
    acc[:, :two] = dot_tn(b_ref[...], dz_ref[...])
    half = mixed_ref.shape[1]
    acc[:, two : two + half] = dot_tn(cot_ref[...].astype(BF16), mixed_ref[...])
    acc[:, two + half :] = jnp.zeros((acc.shape[0], acc.shape[1] - two - half), F32)
    emit_blocks(order_ref, acc, outs)


def back_tile(k, v, qm, dom, lse_row, dot_row):
    prob = jnp.exp(dot_nt(k, qm) - lse_row)
    ds = (prob * (dot_nt(v, dom) - dot_row)).astype(BF16)
    return dot_nn(ds, qm), dot_nn(prob.astype(BF16), dom), dot_tn(ds, k)


def back_kernel(
    n, nw, no, blocks, order_ref, q_ref, attn_ref, lse_ref, hid_ref, cot_ref, g_ref,
    da_ref, db_ref, cos_ref, sin_ref, *rest
):
    keys = rest[:n]
    wos = rest[n : n + nw]
    outs = rest[n + nw : n + nw + no]
    dhid_ref, dqp_ref, kv, wo, dq_s, qm_s, dom_s, row_s, ksem, wsem = rest[n + nw + no :]
    width = q_ref.shape[1]
    pairs = width // 128
    wcopies = weight_copies(order_ref, wos, wo, wsem, (3 * width, width))
    first = key_copies(keys, kv, ksem, 0) if blocks == 1 else None
    xhat, inv = norm_parts(hid_ref[...])
    db = da_ref[...].astype(F32) + db_ref[...].astype(F32)
    dhid = cot_ref[...] + norm_back(db, xhat, inv, g_ref[1:2, :])
    dhid_ref[...] = dhid
    for copy in wcopies:
        copy.wait()
    dattn = dot_nn(dhid.astype(BF16), wo[...]).astype(BF16)
    for p in range(pairs):
        at = slice(p * 128, p * 128 + 128)
        qm_s[p] = two_heads(q_ref[:, at]) * jnp.asarray(SCALE, BF16)
        dom = two_heads(dattn[:, at])
        dom_s[p] = dom
        both = jnp.concatenate([attn_ref[:, at]] * 2, axis=0)
        dots = jnp.sum(dom.astype(F32) * both.astype(F32), axis=1, keepdims=True)
        row_s[p : p + 1, :] = as_row(dots)
    dq_s[...] = jnp.zeros(dq_s.shape, F32)
    block_rows = kv.shape[0]

    def block_work(block):
        for copy in first or key_copies(keys, kv, ksem, block):
            copy.wait()
        for group, out_ref in enumerate(outs):
            size = block_rows // no

            def sub_work(sub):
                start = group * size + sub * SUB_ROWS
                src = pl.ds(pl.multiple_of(start, SUB_ROWS), SUB_ROWS)
                dst = pl.ds(
                    pl.multiple_of(block * block_rows + sub * SUB_ROWS, SUB_ROWS), SUB_ROWS
                )
                for p in range(pairs):
                    at = slice(p * 128, p * 128 + 128)
                    vat = slice(width + p * 128, width + p * 128 + 128)
                    dk, dv, dq = back_tile(
                        kv[src, at], kv[src, vat], qm_s[p], dom_s[p],
                        lse_ref[p : p + 1, :], row_s[p : p + 1, :],
                    )
                    out_ref[dst, at] = dk.astype(BF16)
                    out_ref[dst, vat] = dv.astype(BF16)
                    dq_s[p] += dq

            each(size // SUB_ROWS, sub_work)

    each(blocks, block_work)
    dq = jnp.concatenate([join_heads(dq_s[p]) for p in range(pairs)], axis=1) * SCALE
    dqp_ref[...] = rope_back(
        dq, wide(cos_ref[...], width), wide(sin_ref[...], width)
    ).astype(BF16)


def pick_rows(order_ref, ref, blocks, rows):
    return jnp.concatenate(
        [ref[pl.ds(pl.multiple_of((order_ref[0] ^ j) * rows, 16), rows), :] for j in blocks], axis=0
    )


def qkv_grad_kernel(
    n, nt, no, order_ref, at_ref, dqp_ref, dhid_ref, attn_ref, cos_ref, sin_ref, *rest
):
    terms = rest[:nt]
    chunks = rest[nt : nt + n]
    outs = rest[nt + n : nt + n + no]
    da_ref, w, ht, sems = rest[nt + n + no :]
    width = dqp_ref.shape[1]
    copies = weight_copies(order_ref, chunks, w, sems, (0, 3 * width))
    dkv = total([term[...] for term in terms])
    dkp = rope_back(
        dkv[:, :width], wide(cos_ref[...], width), wide(sin_ref[...], width)
    ).astype(BF16)
    d = jnp.concatenate([dqp_ref[...], dkp, dkv[:, width:].astype(BF16)], axis=1)
    ht[...] = jnp.transpose(dhid_ref[...].astype(BF16))
    if no == 1:
        a_t, h_t = at_ref[...], ht[...]
    else:
        rows = at_ref.shape[0] // 16
        a_t = pick_rows(order_ref, at_ref, chunk_order(), rows)
        h_t = pick_rows(order_ref, ht, chunk_order(), rows)
    one = dot_nn(a_t, d).astype(BF16)
    two = dot_nn(h_t, attn_ref[...]).astype(BF16)
    size = one.shape[0] // no
    for i, out in enumerate(outs):
        out[:, : 3 * width] = one[i * size : (i + 1) * size]
        out[:, 3 * width :] = two[i * size : (i + 1) * size]
    for copy in copies:
        copy.wait()
    da_ref[...] = dot_nt(d, w[...]).astype(BF16)


def call(kernel, out_shape, specs, scratch, args):
    return pl.pallas_call(
        kernel,
        out_shape=out_shape,
        in_specs=specs,
        out_specs=jax.tree.map(lambda _: VM, out_shape),
        scratch_shapes=scratch,
    )(*args)


def rotary_tables(positions):
    half = HEAD_DIM // 2
    inverse = jnp.exp(jnp.arange(half, dtype=F32) * (-2.0 * math.log(THETA) / HEAD_DIM))
    angles = positions.astype(F32)[:, None] * inverse[None, :]
    angles = jnp.concatenate([angles] * 4, axis=-1)
    return jnp.cos(angles), jnp.sin(angles)


def adam_update(tensor, gradient, moment, second):
    moment = BETA_ONE * moment + (1.0 - BETA_ONE) * gradient
    second = BETA_TWO * second + (1.0 - BETA_TWO) * gradient * gradient
    first_hat = moment / (1.0 - BETA_ONE**STEP)
    second_hat = second / (1.0 - BETA_TWO**STEP)
    tensor = tensor - LEARN_RATE * (first_hat / (jnp.sqrt(second_hat) + ADAM_EPS) + DECAY * tensor)
    return tensor, moment, second


def gsum_kernel(nf, width, units, w_ref, *rest):
    firsts, lasts = rest[:nf], rest[nf : 2 * nf]
    g_ref, gain_ref = rest[2 * nf :]
    one = total([term[...] for term in firsts])
    two = total([term[...] for term in lasts])[:, : 3 * units]
    wf = w_ref[...].astype(BF16).astype(F32)
    cut = 4 * width
    sums = [
        jnp.sum(wf[:, : 3 * width] * one[:, : 3 * width], axis=1, keepdims=True),
        jnp.sum(wf[:, cut : cut + 2 * units] * two[:, : 2 * units], axis=1, keepdims=True),
    ]
    lane = lax.broadcasted_iota(jnp.int32, (wf.shape[0], 128), 1)
    cols = jnp.where(lane == 0, sums[0], jnp.where(lane == 1, sums[1], 0.0))
    gain_ref[...] = jnp.transpose(cols)[:2, :]
    g_ref[:, :cut] = one
    g_ref[:, cut:] = two


def adam_kernel(w_ref, g_ref, m_ref, v_ref, w_out, m_out, v_out):
    w_out[...], m_out[...], v_out[...] = adam_update(
        w_ref[...], g_ref[...], m_ref[...], v_ref[...]
    )


def gadam_kernel(a_ref, b_ref, w_ref, m_ref, v_ref, g_out, w_out, m_out, v_out):
    w = w_ref[...]
    grad = (a_ref[...] + b_ref[...]) / w.astype(BF16).astype(F32)
    g_out[...] = grad
    w_out[...], m_out[...], v_out[...] = adam_update(w, grad, m_ref[...], v_ref[...])


def lnback_kernel(
    x_ref, da_ref, db_ref, dhid_ref, g_ref, hid_ref, fa_ref, fb_ref, grad_ref, out_ref
):
    xhat, inv = norm_parts(x_ref[...])
    da = da_ref[...].astype(F32) + db_ref[...].astype(F32)
    grad_ref[...] = dhid_ref[...] + norm_back(da, xhat, inv, g_ref[0:1, :])
    out_ref[...] = hid_ref[...] + (fa_ref[...].astype(F32) + fb_ref[...].astype(F32))


def head_swap(x):
    if lax.axis_size("head") == 1:
        return jnp.zeros_like(x)
    return swap(x, "head", 1)


def layer(
    inputs, cotangent, weights, gains, weight_moment, weight_second, gain_moment, gain_second
):
    heads = lax.axis_size("head")
    width = HEADS // heads * HEAD_DIM
    units = FF // heads
    toks, d = inputs.shape
    rows = weights.shape[0]
    n = lax.axis_size(TOKENS_AX)
    seq = toks * n
    me = lax.axis_index(TOKENS_AX).astype(jnp.int32)
    order = me.reshape(1)
    pairs = width // 128

    wb = weights.astype(BF16)
    gb = gains.astype(BF16)
    wq_cols = 4 * width + 128
    rest_pad = -(3 * units) % 128
    rest_cols = 3 * units + rest_pad
    w_first = jnp.concatenate([wb[:, : 4 * width], jnp.pad(gb.T, ((0, 0), (0, 126)))], axis=1)
    w_rest = jnp.pad(wb[:, 4 * width :], ((0, 0), (0, rest_pad)))
    first_chunks = gather(w_first)
    cos, sin = rotary_tables(me * toks + jnp.arange(toks, dtype=jnp.int32))

    nw = len(first_chunks)
    wsem = pltpu.SemaphoreType.DMA((nw,))
    parts = 4 if staged() else 1

    a_t, q, kv, g = call(
        partial(qkv_kernel, nw),
        [sds((d, toks), BF16), sds((toks, width), BF16), sds((toks, 2 * width), BF16), sds((8, d), F32)],
        [SM, VM, VM, VM] + [ANY] * nw,
        [pltpu.VMEM((d, wq_cols), BF16), wsem],
        [order, inputs, cos, sin] + first_chunks,
    )
    keys = gather(kv)
    rest_chunks = gather(w_rest)
    nk = len(keys)
    block_rows = min(KEY_ROWS, seq)
    blocks = seq // block_rows
    ksem = pltpu.SemaphoreType.DMA((nk,))

    attn, lse, out_part = call(
        partial(attend_kernel, nk, nw, blocks),
        [sds((toks, width), BF16), sds((8, 2 * toks), F32), sds((toks, d), BF16)],
        [SM, VM] + [ANY] * (nk + nw),
        [
            pltpu.VMEM((block_rows, 2 * width), BF16),
            pltpu.VMEM((d, width), BF16),
            pltpu.VMEM((pairs, 2 * toks, 1), F32),
            pltpu.VMEM((pairs, 2 * toks, 1), F32),
            pltpu.VMEM((pairs, 2 * toks, 128), F32),
            ksem,
            wsem,
        ],
        [order, q] + keys + first_chunks,
    )
    out_other = head_swap(out_part)

    hidden, ffn_part, db_part, b, dz, mixed = call(
        partial(ffn_kernel, nw),
        [
            sds((toks, d), F32),
            sds((toks, d), BF16),
            sds((toks, d), BF16),
            sds((toks, d), BF16),
            sds((toks, 2 * units), BF16),
            sds((toks, units), BF16),
        ],
        [SM] + [VM] * 5 + [ANY] * nw,
        [pltpu.VMEM((d, rest_cols), BF16), wsem],
        [order, inputs, out_part, out_other, cotangent, g] + rest_chunks,
    )
    db_other = head_swap(db_part)
    ffn_other = head_swap(ffn_part)
    ffn_grads = call(
        partial(ffn_grad_kernel, parts),
        [sds((d // parts, rest_cols), BF16)] * parts,
        [SM] + [VM] * 4,
        [pltpu.VMEM((d, rest_cols), F32)],
        [order, b, dz, cotangent, mixed],
    )
    if staged():
        ffn_recv = pair_swap(ffn_grads)
    else:
        ffn_terms = native_sum(*ffn_grads)

    both = (pairs, 2 * toks, 128)
    *kv_groups, dhid, dqp = call(
        partial(back_kernel, nk, nw, parts, blocks),
        [sds((seq // parts, 2 * width), BF16)] * parts
        + [sds((toks, d), F32), sds((toks, width), BF16)],
        [SM] + [VM] * 10 + [ANY] * (nk + nw),
        [
            pltpu.VMEM((block_rows, 2 * width), BF16),
            pltpu.VMEM((d, width), BF16),
            pltpu.VMEM(both, F32),
            pltpu.VMEM(both, BF16),
            pltpu.VMEM(both, BF16),
            pltpu.VMEM((8, 2 * toks), F32),
            ksem,
            wsem,
        ],
        [order, q, attn, lse, hidden, cotangent, g, db_part, db_other, cos, sin]
        + keys
        + first_chunks,
    )
    if staged():
        kv_terms = scatter_sum(kv_groups, pair_swap(kv_groups))
        ffn_terms = scatter_sum(ffn_grads, ffn_recv)
    else:
        kv_terms = native_sum(*kv_groups)
    nt = len(kv_terms)
    *w_groups, da_part = call(
        partial(qkv_grad_kernel, nw, nt, parts),
        [sds((d // parts, 4 * width), BF16)] * parts + [sds((toks, d), BF16)],
        [SM] + [VM] * 6 + [VM] * nt + [ANY] * nw,
        [pltpu.VMEM((d, 3 * width), BF16), pltpu.VMEM((d, toks), BF16), wsem],
        [order, a_t, dqp, dhid, attn, cos, sin] + kv_terms + first_chunks,
    )
    da_other = head_swap(da_part)
    input_grad, outputs = call(
        lnback_kernel,
        [sds((toks, d), F32)] * 2,
        [VM] * 8,
        [],
        [inputs, da_part, da_other, dhid, g, hidden, ffn_part, ffn_other],
    )
    if staged():
        first_terms = scatter_sum(w_groups, pair_swap(w_groups))
    else:
        first_terms = native_sum(*w_groups)
    full = weights.shape
    weight_grad, gain_part = call(
        partial(gsum_kernel, nt, width, units),
        [sds(full, F32), sds(gains.shape, F32)],
        [VM] * (1 + 2 * nt),
        [],
        [weights] + first_terms + ffn_terms,
    )
    gain_other = head_swap(gain_part)
    step_rows = rows // 2 if rows % 16 == 0 else rows
    cells = pl.BlockSpec((step_rows, full[1]), lambda i: (i, 0))
    new_weights, new_weight_moment, new_weight_second = pl.pallas_call(
        adam_kernel,
        grid=(rows // step_rows,),
        out_shape=[sds(full, F32)] * 3,
        in_specs=[cells] * 4,
        out_specs=[cells] * 3,
        name="adam",
    )(weights, weight_grad, weight_moment, weight_second)
    gain_grad, new_gains, new_gain_moment, new_gain_second = call(
        gadam_kernel,
        [sds(gains.shape, F32)] * 4,
        [VM] * 5,
        [],
        [gain_part, gain_other, gains, gain_moment, gain_second],
    )
    return (
        outputs,
        input_grad,
        weight_grad,
        gain_grad,
        new_weights,
        new_weight_moment,
        new_weight_second,
        new_gains,
        new_gain_moment,
        new_gain_second,
    )


def solution(mesh):
    rows = P(("blk", "shard"), None)
    cells = P(("blk", "shard"), "head")
    lanes = P(None, ("blk", "shard"))
    return jax.shard_map(
        layer,
        mesh=mesh,
        in_specs=(rows, rows, cells, lanes, cells, cells, lanes, lanes),
        out_specs=(rows, rows, cells, lanes, cells, cells, cells, lanes, lanes, lanes),
        check_vma=False,
    )
```

```python
from functools import partial
import math

import jax
import jax.numpy as jnp
from jax import lax
from jax.experimental import pallas as pl
from jax.experimental.pallas import tpu as pltpu
from jax.sharding import PartitionSpec as P


HEADS = 12
HEAD_DIM = 64
FF = 1152
STEP = 3

NORM_EPS = 1e-05
THETA = 160000.0
BETA_ONE = 0.9
BETA_TWO = 0.98
LEARN_RATE = 0.2
ADAM_EPS = 1e-06
DECAY = 0.01
NEG_LARGE = -1e30
SCALE = 1.0 / math.sqrt(HEAD_DIM)
TOKENS_AX = ("blk", "shard")
F32 = jnp.float32
BF16 = jnp.bfloat16
KEY_ROWS = 2048
SUB_ROWS = 512


VM = pl.BlockSpec(memory_space=pltpu.VMEM)
SM = pl.BlockSpec(memory_space=pltpu.SMEM)
ANY = pl.BlockSpec(memory_space=pl.ANY)
HBM = pl.BlockSpec(memory_space=pltpu.HBM)


def sds(shape, dtype):
    return jax.ShapeDtypeStruct(shape, dtype)


def dot_nn(a, b):
    return lax.dot_general(a, b, (((1,), (0,)), ((), ())), preferred_element_type=F32)


def dot_nt(a, b):
    return lax.dot_general(a, b, (((1,), (1,)), ((), ())), preferred_element_type=F32)


def dot_tn(a, b):
    return lax.dot_general(a, b, (((0,), (0,)), ((), ())), preferred_element_type=F32)


def swap(x, axis, bits):
    size = lax.axis_size(axis)
    return lax.ppermute(x, axis, [(i, i ^ bits) for i in range(size)])


def staged():
    return lax.axis_size("blk") == 4 and lax.axis_size("shard") == 4


def chunk_order():
    return [z * 4 + x * 2 + c for c in range(2) for x in range(2) for z in range(4)]


def gather(x):
    if not staged():
        return [lax.all_gather(x, TOKENS_AX, axis=0, tiled=True)]
    got = {0: x}
    got[8] = swap(x, "blk", 2)
    got[4] = swap(x, "blk", 1)
    got[12] = swap(got[8], "blk", 1)
    for z in range(4):
        got[z * 4 + 2] = swap(got[z * 4], "shard", 2)
    for z in range(4):
        for h in (0, 2):
            got[z * 4 + h + 1] = swap(got[z * 4 + h], "shard", 1)
    return [got[j] for j in chunk_order()]


def add_kernel(keep, recv, *rest):
    outs = rest[:4]
    kept, got, done, sems = rest[4:]
    rows = outs[0].shape[0]
    at = [pl.ds(i * rows, rows) for i in range(4)]
    loads = [
        [
            pltpu.make_async_copy(src.at[at[i], :], dst.at[at[i], :], sems.at[k, i])
            for k, (src, dst) in enumerate(((keep, kept), (recv, got)))
        ]
        for i in range(4)
    ]
    stores = [pltpu.make_async_copy(done.at[at[i], :], outs[i], sems.at[2, i]) for i in range(4)]
    for pair in loads:
        for copy in pair:
            copy.start()
    for i in range(4):
        for copy in loads[i]:
            copy.wait()
        done[at[i], :] = (kept[at[i], :].astype(F32) + got[at[i], :].astype(F32)).astype(BF16)
        stores[i].start()
    for copy in stores:
        copy.wait()


def pair_add(keep, recv):
    rows, cols = keep.shape[0] // 4, keep.shape[1]
    return pl.pallas_call(
        add_kernel,
        out_shape=[sds((rows, cols), BF16)] * 4,
        in_specs=[HBM, HBM],
        out_specs=[HBM] * 4,
        scratch_shapes=[pltpu.VMEM(keep.shape, BF16)] * 3 + [pltpu.SemaphoreType.DMA((3, 4))],
        name="pair_add",
    )(keep, recv)


def native_sum(part):
    return [lax.psum_scatter(part, TOKENS_AX, scatter_dimension=0, tiled=True)]


def pair_swap(groups):
    return [swap(groups[2 + x], "shard", 1) for x in (1, 0)][::-1]


def scatter_sum(groups, recv):
    s = pair_add(groups[1], recv[1])
    got = {z: swap(s[z], "shard", 2) for z in (3, 2, 1, 0)}
    keep = pair_add(groups[0], recv[0])

    def block(z, *more):
        return total([keep[z], got[z], *more]).astype(BF16)

    far = swap(block(3), "blk", 1)
    two = swap(block(2, far), "blk", 2)
    one = swap(block(1), "blk", 1)
    return [keep[0], got[0], one, two]


def total(terms):
    out = terms[0].astype(F32)
    for term in terms[1:]:
        out = out + term.astype(F32)
    return out


def weight_copies(order_ref, chunks, dst, sems, cols=None):
    rows = chunks[0].shape[0]
    copies = []
    for i, chunk in enumerate(chunks):
        src = chunk if cols is None else chunk.at[:, pl.ds(cols[0], cols[1])]
        if len(chunks) == 1:
            at = pl.ds(0, rows)
        else:
            at = pl.ds(pl.multiple_of((order_ref[0] ^ chunk_order()[i]) * rows, 16), rows)
        copies.append(pltpu.make_async_copy(src, dst.at[at, :], sems.at[i]))
    for copy in copies:
        copy.start()
    return copies


def group_copies(src, outs, sems, first_col):
    rows, cols = src.shape[0] // len(outs), src.shape[1]
    copies = [
        pltpu.make_async_copy(
            src.at[pl.ds(i * rows, rows), :], out.at[:, pl.ds(first_col, cols)], sems.at[i]
        )
        for i, out in enumerate(outs)
    ]
    for copy in copies:
        copy.start()
    for copy in copies:
        copy.wait()


def emit_blocks(order_ref, acc, dst, staged_rows):
    if not staged_rows:
        dst[...] = acc[...].astype(BF16)
        return
    rows = acc.shape[0] // 16
    for i, j in enumerate(chunk_order()):
        at = pl.ds(pl.multiple_of((order_ref[0] ^ j) * rows, 8), rows)
        dst[pl.ds(i * rows, rows), :] = acc[at, :].astype(BF16)


def norm_parts(v):
    centre = v - jnp.mean(v, axis=-1, keepdims=True)
    inv = lax.rsqrt(jnp.mean(centre * centre, axis=-1, keepdims=True) + NORM_EPS)
    return centre * inv, inv


def norm_back(u, xhat, inv, g):
    s = u * g
    return inv * (
        s
        - jnp.mean(s, axis=-1, keepdims=True)
        - xhat * jnp.mean(s * xhat, axis=-1, keepdims=True)
    )


def low_half(shape):
    lane = lax.broadcasted_iota(jnp.int32, shape, 1)
    return (lane & (HEAD_DIM - 1)) < HEAD_DIM // 2


def turn(u):
    width = u.shape[1]
    half = HEAD_DIM // 2
    left = pltpu.roll(u, width - half, 1)
    right = pltpu.roll(u, half, 1)
    return left, right, low_half(u.shape)


def rope(u, cos, sin):
    left, right, low = turn(u)
    return u * cos + jnp.where(low, -left, right) * sin


def rope_back(w, cos, sin):
    left, right, low = turn(w * sin)
    return w * cos + jnp.where(low, left, -right)


def wide(table, width):
    return jnp.concatenate([table] * (width // table.shape[1]), axis=1)


def two_heads(pair):
    lane = lax.broadcasted_iota(jnp.int32, pair.shape, 1)
    zero = jnp.zeros_like(pair)
    first = lane < HEAD_DIM
    return jnp.concatenate(
        [jnp.where(first, pair, zero), jnp.where(first, zero, pair)], axis=0
    )


def join_heads(both):
    rows = both.shape[0] // 2
    lane = lax.broadcasted_iota(jnp.int32, (rows, both.shape[1]), 1)
    return jnp.where(lane < HEAD_DIM, both[:rows], both[rows:])


def as_row(col):
    return jnp.transpose(jnp.broadcast_to(col, (col.shape[0], 128)))[0:1, :]


def qkv_kernel(n, order_ref, x_ref, cos_ref, sin_ref, *rest):
    chunks = rest[:n]
    at_ref, q_ref, kv_ref, g_ref, w, sems = rest[n:]
    width = q_ref.shape[1]
    copies = weight_copies(order_ref, chunks, w, sems)
    xhat, _ = norm_parts(x_ref[...])
    for copy in copies:
        copy.wait()
    row = lax.broadcasted_iota(jnp.int32, (8, 128), 0)
    lane = lax.broadcasted_iota(jnp.int32, (8, 128), 1)
    pick = jnp.where(row == lane, 1.0, 0.0).astype(BF16)
    g = dot_nt(pick, w[:, 4 * width : 4 * width + 128])
    g_ref[...] = g
    a = (xhat * g[0:1, :]).astype(BF16)
    at_ref[...] = jnp.transpose(a)
    cos = wide(cos_ref[...], width)
    sin = wide(sin_ref[...], width)
    q_ref[...] = rope(dot_nn(a, w[:, :width]), cos, sin).astype(BF16)
    kv_ref[:, :width] = rope(dot_nn(a, w[:, width : 2 * width]), cos, sin).astype(BF16)
    kv_ref[:, width:] = dot_nn(a, w[:, 2 * width : 3 * width]).astype(BF16)


def key_copies(chunks, dst, sems, block):
    if len(chunks) == 1:
        rows = dst.shape[0]
        at = pl.ds(pl.multiple_of(block * rows, rows), rows)
        copies = [pltpu.make_async_copy(chunks[0].at[at, :], dst, sems.at[0])]
    else:
        rows = chunks[0].shape[0]
        copies = [
            pltpu.make_async_copy(chunk, dst.at[pl.ds(i * rows, rows), :], sems.at[i])
            for i, chunk in enumerate(chunks)
        ]
    for copy in copies:
        copy.start()
    return copies


def each(count, body):
    if count == 1:
        body(0)
    else:
        lax.fori_loop(0, count, lambda i, c: (body(i), c)[1], 0)


def attend_kernel(n, nw, blocks, order_ref, q_ref, *rest):
    keys = rest[:n]
    wos = rest[n : n + nw]
    attn_ref, lse_ref, out_ref, kv, wo, m_s, l_s, acc_s, ksem, wsem = rest[n + nw :]
    width = q_ref.shape[1]
    pairs = width // 128
    wcopies = weight_copies(order_ref, wos, wo, wsem, (3 * width, width))
    m_s[...] = jnp.full(m_s.shape, NEG_LARGE, F32)
    l_s[...] = jnp.zeros(l_s.shape, F32)
    acc_s[...] = jnp.zeros(acc_s.shape, F32)

    def block_work(block):
        for copy in key_copies(keys, kv, ksem, block):
            copy.wait()
        for p in range(pairs):
            at = slice(p * 128, p * 128 + 128)
            qm = two_heads(q_ref[:, at]) * jnp.asarray(SCALE, BF16)
            s = dot_nt(qm, kv[:, at])
            m_old = m_s[p]
            m_new = jnp.maximum(m_old, jnp.max(s, axis=1, keepdims=True))
            factor = jnp.exp(m_old - m_new)
            e = jnp.exp(s - m_new)
            l_s[p] = l_s[p] * factor + jnp.sum(e, axis=1, keepdims=True)
            m_s[p] = m_new
            acc_s[p] = acc_s[p] * factor + dot_nn(
                e.astype(BF16), kv[:, width + p * 128 : width + p * 128 + 128]
            )

    each(blocks, block_work)
    for p in range(pairs):
        attn_ref[:, p * 128 : p * 128 + 128] = join_heads(acc_s[p] / l_s[p]).astype(BF16)
        lse_ref[p : p + 1, :] = as_row(m_s[p] + jnp.log(l_s[p]))
    for copy in wcopies:
        copy.wait()
    out_ref[...] = dot_nt(attn_ref[...], wo[...]).astype(BF16)


def gelu_parts(z):
    cdf = 0.5 * (1.0 + lax.erf(z * 0.7071067811865476))
    density = jnp.exp(-0.5 * z * z) * 0.3989422804014327
    return z * cdf, cdf + z * density


def ffn_kernel(nw, order_ref, x_ref, pa_ref, pb_ref, cot_ref, g_ref, *rest):
    ws = rest[:nw]
    hid_ref, out_ref, db_ref, b_ref, dz_ref, mixed_ref, w, wsem = rest[nw:]
    units = mixed_ref.shape[1]
    copies = weight_copies(order_ref, ws, w, wsem)
    hidden = x_ref[...] + (pa_ref[...].astype(F32) + pb_ref[...].astype(F32))
    hid_ref[...] = hidden
    xhat, _ = norm_parts(hidden)
    b = (xhat * g_ref[1:2, :]).astype(BF16)
    b_ref[...] = b
    cb = cot_ref[...].astype(BF16)
    for copy in copies:
        copy.wait()
    z = dot_nn(b, w[:, : 2 * units])
    gate = z[:, units:]
    act, slope = gelu_parts(z[:, :units])
    dmix = dot_nn(cb, w[:, 2 * units : 3 * units])
    dz = jnp.concatenate([dmix * gate * slope, dmix * act], axis=1).astype(BF16)
    dz_ref[...] = dz
    db_ref[...] = dot_nt(dz, w[:, : 2 * units]).astype(BF16)
    mixed = (act * gate).astype(BF16)
    mixed_ref[...] = mixed
    out_ref[...] = dot_nt(mixed, w[:, 2 * units : 3 * units]).astype(BF16)


def ffn_grad_kernel(no, order_ref, b_ref, dz_ref, cot_ref, mixed_ref, *rest):
    outs = rest[:no]
    acc, dst, sems = rest[no:]
    two = dz_ref.shape[1]
    acc[:, :two] = dot_tn(b_ref[...], dz_ref[...])
    half = mixed_ref.shape[1]
    acc[:, two : two + half] = dot_tn(cot_ref[...].astype(BF16), mixed_ref[...])
    acc[:, two + half :] = jnp.zeros((acc.shape[0], acc.shape[1] - two - half), F32)
    emit_blocks(order_ref, acc, dst, no > 1)
    group_copies(dst, outs, sems, 0)


def oq_grad_kernel(no, first_col, order_ref, at_ref, dqp_ref, dhid_ref, attn_ref, *rest):
    outs = rest[no : 2 * no]
    ht, dst, sems = rest[2 * no :]
    width = dqp_ref.shape[1]
    ht[...] = jnp.transpose(dhid_ref[...].astype(BF16))
    a_t, h_t = rows_in_order(order_ref, at_ref, no), rows_in_order(order_ref, ht, no)
    dst[:, :width] = dot_nn(a_t, dqp_ref[...]).astype(BF16)
    dst[:, width:] = dot_nn(h_t, attn_ref[...]).astype(BF16)
    group_copies(dst, outs, sems, first_col)


def back_tile(k, v, qm, dom, lse_row, dot_row):
    prob = jnp.exp(dot_nt(k, qm) - lse_row)
    ds = (prob * (dot_nt(v, dom) - dot_row)).astype(BF16)
    return dot_nn(ds, qm), dot_nn(prob.astype(BF16), dom), dot_tn(ds, k)


def back_kernel(
    n, nw, no, blocks, order_ref, q_ref, attn_ref, lse_ref, hid_ref, cot_ref, g_ref,
    da_ref, db_ref, cos_ref, sin_ref, *rest
):
    keys = rest[:n]
    wos = rest[n : n + nw]
    outs = rest[n + nw : n + nw + no]
    dhid_ref, dqp_ref, kv, wo, dq_s, qm_s, dom_s, row_s, ksem, wsem = rest[n + nw + no :]
    width = q_ref.shape[1]
    pairs = width // 128
    wcopies = weight_copies(order_ref, wos, wo, wsem, (3 * width, width))
    first = key_copies(keys, kv, ksem, 0) if blocks == 1 else None
    xhat, inv = norm_parts(hid_ref[...])
    db = da_ref[...].astype(F32) + db_ref[...].astype(F32)
    dhid = cot_ref[...] + norm_back(db, xhat, inv, g_ref[1:2, :])
    dhid_ref[...] = dhid
    for copy in wcopies:
        copy.wait()
    dattn = dot_nn(dhid.astype(BF16), wo[...]).astype(BF16)
    for p in range(pairs):
        at = slice(p * 128, p * 128 + 128)
        qm_s[p] = two_heads(q_ref[:, at]) * jnp.asarray(SCALE, BF16)
        dom = two_heads(dattn[:, at])
        dom_s[p] = dom
        both = jnp.concatenate([attn_ref[:, at]] * 2, axis=0)
        dots = jnp.sum(dom.astype(F32) * both.astype(F32), axis=1, keepdims=True)
        row_s[p : p + 1, :] = as_row(dots)
    dq_s[...] = jnp.zeros(dq_s.shape, F32)
    block_rows = kv.shape[0]

    def block_work(block):
        for copy in first or key_copies(keys, kv, ksem, block):
            copy.wait()
        for group, out_ref in enumerate(outs):
            size = block_rows // no

            def sub_work(sub):
                start = group * size + sub * SUB_ROWS
                src = pl.ds(pl.multiple_of(start, SUB_ROWS), SUB_ROWS)
                dst = pl.ds(
                    pl.multiple_of(block * block_rows + sub * SUB_ROWS, SUB_ROWS), SUB_ROWS
                )
                for p in range(pairs):
                    at = slice(p * 128, p * 128 + 128)
                    vat = slice(width + p * 128, width + p * 128 + 128)
                    dk, dv, dq = back_tile(
                        kv[src, at], kv[src, vat], qm_s[p], dom_s[p],
                        lse_ref[p : p + 1, :], row_s[p : p + 1, :],
                    )
                    out_ref[dst, at] = dk.astype(BF16)
                    out_ref[dst, vat] = dv.astype(BF16)
                    dq_s[p] += dq

            each(size // SUB_ROWS, sub_work)

    each(blocks, block_work)
    dq = jnp.concatenate([join_heads(dq_s[p]) for p in range(pairs)], axis=1) * SCALE
    dqp_ref[...] = rope_back(
        dq, wide(cos_ref[...], width), wide(sin_ref[...], width)
    ).astype(BF16)


def rows_in_order(order_ref, ref, groups):
    if groups == 1:
        return ref[...]
    rows = ref.shape[0] // 16
    return jnp.concatenate(
        [
            ref[pl.ds(pl.multiple_of((order_ref[0] ^ j) * rows, 16), rows), :]
            for j in chunk_order()
        ],
        axis=0,
    )


def qkv_grad_kernel(n, nt, no, order_ref, at_ref, dqp_ref, cos_ref, sin_ref, *rest):
    terms = rest[:nt]
    chunks = rest[nt : nt + n]
    outs = rest[nt + n : nt + n + no]
    da_ref, w, sems = rest[nt + n + no :]
    width = dqp_ref.shape[1]
    copies = weight_copies(order_ref, chunks, w, sems, (0, 3 * width))
    dkv = total([term[...] for term in terms])
    dkp = rope_back(
        dkv[:, :width], wide(cos_ref[...], width), wide(sin_ref[...], width)
    ).astype(BF16)
    d = jnp.concatenate([dkp, dkv[:, width:].astype(BF16)], axis=1)
    both = dot_nn(rows_in_order(order_ref, at_ref, no), d).astype(BF16)
    size = both.shape[0] // no
    for i, out in enumerate(outs):
        out[...] = both[i * size : (i + 1) * size]
    for copy in copies:
        copy.wait()
    da = dot_nt(dqp_ref[...], w[:, :width]) + dot_nt(d, w[:, width:])
    da_ref[...] = da.astype(BF16)


def call(kernel, out_shape, specs, scratch, args):
    return pl.pallas_call(
        kernel,
        out_shape=out_shape,
        in_specs=specs,
        out_specs=jax.tree.map(lambda _: VM, out_shape),
        scratch_shapes=scratch,
    )(*args)


def rotary_tables(positions):
    half = HEAD_DIM // 2
    inverse = jnp.exp(jnp.arange(half, dtype=F32) * (-2.0 * math.log(THETA) / HEAD_DIM))
    angles = positions.astype(F32)[:, None] * inverse[None, :]
    angles = jnp.concatenate([angles] * 4, axis=-1)
    return jnp.cos(angles), jnp.sin(angles)


def adam_update(tensor, gradient, moment, second):
    moment = BETA_ONE * moment + (1.0 - BETA_ONE) * gradient
    second = BETA_TWO * second + (1.0 - BETA_TWO) * gradient * gradient
    first_hat = moment / (1.0 - BETA_ONE**STEP)
    second_hat = second / (1.0 - BETA_TWO**STEP)
    tensor = tensor - LEARN_RATE * (first_hat / (jnp.sqrt(second_hat) + ADAM_EPS) + DECAY * tensor)
    return tensor, moment, second


def gsum_kernel(nf, width, units, w_ref, *rest):
    firsts, lasts = rest[:nf], rest[nf : 2 * nf]
    g_ref, gain_ref = rest[2 * nf :]
    kv = total([term[...] for term in firsts])
    rest_sum = total([term[...] for term in lasts])
    two = rest_sum[:, : 3 * units]
    oq = rest_sum[:, rest_sum.shape[1] - 2 * width :]
    one = jnp.concatenate([oq[:, :width], kv, oq[:, width:]], axis=1)
    wf = w_ref[...].astype(BF16).astype(F32)
    cut = 4 * width
    sums = [
        jnp.sum(wf[:, : 3 * width] * one[:, : 3 * width], axis=1, keepdims=True),
        jnp.sum(wf[:, cut : cut + 2 * units] * two[:, : 2 * units], axis=1, keepdims=True),
    ]
    lane = lax.broadcasted_iota(jnp.int32, (wf.shape[0], 128), 1)
    cols = jnp.where(lane == 0, sums[0], jnp.where(lane == 1, sums[1], 0.0))
    gain_ref[...] = jnp.transpose(cols)[:2, :]
    g_ref[:, :cut] = one
    g_ref[:, cut:] = two


def adam_kernel(w_ref, g_ref, m_ref, v_ref, w_out, m_out, v_out):
    w_out[...], m_out[...], v_out[...] = adam_update(
        w_ref[...], g_ref[...], m_ref[...], v_ref[...]
    )


def gadam_kernel(a_ref, b_ref, w_ref, m_ref, v_ref, g_out, w_out, m_out, v_out):
    w = w_ref[...]
    grad = (a_ref[...] + b_ref[...]) / w.astype(BF16).astype(F32)
    g_out[...] = grad
    w_out[...], m_out[...], v_out[...] = adam_update(w, grad, m_ref[...], v_ref[...])


def lnback_kernel(
    x_ref, da_ref, db_ref, dhid_ref, g_ref, hid_ref, fa_ref, fb_ref, grad_ref, out_ref
):
    xhat, inv = norm_parts(x_ref[...])
    da = da_ref[...].astype(F32) + db_ref[...].astype(F32)
    grad_ref[...] = dhid_ref[...] + norm_back(da, xhat, inv, g_ref[0:1, :])
    out_ref[...] = hid_ref[...] + (fa_ref[...].astype(F32) + fb_ref[...].astype(F32))


def head_swap(x):
    if lax.axis_size("head") == 1:
        return jnp.zeros_like(x)
    return swap(x, "head", 1)


def layer(
    inputs, cotangent, weights, gains, weight_moment, weight_second, gain_moment, gain_second
):
    heads = lax.axis_size("head")
    width = HEADS // heads * HEAD_DIM
    units = FF // heads
    toks, d = inputs.shape
    rows = weights.shape[0]
    n = lax.axis_size(TOKENS_AX)
    seq = toks * n
    me = lax.axis_index(TOKENS_AX).astype(jnp.int32)
    order = me.reshape(1)
    pairs = width // 128

    wb = weights.astype(BF16)
    gb = gains.astype(BF16)
    wq_cols = 4 * width + 128
    rest_pad = -(3 * units) % 128
    rest_cols = 3 * units + rest_pad
    w_first = jnp.concatenate([wb[:, : 4 * width], jnp.pad(gb.T, ((0, 0), (0, 126)))], axis=1)
    w_rest = jnp.pad(wb[:, 4 * width :], ((0, 0), (0, rest_pad)))
    first_chunks = gather(w_first)
    cos, sin = rotary_tables(me * toks + jnp.arange(toks, dtype=jnp.int32))

    nw = len(first_chunks)
    wsem = pltpu.SemaphoreType.DMA((nw,))
    parts = 4 if staged() else 1

    a_t, q, kv, g = call(
        partial(qkv_kernel, nw),
        [sds((d, toks), BF16), sds((toks, width), BF16), sds((toks, 2 * width), BF16), sds((8, d), F32)],
        [SM, VM, VM, VM] + [ANY] * nw,
        [pltpu.VMEM((d, wq_cols), BF16), wsem],
        [order, inputs, cos, sin] + first_chunks,
    )
    keys = gather(kv)
    rest_chunks = gather(w_rest)
    nk = len(keys)
    block_rows = min(KEY_ROWS, seq)
    blocks = seq // block_rows
    ksem = pltpu.SemaphoreType.DMA((nk,))

    attn, lse, out_part = call(
        partial(attend_kernel, nk, nw, blocks),
        [sds((toks, width), BF16), sds((8, 2 * toks), F32), sds((toks, d), BF16)],
        [SM, VM] + [ANY] * (nk + nw),
        [
            pltpu.VMEM((block_rows, 2 * width), BF16),
            pltpu.VMEM((d, width), BF16),
            pltpu.VMEM((pairs, 2 * toks, 1), F32),
            pltpu.VMEM((pairs, 2 * toks, 1), F32),
            pltpu.VMEM((pairs, 2 * toks, 128), F32),
            ksem,
            wsem,
        ],
        [order, q] + keys + first_chunks,
    )
    out_other = head_swap(out_part)

    hidden, ffn_part, db_part, b, dz, mixed = call(
        partial(ffn_kernel, nw),
        [
            sds((toks, d), F32),
            sds((toks, d), BF16),
            sds((toks, d), BF16),
            sds((toks, d), BF16),
            sds((toks, 2 * units), BF16),
            sds((toks, units), BF16),
        ],
        [SM] + [VM] * 5 + [ANY] * nw,
        [pltpu.VMEM((d, rest_cols), BF16), wsem],
        [order, inputs, out_part, out_other, cotangent, g] + rest_chunks,
    )
    db_other = head_swap(db_part)
    ffn_other = head_swap(ffn_part)
    grad_cols = rest_cols + 2 * width
    part_sem = pltpu.SemaphoreType.DMA((parts,))
    group = [sds((d // parts, grad_cols), BF16)] * parts
    rest_grads = pl.pallas_call(
        partial(ffn_grad_kernel, parts),
        out_shape=group,
        in_specs=[SM] + [VM] * 4,
        out_specs=[HBM] * parts,
        scratch_shapes=[
            pltpu.VMEM((d, rest_cols), F32),
            pltpu.VMEM((d, rest_cols), BF16),
            part_sem,
        ],
        name="ffngrad",
    )(order, b, dz, cotangent, mixed)

    both = (pairs, 2 * toks, 128)
    *kv_groups, dhid, dqp = call(
        partial(back_kernel, nk, nw, parts, blocks),
        [sds((seq // parts, 2 * width), BF16)] * parts
        + [sds((toks, d), F32), sds((toks, width), BF16)],
        [SM] + [VM] * 10 + [ANY] * (nk + nw),
        [
            pltpu.VMEM((block_rows, 2 * width), BF16),
            pltpu.VMEM((d, width), BF16),
            pltpu.VMEM(both, F32),
            pltpu.VMEM(both, BF16),
            pltpu.VMEM(both, BF16),
            pltpu.VMEM((8, 2 * toks), F32),
            ksem,
            wsem,
        ],
        [order, q, attn, lse, hidden, cotangent, g, db_part, db_other, cos, sin]
        + keys
        + first_chunks,
    )
    rest_grads = pl.pallas_call(
        partial(oq_grad_kernel, parts, rest_cols),
        out_shape=group,
        in_specs=[SM] + [VM] * 4 + [HBM] * parts,
        out_specs=[HBM] * parts,
        scratch_shapes=[pltpu.VMEM((d, toks), BF16), pltpu.VMEM((d, 2 * width), BF16), part_sem],
        input_output_aliases={5 + i: i for i in range(parts)},
        name="oqgrad",
    )(order, a_t, dqp, dhid, attn, *rest_grads)
    if staged():
        kv_terms = scatter_sum(kv_groups, pair_swap(kv_groups))
        rest_terms = scatter_sum(rest_grads, pair_swap(rest_grads))
    else:
        kv_terms = native_sum(*kv_groups)
        rest_terms = native_sum(*rest_grads)
    nt = len(kv_terms)
    *w_groups, da_part = call(
        partial(qkv_grad_kernel, nw, nt, parts),
        [sds((d // parts, 2 * width), BF16)] * parts + [sds((toks, d), BF16)],
        [SM] + [VM] * 4 + [VM] * nt + [ANY] * nw,
        [pltpu.VMEM((d, 3 * width), BF16), wsem],
        [order, a_t, dqp, cos, sin] + kv_terms + first_chunks,
    )
    da_other = head_swap(da_part)
    input_grad, outputs = call(
        lnback_kernel,
        [sds((toks, d), F32)] * 2,
        [VM] * 8,
        [],
        [inputs, da_part, da_other, dhid, g, hidden, ffn_part, ffn_other],
    )
    if staged():
        first_terms = scatter_sum(w_groups, pair_swap(w_groups))
    else:
        first_terms = native_sum(*w_groups)
    full = weights.shape
    weight_grad, gain_part = call(
        partial(gsum_kernel, nt, width, units),
        [sds(full, F32), sds(gains.shape, F32)],
        [VM] * (1 + 2 * nt),
        [],
        [weights] + first_terms + rest_terms,
    )
    gain_other = head_swap(gain_part)
    step_rows = rows // 2 if rows % 16 == 0 else rows
    cells = pl.BlockSpec((step_rows, full[1]), lambda i: (i, 0))
    new_weights, new_weight_moment, new_weight_second = pl.pallas_call(
        adam_kernel,
        grid=(rows // step_rows,),
        out_shape=[sds(full, F32)] * 3,
        in_specs=[cells] * 4,
        out_specs=[cells] * 3,
        name="adam",
    )(weights, weight_grad, weight_moment, weight_second)
    gain_grad, new_gains, new_gain_moment, new_gain_second = call(
        gadam_kernel,
        [sds(gains.shape, F32)] * 4,
        [VM] * 5,
        [],
        [gain_part, gain_other, gains, gain_moment, gain_second],
    )
    return (
        outputs,
        input_grad,
        weight_grad,
        gain_grad,
        new_weights,
        new_weight_moment,
        new_weight_second,
        new_gains,
        new_gain_moment,
        new_gain_second,
    )


def solution(mesh):
    rows = P(("blk", "shard"), None)
    cells = P(("blk", "shard"), "head")
    lanes = P(None, ("blk", "shard"))
    return jax.shard_map(
        layer,
        mesh=mesh,
        in_specs=(rows, rows, cells, lanes, cells, cells, lanes, lanes),
        out_specs=(rows, rows, cells, lanes, cells, cells, cells, lanes, lanes, lanes),
        check_vma=False,
    )
```

```python
from functools import partial
import math

import jax
import jax.numpy as jnp
from jax import lax
from jax.experimental import pallas as pl
from jax.experimental.pallas import tpu as pltpu
from jax.sharding import PartitionSpec as P


HEADS = 12
HEAD_DIM = 64
FF = 1152
STEP = 3

NORM_EPS = 1e-05
THETA = 160000.0
BETA_ONE = 0.9
BETA_TWO = 0.98
LEARN_RATE = 0.2
ADAM_EPS = 1e-06
DECAY = 0.01
NEG_LARGE = -1e30
SCALE = 1.0 / math.sqrt(HEAD_DIM)
TOKENS_AX = ("blk", "shard")
F32 = jnp.float32
BF16 = jnp.bfloat16
KEY_ROWS = 2048
SUB_ROWS = 512


VM = pl.BlockSpec(memory_space=pltpu.VMEM)
SM = pl.BlockSpec(memory_space=pltpu.SMEM)
ANY = pl.BlockSpec(memory_space=pl.ANY)
HBM = pl.BlockSpec(memory_space=pltpu.HBM)


def near(x):
    return pltpu.with_memory_space_constraint(x, pltpu.VMEM) if staged() else x


def sds(shape, dtype):
    return jax.ShapeDtypeStruct(shape, dtype)


def dot_nn(a, b):
    return lax.dot_general(a, b, (((1,), (0,)), ((), ())), preferred_element_type=F32)


def dot_nt(a, b):
    return lax.dot_general(a, b, (((1,), (1,)), ((), ())), preferred_element_type=F32)


def dot_tn(a, b):
    return lax.dot_general(a, b, (((0,), (0,)), ((), ())), preferred_element_type=F32)


def swap(x, axis, bits):
    size = lax.axis_size(axis)
    return lax.ppermute(x, axis, [(i, i ^ bits) for i in range(size)])


def staged():
    return lax.axis_size("blk") == 4 and lax.axis_size("shard") == 4


def chunk_order():
    return [z * 4 + x * 2 + c for c in range(2) for x in range(2) for z in range(4)]


def gather(x):
    if not staged():
        return [lax.all_gather(x, TOKENS_AX, axis=0, tiled=True)]
    got = {0: x}
    got[8] = swap(x, "blk", 2)
    got[4] = swap(x, "blk", 1)
    got[12] = swap(got[8], "blk", 1)
    for z in range(4):
        got[z * 4 + 2] = swap(got[z * 4], "shard", 2)
    for z in range(4):
        for h in (0, 2):
            got[z * 4 + h + 1] = swap(got[z * 4 + h], "shard", 1)
    return [got[j] for j in chunk_order()]


def add_kernel(keep, got, *rest):
    outs = rest[:4]
    kept, done, sems = rest[4:]
    rows = outs[0].shape[0]
    at = [pl.ds(i * rows, rows) for i in range(4)]
    loads = [
        pltpu.make_async_copy(keep.at[at[i], :], kept.at[at[i], :], sems.at[0, i])
        for i in range(4)
    ]
    stores = [pltpu.make_async_copy(done.at[at[i], :], outs[i], sems.at[1, i]) for i in range(4)]
    for copy in loads:
        copy.start()
    for i in range(4):
        loads[i].wait()
        done[at[i], :] = (kept[at[i], :].astype(F32) + got[at[i], :].astype(F32)).astype(BF16)
        stores[i].start()
    for copy in stores:
        copy.wait()


def pair_add(keep, recv):
    rows, cols = keep.shape[0] // 4, keep.shape[1]
    return pl.pallas_call(
        add_kernel,
        out_shape=[sds((rows, cols), BF16)] * 4,
        in_specs=[HBM, VM],
        out_specs=[HBM] * 4,
        scratch_shapes=[pltpu.VMEM(keep.shape, BF16)] * 2 + [pltpu.SemaphoreType.DMA((2, 4))],
        name="pair_add",
    )(keep, near(recv))


def native_sum(part):
    return [lax.psum_scatter(part, TOKENS_AX, scatter_dimension=0, tiled=True)]


def pair_swap(groups):
    return [swap(groups[2 + x], "shard", 1) for x in (1, 0)][::-1]


def scatter_sum(groups, recv):
    s = pair_add(groups[1], recv[1])
    got = {z: swap(s[z], "shard", 2) for z in (3, 2, 1, 0)}
    keep = pair_add(groups[0], recv[0])

    def block(z, *more):
        return total([keep[z], got[z], *more]).astype(BF16)

    far = swap(block(3), "blk", 1)
    two = swap(block(2, far), "blk", 2)
    one = swap(block(1), "blk", 1)
    return [keep[0], got[0], one, two]


def total(terms):
    out = terms[0].astype(F32)
    for term in terms[1:]:
        out = out + term.astype(F32)
    return out


def weight_copies(order_ref, chunks, dst, sems, cols=None):
    rows = chunks[0].shape[0]
    copies = []
    for i, chunk in enumerate(chunks):
        src = chunk if cols is None else chunk.at[:, pl.ds(cols[0], cols[1])]
        if len(chunks) == 1:
            at = pl.ds(0, rows)
        else:
            at = pl.ds(pl.multiple_of((order_ref[0] ^ chunk_order()[i]) * rows, 16), rows)
        copies.append(pltpu.make_async_copy(src, dst.at[at, :], sems.at[i]))
    for copy in copies:
        copy.start()
    return copies


def group_copies(src, outs, sems, first_col):
    rows, cols = src.shape[0] // len(outs), src.shape[1]
    copies = [
        pltpu.make_async_copy(
            src.at[pl.ds(i * rows, rows), :], out.at[:, pl.ds(first_col, cols)], sems.at[i]
        )
        for i, out in enumerate(outs)
    ]
    for copy in copies:
        copy.start()
    for copy in copies:
        copy.wait()


def emit_blocks(order_ref, acc, dst, staged_rows):
    if not staged_rows:
        dst[...] = acc[...].astype(BF16)
        return
    rows = acc.shape[0] // 16
    for i, j in enumerate(chunk_order()):
        at = pl.ds(pl.multiple_of((order_ref[0] ^ j) * rows, 8), rows)
        dst[pl.ds(i * rows, rows), :] = acc[at, :].astype(BF16)


def norm_parts(v):
    centre = v - jnp.mean(v, axis=-1, keepdims=True)
    inv = lax.rsqrt(jnp.mean(centre * centre, axis=-1, keepdims=True) + NORM_EPS)
    return centre * inv, inv


def norm_back(u, xhat, inv, g):
    s = u * g
    return inv * (
        s
        - jnp.mean(s, axis=-1, keepdims=True)
        - xhat * jnp.mean(s * xhat, axis=-1, keepdims=True)
    )


def low_half(shape):
    lane = lax.broadcasted_iota(jnp.int32, shape, 1)
    return (lane & (HEAD_DIM - 1)) < HEAD_DIM // 2


def turn(u):
    width = u.shape[1]
    half = HEAD_DIM // 2
    left = pltpu.roll(u, width - half, 1)
    right = pltpu.roll(u, half, 1)
    return left, right, low_half(u.shape)


def rope(u, cos, sin):
    left, right, low = turn(u)
    return u * cos + jnp.where(low, -left, right) * sin


def rope_back(w, cos, sin):
    left, right, low = turn(w * sin)
    return w * cos + jnp.where(low, left, -right)


def wide(table, width):
    return jnp.concatenate([table] * (width // table.shape[1]), axis=1)


def two_heads(pair):
    lane = lax.broadcasted_iota(jnp.int32, pair.shape, 1)
    zero = jnp.zeros_like(pair)
    first = lane < HEAD_DIM
    return jnp.concatenate(
        [jnp.where(first, pair, zero), jnp.where(first, zero, pair)], axis=0
    )


def join_heads(both):
    rows = both.shape[0] // 2
    lane = lax.broadcasted_iota(jnp.int32, (rows, both.shape[1]), 1)
    return jnp.where(lane < HEAD_DIM, both[:rows], both[rows:])


def as_row(col):
    return jnp.transpose(jnp.broadcast_to(col, (col.shape[0], 128)))[0:1, :]


def qkv_kernel(n, order_ref, x_ref, cos_ref, sin_ref, *rest):
    chunks = rest[:n]
    at_ref, q_ref, kv_ref, g_ref, w, sems = rest[n:]
    width = q_ref.shape[1]
    copies = weight_copies(order_ref, chunks, w, sems)
    xhat, _ = norm_parts(x_ref[...])
    for copy in copies:
        copy.wait()
    row = lax.broadcasted_iota(jnp.int32, (8, 128), 0)
    lane = lax.broadcasted_iota(jnp.int32, (8, 128), 1)
    pick = jnp.where(row == lane, 1.0, 0.0).astype(BF16)
    g = dot_nt(pick, w[:, 4 * width : 4 * width + 128])
    g_ref[...] = g
    a = (xhat * g[0:1, :]).astype(BF16)
    at_ref[...] = jnp.transpose(a)
    cos = wide(cos_ref[...], width)
    sin = wide(sin_ref[...], width)
    q_ref[...] = rope(dot_nn(a, w[:, :width]), cos, sin).astype(BF16)
    kv_ref[:, :width] = rope(dot_nn(a, w[:, width : 2 * width]), cos, sin).astype(BF16)
    kv_ref[:, width:] = dot_nn(a, w[:, 2 * width : 3 * width]).astype(BF16)


def key_copies(chunks, dst, sems, block):
    if len(chunks) == 1:
        rows = dst.shape[0]
        at = pl.ds(pl.multiple_of(block * rows, rows), rows)
        copies = [pltpu.make_async_copy(chunks[0].at[at, :], dst, sems.at[0])]
    else:
        rows = chunks[0].shape[0]
        copies = [
            pltpu.make_async_copy(chunk, dst.at[pl.ds(i * rows, rows), :], sems.at[i])
            for i, chunk in enumerate(chunks)
        ]
    for copy in copies:
        copy.start()
    return copies


def each(count, body):
    if count == 1:
        body(0)
    else:
        lax.fori_loop(0, count, lambda i, c: (body(i), c)[1], 0)


def attend_kernel(n, nw, blocks, order_ref, q_ref, *rest):
    keys = rest[:n]
    wos = rest[n : n + nw]
    attn_ref, lse_ref, out_ref, kv, wo, m_s, l_s, acc_s, ksem, wsem = rest[n + nw :]
    width = q_ref.shape[1]
    pairs = width // 128
    wcopies = weight_copies(order_ref, wos, wo, wsem, (3 * width, width))
    m_s[...] = jnp.full(m_s.shape, NEG_LARGE, F32)
    l_s[...] = jnp.zeros(l_s.shape, F32)
    acc_s[...] = jnp.zeros(acc_s.shape, F32)

    def block_work(block):
        for copy in key_copies(keys, kv, ksem, block):
            copy.wait()
        for p in range(pairs):
            at = slice(p * 128, p * 128 + 128)
            qm = two_heads(q_ref[:, at]) * jnp.asarray(SCALE, BF16)
            s = dot_nt(qm, kv[:, at])
            m_old = m_s[p]
            m_new = jnp.maximum(m_old, jnp.max(s, axis=1, keepdims=True))
            factor = jnp.exp(m_old - m_new)
            e = jnp.exp(s - m_new)
            l_s[p] = l_s[p] * factor + jnp.sum(e, axis=1, keepdims=True)
            m_s[p] = m_new
            acc_s[p] = acc_s[p] * factor + dot_nn(
                e.astype(BF16), kv[:, width + p * 128 : width + p * 128 + 128]
            )

    each(blocks, block_work)
    for p in range(pairs):
        attn_ref[:, p * 128 : p * 128 + 128] = join_heads(acc_s[p] / l_s[p]).astype(BF16)
        lse_ref[p : p + 1, :] = as_row(m_s[p] + jnp.log(l_s[p]))
    for copy in wcopies:
        copy.wait()
    out_ref[...] = dot_nt(attn_ref[...], wo[...]).astype(BF16)


def gelu_parts(z):
    cdf = 0.5 * (1.0 + lax.erf(z * 0.7071067811865476))
    density = jnp.exp(-0.5 * z * z) * 0.3989422804014327
    return z * cdf, cdf + z * density


def ffn_kernel(nw, order_ref, x_ref, pa_ref, pb_ref, cot_ref, g_ref, *rest):
    ws = rest[:nw]
    hid_ref, out_ref, db_ref, b_ref, dz_ref, mixed_ref, w, wsem = rest[nw:]
    units = mixed_ref.shape[1]
    copies = weight_copies(order_ref, ws, w, wsem)
    hidden = x_ref[...] + (pa_ref[...].astype(F32) + pb_ref[...].astype(F32))
    hid_ref[...] = hidden
    xhat, _ = norm_parts(hidden)
    b = (xhat * g_ref[1:2, :]).astype(BF16)
    b_ref[...] = b
    cb = cot_ref[...].astype(BF16)
    for copy in copies:
        copy.wait()
    z = dot_nn(b, w[:, : 2 * units])
    gate = z[:, units:]
    act, slope = gelu_parts(z[:, :units])
    dmix = dot_nn(cb, w[:, 2 * units : 3 * units])
    dz = jnp.concatenate([dmix * gate * slope, dmix * act], axis=1).astype(BF16)
    dz_ref[...] = dz
    db_ref[...] = dot_nt(dz, w[:, : 2 * units]).astype(BF16)
    mixed = (act * gate).astype(BF16)
    mixed_ref[...] = mixed
    out_ref[...] = dot_nt(mixed, w[:, 2 * units : 3 * units]).astype(BF16)


def ffn_grad_kernel(no, order_ref, b_ref, dz_ref, cot_ref, mixed_ref, *rest):
    outs = rest[:no]
    acc, dst, sems = rest[no:]
    two = dz_ref.shape[1]
    acc[:, :two] = dot_tn(b_ref[...], dz_ref[...])
    half = mixed_ref.shape[1]
    acc[:, two : two + half] = dot_tn(cot_ref[...].astype(BF16), mixed_ref[...])
    acc[:, two + half :] = jnp.zeros((acc.shape[0], acc.shape[1] - two - half), F32)
    emit_blocks(order_ref, acc, dst, no > 1)
    group_copies(dst, outs, sems, 0)


def oq_grad_kernel(no, first_col, order_ref, at_ref, dqp_ref, dhid_ref, attn_ref, *rest):
    outs = rest[no : 2 * no]
    ht, dst, sems = rest[2 * no :]
    width = dqp_ref.shape[1]
    ht[...] = jnp.transpose(dhid_ref[...].astype(BF16))
    a_t, h_t = rows_in_order(order_ref, at_ref, no), rows_in_order(order_ref, ht, no)
    dst[:, :width] = dot_nn(a_t, dqp_ref[...]).astype(BF16)
    dst[:, width:] = dot_nn(h_t, attn_ref[...]).astype(BF16)
    group_copies(dst, outs, sems, first_col)


def back_tile(k, v, qm, dom, lse_row, dot_row):
    prob = jnp.exp(dot_nt(k, qm) - lse_row)
    ds = (prob * (dot_nt(v, dom) - dot_row)).astype(BF16)
    return dot_nn(ds, qm), dot_nn(prob.astype(BF16), dom), dot_tn(ds, k)


def back_kernel(
    n, nw, no, blocks, order_ref, q_ref, attn_ref, lse_ref, hid_ref, cot_ref, g_ref,
    da_ref, db_ref, cos_ref, sin_ref, *rest
):
    keys = rest[:n]
    wos = rest[n : n + nw]
    outs = rest[n + nw : n + nw + no]
    dhid_ref, dqp_ref, kv, wo, dq_s, qm_s, dom_s, row_s, ksem, wsem = rest[n + nw + no :]
    width = q_ref.shape[1]
    pairs = width // 128
    wcopies = weight_copies(order_ref, wos, wo, wsem, (3 * width, width))
    first = key_copies(keys, kv, ksem, 0) if blocks == 1 else None
    xhat, inv = norm_parts(hid_ref[...])
    db = da_ref[...].astype(F32) + db_ref[...].astype(F32)
    dhid = cot_ref[...] + norm_back(db, xhat, inv, g_ref[1:2, :])
    dhid_ref[...] = dhid
    for copy in wcopies:
        copy.wait()
    dattn = dot_nn(dhid.astype(BF16), wo[...]).astype(BF16)
    for p in range(pairs):
        at = slice(p * 128, p * 128 + 128)
        qm_s[p] = two_heads(q_ref[:, at]) * jnp.asarray(SCALE, BF16)
        dom = two_heads(dattn[:, at])
        dom_s[p] = dom
        both = jnp.concatenate([attn_ref[:, at]] * 2, axis=0)
        dots = jnp.sum(dom.astype(F32) * both.astype(F32), axis=1, keepdims=True)
        row_s[p : p + 1, :] = as_row(dots)
    dq_s[...] = jnp.zeros(dq_s.shape, F32)
    block_rows = kv.shape[0]

    def block_work(block):
        for copy in first or key_copies(keys, kv, ksem, block):
            copy.wait()
        for group, out_ref in enumerate(outs):
            size = block_rows // no

            def sub_work(sub):
                start = group * size + sub * SUB_ROWS
                src = pl.ds(pl.multiple_of(start, SUB_ROWS), SUB_ROWS)
                dst = pl.ds(
                    pl.multiple_of(block * block_rows + sub * SUB_ROWS, SUB_ROWS), SUB_ROWS
                )
                for p in range(pairs):
                    at = slice(p * 128, p * 128 + 128)
                    vat = slice(width + p * 128, width + p * 128 + 128)
                    dk, dv, dq = back_tile(
                        kv[src, at], kv[src, vat], qm_s[p], dom_s[p],
                        lse_ref[p : p + 1, :], row_s[p : p + 1, :],
                    )
                    out_ref[dst, at] = dk.astype(BF16)
                    out_ref[dst, vat] = dv.astype(BF16)
                    dq_s[p] += dq

            each(size // SUB_ROWS, sub_work)

    each(blocks, block_work)
    dq = jnp.concatenate([join_heads(dq_s[p]) for p in range(pairs)], axis=1) * SCALE
    dqp_ref[...] = rope_back(
        dq, wide(cos_ref[...], width), wide(sin_ref[...], width)
    ).astype(BF16)


def rows_in_order(order_ref, ref, groups):
    if groups == 1:
        return ref[...]
    rows = ref.shape[0] // 16
    return jnp.concatenate(
        [
            ref[pl.ds(pl.multiple_of((order_ref[0] ^ j) * rows, 16), rows), :]
            for j in chunk_order()
        ],
        axis=0,
    )


def qkv_grad_kernel(n, nt, no, order_ref, at_ref, dqp_ref, cos_ref, sin_ref, *rest):
    terms = rest[:nt]
    chunks = rest[nt : nt + n]
    outs = rest[nt + n : nt + n + no]
    da_ref, w, sems = rest[nt + n + no :]
    width = dqp_ref.shape[1]
    copies = weight_copies(order_ref, chunks, w, sems, (0, 3 * width))
    dkv = total([term[...] for term in terms])
    dkp = rope_back(
        dkv[:, :width], wide(cos_ref[...], width), wide(sin_ref[...], width)
    ).astype(BF16)
    d = jnp.concatenate([dkp, dkv[:, width:].astype(BF16)], axis=1)
    both = dot_nn(rows_in_order(order_ref, at_ref, no), d).astype(BF16)
    size = both.shape[0] // no
    for i, out in enumerate(outs):
        out[...] = both[i * size : (i + 1) * size]
    for copy in copies:
        copy.wait()
    da = dot_nt(dqp_ref[...], w[:, :width]) + dot_nt(d, w[:, width:])
    da_ref[...] = da.astype(BF16)


def call(kernel, out_shape, specs, scratch, args):
    return pl.pallas_call(
        kernel,
        out_shape=out_shape,
        in_specs=specs,
        out_specs=jax.tree.map(lambda _: VM, out_shape),
        scratch_shapes=scratch,
    )(*args)


def rotary_tables(positions):
    half = HEAD_DIM // 2
    inverse = jnp.exp(jnp.arange(half, dtype=F32) * (-2.0 * math.log(THETA) / HEAD_DIM))
    angles = positions.astype(F32)[:, None] * inverse[None, :]
    angles = jnp.concatenate([angles] * 4, axis=-1)
    return jnp.cos(angles), jnp.sin(angles)


def adam_update(tensor, gradient, moment, second):
    moment = BETA_ONE * moment + (1.0 - BETA_ONE) * gradient
    second = BETA_TWO * second + (1.0 - BETA_TWO) * gradient * gradient
    first_hat = moment / (1.0 - BETA_ONE**STEP)
    second_hat = second / (1.0 - BETA_TWO**STEP)
    tensor = tensor - LEARN_RATE * (first_hat / (jnp.sqrt(second_hat) + ADAM_EPS) + DECAY * tensor)
    return tensor, moment, second


def gsum_kernel(nf, width, units, w_ref, *rest):
    firsts, lasts = rest[:nf], rest[nf : 2 * nf]
    g_ref, gain_ref = rest[2 * nf :]
    kv = total([term[...] for term in firsts])
    rest_sum = total([term[...] for term in lasts])
    two = rest_sum[:, : 3 * units]
    oq = rest_sum[:, rest_sum.shape[1] - 2 * width :]
    one = jnp.concatenate([oq[:, :width], kv, oq[:, width:]], axis=1)
    wf = w_ref[...].astype(BF16).astype(F32)
    cut = 4 * width
    sums = [
        jnp.sum(wf[:, : 3 * width] * one[:, : 3 * width], axis=1, keepdims=True),
        jnp.sum(wf[:, cut : cut + 2 * units] * two[:, : 2 * units], axis=1, keepdims=True),
    ]
    lane = lax.broadcasted_iota(jnp.int32, (wf.shape[0], 128), 1)
    cols = jnp.where(lane == 0, sums[0], jnp.where(lane == 1, sums[1], 0.0))
    gain_ref[...] = jnp.transpose(cols)[:2, :]
    g_ref[:, :cut] = one
    g_ref[:, cut:] = two


def adam_kernel(w_ref, g_ref, m_ref, v_ref, w_out, m_out, v_out):
    w_out[...], m_out[...], v_out[...] = adam_update(
        w_ref[...], g_ref[...], m_ref[...], v_ref[...]
    )


def gadam_kernel(a_ref, b_ref, w_ref, m_ref, v_ref, g_out, w_out, m_out, v_out):
    w = w_ref[...]
    grad = (a_ref[...] + b_ref[...]) / w.astype(BF16).astype(F32)
    g_out[...] = grad
    w_out[...], m_out[...], v_out[...] = adam_update(w, grad, m_ref[...], v_ref[...])


def lnback_kernel(
    x_ref, da_ref, db_ref, dhid_ref, g_ref, hid_ref, fa_ref, fb_ref, grad_ref, out_ref
):
    xhat, inv = norm_parts(x_ref[...])
    da = da_ref[...].astype(F32) + db_ref[...].astype(F32)
    grad_ref[...] = dhid_ref[...] + norm_back(da, xhat, inv, g_ref[0:1, :])
    out_ref[...] = hid_ref[...] + (fa_ref[...].astype(F32) + fb_ref[...].astype(F32))


def head_swap(x):
    if lax.axis_size("head") == 1:
        return jnp.zeros_like(x)
    return swap(x, "head", 1)


def layer(
    inputs, cotangent, weights, gains, weight_moment, weight_second, gain_moment, gain_second
):
    heads = lax.axis_size("head")
    width = HEADS // heads * HEAD_DIM
    units = FF // heads
    toks, d = inputs.shape
    rows = weights.shape[0]
    n = lax.axis_size(TOKENS_AX)
    seq = toks * n
    me = lax.axis_index(TOKENS_AX).astype(jnp.int32)
    order = me.reshape(1)
    pairs = width // 128

    wb = weights.astype(BF16)
    gb = gains.astype(BF16)
    wq_cols = 4 * width + 128
    rest_pad = -(3 * units) % 128
    rest_cols = 3 * units + rest_pad
    w_first = jnp.concatenate([wb[:, : 4 * width], jnp.pad(gb.T, ((0, 0), (0, 126)))], axis=1)
    w_rest = jnp.pad(wb[:, 4 * width :], ((0, 0), (0, rest_pad)))
    first_chunks = gather(w_first)
    cos, sin = rotary_tables(me * toks + jnp.arange(toks, dtype=jnp.int32))

    nw = len(first_chunks)
    wsem = pltpu.SemaphoreType.DMA((nw,))
    parts = 4 if staged() else 1

    a_t, q, kv, g = call(
        partial(qkv_kernel, nw),
        [sds((d, toks), BF16), sds((toks, width), BF16), sds((toks, 2 * width), BF16), sds((8, d), F32)],
        [SM, VM, VM, VM] + [ANY] * nw,
        [pltpu.VMEM((d, wq_cols), BF16), wsem],
        [order, inputs, cos, sin] + [near(x) for x in first_chunks],
    )
    keys = gather(kv)
    rest_chunks = gather(w_rest)
    nk = len(keys)
    block_rows = min(KEY_ROWS, seq)
    blocks = seq // block_rows
    ksem = pltpu.SemaphoreType.DMA((nk,))

    attn, lse, out_part = call(
        partial(attend_kernel, nk, nw, blocks),
        [sds((toks, width), BF16), sds((8, 2 * toks), F32), sds((toks, d), BF16)],
        [SM, VM] + [ANY] * (nk + nw),
        [
            pltpu.VMEM((block_rows, 2 * width), BF16),
            pltpu.VMEM((d, width), BF16),
            pltpu.VMEM((pairs, 2 * toks, 1), F32),
            pltpu.VMEM((pairs, 2 * toks, 1), F32),
            pltpu.VMEM((pairs, 2 * toks, 128), F32),
            ksem,
            wsem,
        ],
        [order, q] + [near(x) for x in keys] + first_chunks,
    )
    out_other = head_swap(out_part)

    hidden, ffn_part, db_part, b, dz, mixed = call(
        partial(ffn_kernel, nw),
        [
            sds((toks, d), F32),
            sds((toks, d), BF16),
            sds((toks, d), BF16),
            sds((toks, d), BF16),
            sds((toks, 2 * units), BF16),
            sds((toks, units), BF16),
        ],
        [SM] + [VM] * 5 + [ANY] * nw,
        [pltpu.VMEM((d, rest_cols), BF16), wsem],
        [order, inputs, out_part, near(out_other), cotangent, g] + [near(x) for x in rest_chunks],
    )
    db_other = head_swap(db_part)
    ffn_other = head_swap(ffn_part)
    grad_cols = rest_cols + 2 * width
    part_sem = pltpu.SemaphoreType.DMA((parts,))
    group = [sds((d // parts, grad_cols), BF16)] * parts
    rest_grads = pl.pallas_call(
        partial(ffn_grad_kernel, parts),
        out_shape=group,
        in_specs=[SM] + [VM] * 4,
        out_specs=[HBM] * parts,
        scratch_shapes=[
            pltpu.VMEM((d, rest_cols), F32),
            pltpu.VMEM((d, rest_cols), BF16),
            part_sem,
        ],
        name="ffngrad",
    )(order, b, dz, cotangent, mixed)

    both = (pairs, 2 * toks, 128)
    *kv_groups, dhid, dqp = call(
        partial(back_kernel, nk, nw, parts, blocks),
        [sds((seq // parts, 2 * width), BF16)] * parts
        + [sds((toks, d), F32), sds((toks, width), BF16)],
        [SM] + [VM] * 10 + [ANY] * (nk + nw),
        [
            pltpu.VMEM((block_rows, 2 * width), BF16),
            pltpu.VMEM((d, width), BF16),
            pltpu.VMEM(both, F32),
            pltpu.VMEM(both, BF16),
            pltpu.VMEM(both, BF16),
            pltpu.VMEM((8, 2 * toks), F32),
            ksem,
            wsem,
        ],
        [order, q, attn, lse, hidden, cotangent, g, db_part, near(db_other), cos, sin]
        + keys
        + first_chunks,
    )
    rest_grads = pl.pallas_call(
        partial(oq_grad_kernel, parts, rest_cols),
        out_shape=group,
        in_specs=[SM] + [VM] * 4 + [HBM] * parts,
        out_specs=[HBM] * parts,
        scratch_shapes=[pltpu.VMEM((d, toks), BF16), pltpu.VMEM((d, 2 * width), BF16), part_sem],
        input_output_aliases={5 + i: i for i in range(parts)},
        name="oqgrad",
    )(order, a_t, dqp, dhid, attn, *rest_grads)
    if staged():
        kv_terms = scatter_sum(kv_groups, pair_swap(kv_groups))
        rest_terms = scatter_sum(rest_grads, pair_swap(rest_grads))
    else:
        kv_terms = native_sum(*kv_groups)
        rest_terms = native_sum(*rest_grads)
    nt = len(kv_terms)
    *w_groups, da_part = call(
        partial(qkv_grad_kernel, nw, nt, parts),
        [sds((d // parts, 2 * width), BF16)] * parts + [sds((toks, d), BF16)],
        [SM] + [VM] * 4 + [VM] * nt + [ANY] * nw,
        [pltpu.VMEM((d, 3 * width), BF16), wsem],
        [order, a_t, dqp, cos, sin] + [near(x) for x in kv_terms] + first_chunks,
    )
    da_other = head_swap(da_part)
    input_grad, outputs = call(
        lnback_kernel,
        [sds((toks, d), F32)] * 2,
        [VM] * 8,
        [],
        [inputs, da_part, near(da_other), dhid, g, hidden, ffn_part, near(ffn_other)],
    )
    if staged():
        first_terms = scatter_sum(w_groups, pair_swap(w_groups))
    else:
        first_terms = native_sum(*w_groups)
    full = weights.shape
    weight_grad, gain_part = call(
        partial(gsum_kernel, nt, width, units),
        [sds(full, F32), sds(gains.shape, F32)],
        [VM] * (1 + 2 * nt),
        [],
        [weights] + [near(x) for x in first_terms + rest_terms],
    )
    gain_other = head_swap(gain_part)
    step_rows = rows // 2 if rows % 16 == 0 else rows
    cells = pl.BlockSpec((step_rows, full[1]), lambda i: (i, 0))
    new_weights, new_weight_moment, new_weight_second = pl.pallas_call(
        adam_kernel,
        grid=(rows // step_rows,),
        out_shape=[sds(full, F32)] * 3,
        in_specs=[cells] * 4,
        out_specs=[cells] * 3,
        name="adam",
    )(weights, weight_grad, weight_moment, weight_second)
    gain_grad, new_gains, new_gain_moment, new_gain_second = call(
        gadam_kernel,
        [sds(gains.shape, F32)] * 4,
        [VM] * 5,
        [],
        [near(gain_part), near(gain_other), gains, gain_moment, gain_second],
    )
    return (
        outputs,
        input_grad,
        weight_grad,
        gain_grad,
        new_weights,
        new_weight_moment,
        new_weight_second,
        new_gains,
        new_gain_moment,
        new_gain_second,
    )


def solution(mesh):
    rows = P(("blk", "shard"), None)
    cells = P(("blk", "shard"), "head")
    lanes = P(None, ("blk", "shard"))
    return jax.shard_map(
        layer,
        mesh=mesh,
        in_specs=(rows, rows, cells, lanes, cells, cells, lanes, lanes),
        out_specs=(rows, rows, cells, lanes, cells, cells, cells, lanes, lanes, lanes),
        check_vma=False,
    )
```

```python
from functools import partial
import math

import jax
import jax.numpy as jnp
from jax import lax
from jax.experimental import pallas as pl
from jax.experimental.pallas import tpu as pltpu
from jax.sharding import PartitionSpec as P


HEADS = 12
HEAD_DIM = 64
FF = 1152
STEP = 3

NORM_EPS = 1e-05
THETA = 160000.0
BETA_ONE = 0.9
BETA_TWO = 0.98
LEARN_RATE = 0.2
ADAM_EPS = 1e-06
DECAY = 0.01
NEG_LARGE = -1e30
SCALE = 1.0 / math.sqrt(HEAD_DIM)
TOKENS_AX = ("blk", "shard")
F32 = jnp.float32
BF16 = jnp.bfloat16
KEY_ROWS = 2048
SUB_ROWS = 512


VM = pl.BlockSpec(memory_space=pltpu.VMEM)
SM = pl.BlockSpec(memory_space=pltpu.SMEM)
ANY = pl.BlockSpec(memory_space=pl.ANY)
HBM = pl.BlockSpec(memory_space=pltpu.HBM)


def near(x):
    return pltpu.with_memory_space_constraint(x, pltpu.VMEM) if staged() else x


def sds(shape, dtype):
    return jax.ShapeDtypeStruct(shape, dtype)


def dot_nn(a, b):
    return lax.dot_general(a, b, (((1,), (0,)), ((), ())), preferred_element_type=F32)


def dot_nt(a, b):
    return lax.dot_general(a, b, (((1,), (1,)), ((), ())), preferred_element_type=F32)


def dot_tn(a, b):
    return lax.dot_general(a, b, (((0,), (0,)), ((), ())), preferred_element_type=F32)


def swap(x, axis, bits):
    size = lax.axis_size(axis)
    return lax.ppermute(x, axis, [(i, i ^ bits) for i in range(size)])


def staged():
    return lax.axis_size("blk") == 4 and lax.axis_size("shard") == 4


def chunk_order():
    return [z * 4 + x * 2 + c for c in range(2) for x in range(2) for z in range(4)]


def gather(x):
    if not staged():
        return [lax.all_gather(x, TOKENS_AX, axis=0, tiled=True)]
    got = {0: x}
    got[8] = swap(x, "blk", 2)
    got[4] = swap(x, "blk", 1)
    got[12] = swap(got[8], "blk", 1)
    for z in range(4):
        got[z * 4 + 2] = swap(got[z * 4], "shard", 2)
    for z in range(4):
        for h in (0, 2):
            got[z * 4 + h + 1] = swap(got[z * 4 + h], "shard", 1)
    return [got[j] for j in chunk_order()]


def add_kernel(keep, got, *rest):
    outs = rest[:4]
    kept, done, sems = rest[4:]
    rows = outs[0].shape[0]
    at = [pl.ds(i * rows, rows) for i in range(4)]
    loads = [
        pltpu.make_async_copy(keep.at[at[i], :], kept.at[at[i], :], sems.at[0, i])
        for i in range(4)
    ]
    stores = [pltpu.make_async_copy(done.at[at[i], :], outs[i], sems.at[1, i]) for i in range(4)]
    for copy in loads:
        copy.start()
    for i in range(4):
        loads[i].wait()
        done[at[i], :] = (kept[at[i], :].astype(F32) + got[at[i], :].astype(F32)).astype(BF16)
        stores[i].start()
    for copy in stores:
        copy.wait()


def pair_add(keep, recv):
    rows, cols = keep.shape[0] // 4, keep.shape[1]
    return pl.pallas_call(
        add_kernel,
        out_shape=[sds((rows, cols), BF16)] * 4,
        in_specs=[HBM, VM],
        out_specs=[HBM] * 4,
        scratch_shapes=[pltpu.VMEM(keep.shape, BF16)] * 2 + [pltpu.SemaphoreType.DMA((2, 4))],
        name="pair_add",
    )(keep, near(recv))


def native_sum(part):
    return [lax.psum_scatter(part, TOKENS_AX, scatter_dimension=0, tiled=True)]


def pair_swap(groups):
    return [swap(groups[2 + x], "shard", 1) for x in (1, 0)][::-1]


def scatter_sum(groups, recv):
    s = pair_add(groups[1], recv[1])
    got = {z: swap(s[z], "shard", 2) for z in (3, 2, 1, 0)}
    keep = pair_add(groups[0], recv[0])

    def block(z, *more):
        return total([keep[z], got[z], *more]).astype(BF16)

    far = swap(block(3), "blk", 1)
    two = swap(block(2, far), "blk", 2)
    one = swap(block(1), "blk", 1)
    return [keep[0], got[0], one, two]


def total(terms):
    out = terms[0].astype(F32)
    for term in terms[1:]:
        out = out + term.astype(F32)
    return out


def weight_copies(order_ref, chunks, dst, sems, cols=None):
    rows = chunks[0].shape[0]
    copies = []
    for i, chunk in enumerate(chunks):
        src = chunk if cols is None else chunk.at[:, pl.ds(cols[0], cols[1])]
        if len(chunks) == 1:
            at = pl.ds(0, rows)
        else:
            at = pl.ds(pl.multiple_of((order_ref[0] ^ chunk_order()[i]) * rows, 16), rows)
        copies.append(pltpu.make_async_copy(src, dst.at[at, :], sems.at[i]))
    for copy in copies:
        copy.start()
    return copies


def group_copies(src, outs, sems, first_col):
    rows, cols = src.shape[0] // len(outs), src.shape[1]
    copies = [
        pltpu.make_async_copy(
            src.at[pl.ds(i * rows, rows), :], out.at[:, pl.ds(first_col, cols)], sems.at[i]
        )
        for i, out in enumerate(outs)
    ]
    for copy in copies:
        copy.start()
    for copy in copies:
        copy.wait()


def emit_blocks(order_ref, acc, dst, staged_rows):
    if not staged_rows:
        dst[...] = acc[...].astype(BF16)
        return
    rows = acc.shape[0] // 16
    for i, j in enumerate(chunk_order()):
        at = pl.ds(pl.multiple_of((order_ref[0] ^ j) * rows, 8), rows)
        dst[pl.ds(i * rows, rows), :] = acc[at, :].astype(BF16)


def norm_parts(v):
    centre = v - jnp.mean(v, axis=-1, keepdims=True)
    inv = lax.rsqrt(jnp.mean(centre * centre, axis=-1, keepdims=True) + NORM_EPS)
    return centre * inv, inv


def norm_back(u, xhat, inv, g):
    s = u * g
    return inv * (
        s
        - jnp.mean(s, axis=-1, keepdims=True)
        - xhat * jnp.mean(s * xhat, axis=-1, keepdims=True)
    )


def low_half(shape):
    lane = lax.broadcasted_iota(jnp.int32, shape, 1)
    return (lane & (HEAD_DIM - 1)) < HEAD_DIM // 2


def turn(u):
    width = u.shape[1]
    half = HEAD_DIM // 2
    left = pltpu.roll(u, width - half, 1)
    right = pltpu.roll(u, half, 1)
    return left, right, low_half(u.shape)


def rope(u, cos, sin):
    left, right, low = turn(u)
    return u * cos + jnp.where(low, -left, right) * sin


def rope_back(w, cos, sin):
    left, right, low = turn(w * sin)
    return w * cos + jnp.where(low, left, -right)


def wide(table, width):
    return jnp.concatenate([table] * (width // table.shape[1]), axis=1)


def two_heads(pair):
    lane = lax.broadcasted_iota(jnp.int32, pair.shape, 1)
    zero = jnp.zeros_like(pair)
    first = lane < HEAD_DIM
    return jnp.concatenate(
        [jnp.where(first, pair, zero), jnp.where(first, zero, pair)], axis=0
    )


def join_heads(both):
    rows = both.shape[0] // 2
    lane = lax.broadcasted_iota(jnp.int32, (rows, both.shape[1]), 1)
    return jnp.where(lane < HEAD_DIM, both[:rows], both[rows:])


def as_row(col):
    return jnp.transpose(jnp.broadcast_to(col, (col.shape[0], 128)))[0:1, :]


def qkv_kernel(n, order_ref, x_ref, cos_ref, sin_ref, *rest):
    chunks = rest[:n]
    at_ref, q_ref, kv_ref, g_ref, w, sems = rest[n:]
    width = q_ref.shape[1]
    copies = weight_copies(order_ref, chunks, w, sems)
    xhat, _ = norm_parts(x_ref[...])
    for copy in copies:
        copy.wait()
    row = lax.broadcasted_iota(jnp.int32, (8, 128), 0)
    lane = lax.broadcasted_iota(jnp.int32, (8, 128), 1)
    pick = jnp.where(row == lane, 1.0, 0.0).astype(BF16)
    g = dot_nt(pick, w[:, 4 * width : 4 * width + 128])
    g_ref[...] = g
    a = (xhat * g[0:1, :]).astype(BF16)
    at_ref[...] = jnp.transpose(a)
    cos = wide(cos_ref[...], width)
    sin = wide(sin_ref[...], width)
    q_ref[...] = rope(dot_nn(a, w[:, :width]), cos, sin).astype(BF16)
    kv_ref[:, :width] = rope(dot_nn(a, w[:, width : 2 * width]), cos, sin).astype(BF16)
    kv_ref[:, width:] = dot_nn(a, w[:, 2 * width : 3 * width]).astype(BF16)


def key_copies(chunks, dst, sems, block):
    if len(chunks) == 1:
        rows = dst.shape[0]
        at = pl.ds(pl.multiple_of(block * rows, rows), rows)
        copies = [pltpu.make_async_copy(chunks[0].at[at, :], dst, sems.at[0])]
    else:
        rows = chunks[0].shape[0]
        copies = [
            pltpu.make_async_copy(chunk, dst.at[pl.ds(i * rows, rows), :], sems.at[i])
            for i, chunk in enumerate(chunks)
        ]
    for copy in copies:
        copy.start()
    return copies


def each(count, body):
    if count == 1:
        body(0)
    else:
        lax.fori_loop(0, count, lambda i, c: (body(i), c)[1], 0)


def attend_kernel(n, nw, blocks, order_ref, q_ref, *rest):
    keys = rest[:n]
    wos = rest[n : n + nw]
    attn_ref, lse_ref, out_ref, kv, wo, m_s, l_s, acc_s, ksem, wsem = rest[n + nw :]
    width = q_ref.shape[1]
    pairs = width // 128
    wcopies = weight_copies(order_ref, wos, wo, wsem, (3 * width, width))
    m_s[...] = jnp.full(m_s.shape, NEG_LARGE, F32)
    l_s[...] = jnp.zeros(l_s.shape, F32)
    acc_s[...] = jnp.zeros(acc_s.shape, F32)

    def block_work(block):
        for copy in key_copies(keys, kv, ksem, block):
            copy.wait()
        for p in range(pairs):
            at = slice(p * 128, p * 128 + 128)
            qm = two_heads(q_ref[:, at]) * jnp.asarray(SCALE, BF16)
            s = dot_nt(qm, kv[:, at])
            m_old = m_s[p]
            m_new = jnp.maximum(m_old, jnp.max(s, axis=1, keepdims=True))
            factor = jnp.exp(m_old - m_new)
            e = jnp.exp(s - m_new)
            l_s[p] = l_s[p] * factor + jnp.sum(e, axis=1, keepdims=True)
            m_s[p] = m_new
            acc_s[p] = acc_s[p] * factor + dot_nn(
                e.astype(BF16), kv[:, width + p * 128 : width + p * 128 + 128]
            )

    each(blocks, block_work)
    for p in range(pairs):
        attn_ref[:, p * 128 : p * 128 + 128] = join_heads(acc_s[p] / l_s[p]).astype(BF16)
        lse_ref[p : p + 1, :] = as_row(m_s[p] + jnp.log(l_s[p]))
    for copy in wcopies:
        copy.wait()
    out_ref[...] = dot_nt(attn_ref[...], wo[...]).astype(BF16)


def gelu_parts(z):
    cdf = 0.5 * (1.0 + lax.erf(z * 0.7071067811865476))
    density = jnp.exp(-0.5 * z * z) * 0.3989422804014327
    return z * cdf, cdf + z * density


def ffn_kernel(nw, order_ref, x_ref, pa_ref, pb_ref, cot_ref, g_ref, *rest):
    ws = rest[:nw]
    hid_ref, out_ref, db_ref, b_ref, dz_ref, mixed_ref, w, wsem = rest[nw:]
    units = mixed_ref.shape[1]
    copies = weight_copies(order_ref, ws, w, wsem)
    hidden = x_ref[...] + (pa_ref[...].astype(F32) + pb_ref[...].astype(F32))
    hid_ref[...] = hidden
    xhat, _ = norm_parts(hidden)
    b = (xhat * g_ref[1:2, :]).astype(BF16)
    b_ref[...] = b
    cb = cot_ref[...].astype(BF16)
    for copy in copies:
        copy.wait()
    z = dot_nn(b, w[:, : 2 * units])
    gate = z[:, units:]
    act, slope = gelu_parts(z[:, :units])
    dmix = dot_nn(cb, w[:, 2 * units : 3 * units])
    dz = jnp.concatenate([dmix * gate * slope, dmix * act], axis=1).astype(BF16)
    dz_ref[...] = dz
    db_ref[...] = dot_nt(dz, w[:, : 2 * units]).astype(BF16)
    mixed = (act * gate).astype(BF16)
    mixed_ref[...] = mixed
    out_ref[...] = dot_nt(mixed, w[:, 2 * units : 3 * units]).astype(BF16)


def ffn_grad_kernel(no, order_ref, b_ref, dz_ref, cot_ref, mixed_ref, *rest):
    outs = rest[:no]
    acc, dst, sems = rest[no:]
    two = dz_ref.shape[1]
    acc[:, :two] = dot_tn(b_ref[...], dz_ref[...])
    half = mixed_ref.shape[1]
    acc[:, two : two + half] = dot_tn(cot_ref[...].astype(BF16), mixed_ref[...])
    acc[:, two + half :] = jnp.zeros((acc.shape[0], acc.shape[1] - two - half), F32)
    emit_blocks(order_ref, acc, dst, no > 1)
    group_copies(dst, outs, sems, 0)


def oq_grad_kernel(no, first_col, order_ref, at_ref, dqp_ref, dhid_ref, attn_ref, *rest):
    outs = rest[no : 2 * no]
    ht, dst, sems = rest[2 * no :]
    width = dqp_ref.shape[1]
    ht[...] = jnp.transpose(dhid_ref[...].astype(BF16))
    a_t, h_t = rows_in_order(order_ref, at_ref, no), rows_in_order(order_ref, ht, no)
    dst[:, :width] = dot_nn(a_t, dqp_ref[...]).astype(BF16)
    dst[:, width:] = dot_nn(h_t, attn_ref[...]).astype(BF16)
    group_copies(dst, outs, sems, first_col)


def back_tile(k, v, qm, dom, lse_row, dot_row):
    prob = jnp.exp(dot_nt(k, qm) - lse_row)
    ds = (prob * (dot_nt(v, dom) - dot_row)).astype(BF16)
    return dot_nn(ds, qm), dot_nn(prob.astype(BF16), dom), dot_tn(ds, k)


def back_kernel(
    n, nw, no, blocks, order_ref, q_ref, attn_ref, lse_ref, hid_ref, cot_ref, g_ref,
    da_ref, db_ref, cos_ref, sin_ref, *rest
):
    keys = rest[:n]
    wos = rest[n : n + nw]
    outs = rest[n + nw : n + nw + no]
    dhid_ref, dqp_ref, kv, wo, dq_s, qm_s, dom_s, row_s, ksem, wsem = rest[n + nw + no :]
    width = q_ref.shape[1]
    pairs = width // 128
    wcopies = weight_copies(order_ref, wos, wo, wsem, (3 * width, width))
    first = key_copies(keys, kv, ksem, 0) if blocks == 1 else None
    xhat, inv = norm_parts(hid_ref[...])
    db = da_ref[...].astype(F32) + db_ref[...].astype(F32)
    dhid = cot_ref[...] + norm_back(db, xhat, inv, g_ref[1:2, :])
    dhid_ref[...] = dhid
    for copy in wcopies:
        copy.wait()
    dattn = dot_nn(dhid.astype(BF16), wo[...]).astype(BF16)
    for p in range(pairs):
        at = slice(p * 128, p * 128 + 128)
        qm_s[p] = two_heads(q_ref[:, at]) * jnp.asarray(SCALE, BF16)
        dom = two_heads(dattn[:, at])
        dom_s[p] = dom
        both = jnp.concatenate([attn_ref[:, at]] * 2, axis=0)
        dots = jnp.sum(dom.astype(F32) * both.astype(F32), axis=1, keepdims=True)
        row_s[p : p + 1, :] = as_row(dots)
    dq_s[...] = jnp.zeros(dq_s.shape, F32)
    block_rows = kv.shape[0]

    def block_work(block):
        for copy in first or key_copies(keys, kv, ksem, block):
            copy.wait()
        for group, out_ref in enumerate(outs):
            size = block_rows // no

            def sub_work(sub):
                start = group * size + sub * SUB_ROWS
                src = pl.ds(pl.multiple_of(start, SUB_ROWS), SUB_ROWS)
                dst = pl.ds(
                    pl.multiple_of(block * block_rows + sub * SUB_ROWS, SUB_ROWS), SUB_ROWS
                )
                for p in range(pairs):
                    at = slice(p * 128, p * 128 + 128)
                    vat = slice(width + p * 128, width + p * 128 + 128)
                    dk, dv, dq = back_tile(
                        kv[src, at], kv[src, vat], qm_s[p], dom_s[p],
                        lse_ref[p : p + 1, :], row_s[p : p + 1, :],
                    )
                    out_ref[dst, at] = dk.astype(BF16)
                    out_ref[dst, vat] = dv.astype(BF16)
                    dq_s[p] += dq

            each(size // SUB_ROWS, sub_work)

    each(blocks, block_work)
    dq = jnp.concatenate([join_heads(dq_s[p]) for p in range(pairs)], axis=1) * SCALE
    dqp_ref[...] = rope_back(
        dq, wide(cos_ref[...], width), wide(sin_ref[...], width)
    ).astype(BF16)


def rows_in_order(order_ref, ref, groups):
    if groups == 1:
        return ref[...]
    rows = ref.shape[0] // 16
    return jnp.concatenate(
        [
            ref[pl.ds(pl.multiple_of((order_ref[0] ^ j) * rows, 16), rows), :]
            for j in chunk_order()
        ],
        axis=0,
    )


def qkv_grad_kernel(n, nt, no, order_ref, at_ref, dqp_ref, cos_ref, sin_ref, *rest):
    terms = rest[:nt]
    chunks = rest[nt : nt + n]
    outs = rest[nt + n : nt + n + no]
    da_ref, w, sems = rest[nt + n + no :]
    width = dqp_ref.shape[1]
    copies = weight_copies(order_ref, chunks, w, sems, (0, 3 * width))
    dkv = total([term[...] for term in terms])
    dkp = rope_back(
        dkv[:, :width], wide(cos_ref[...], width), wide(sin_ref[...], width)
    ).astype(BF16)
    d = jnp.concatenate([dkp, dkv[:, width:].astype(BF16)], axis=1)
    both = dot_nn(rows_in_order(order_ref, at_ref, no), d).astype(BF16)
    size = both.shape[0] // no
    for i, out in enumerate(outs):
        out[...] = both[i * size : (i + 1) * size]
    for copy in copies:
        copy.wait()
    da = dot_nt(dqp_ref[...], w[:, :width]) + dot_nt(d, w[:, width:])
    da_ref[...] = da.astype(BF16)


def call(kernel, out_shape, specs, scratch, args):
    return pl.pallas_call(
        kernel,
        out_shape=out_shape,
        in_specs=specs,
        out_specs=jax.tree.map(lambda _: VM, out_shape),
        scratch_shapes=scratch,
    )(*args)


def rotary_tables(positions):
    half = HEAD_DIM // 2
    inverse = jnp.exp(jnp.arange(half, dtype=F32) * (-2.0 * math.log(THETA) / HEAD_DIM))
    angles = positions.astype(F32)[:, None] * inverse[None, :]
    angles = jnp.concatenate([angles] * 4, axis=-1)
    return jnp.cos(angles), jnp.sin(angles)


def adam_update(tensor, gradient, moment, second):
    moment = BETA_ONE * moment + (1.0 - BETA_ONE) * gradient
    second = BETA_TWO * second + (1.0 - BETA_TWO) * gradient * gradient
    first_hat = moment / (1.0 - BETA_ONE**STEP)
    second_hat = second / (1.0 - BETA_TWO**STEP)
    tensor = tensor - LEARN_RATE * (first_hat / (jnp.sqrt(second_hat) + ADAM_EPS) + DECAY * tensor)
    return tensor, moment, second


def gsum_kernel(nf, width, units, w_ref, *rest):
    firsts, lasts = rest[:nf], rest[nf : 2 * nf]
    g_ref, gain_ref = rest[2 * nf :]
    kv = total([term[...] for term in firsts])
    rest_sum = total([term[...] for term in lasts])
    two = rest_sum[:, : 3 * units]
    oq = rest_sum[:, rest_sum.shape[1] - 2 * width :]
    one = jnp.concatenate([oq[:, :width], kv, oq[:, width:]], axis=1)
    wf = w_ref[...].astype(BF16).astype(F32)
    cut = 4 * width
    sums = [
        jnp.sum(wf[:, : 3 * width] * one[:, : 3 * width], axis=1, keepdims=True),
        jnp.sum(wf[:, cut : cut + 2 * units] * two[:, : 2 * units], axis=1, keepdims=True),
    ]
    lane = lax.broadcasted_iota(jnp.int32, (wf.shape[0], 128), 1)
    cols = jnp.where(lane == 0, sums[0], jnp.where(lane == 1, sums[1], 0.0))
    gain_ref[...] = jnp.transpose(cols)[:2, :]
    g_ref[:, :cut] = one
    g_ref[:, cut:] = two


def adam_kernel(w_ref, g_ref, m_ref, v_ref, w_out, m_out, v_out):
    w_out[...], m_out[...], v_out[...] = adam_update(
        w_ref[...], g_ref[...], m_ref[...], v_ref[...]
    )


def gadam_kernel(a_ref, b_ref, w_ref, m_ref, v_ref, g_out, w_out, m_out, v_out):
    w = w_ref[...]
    grad = (a_ref[...] + b_ref[...]) / w.astype(BF16).astype(F32)
    g_out[...] = grad
    w_out[...], m_out[...], v_out[...] = adam_update(w, grad, m_ref[...], v_ref[...])


def lnback_kernel(
    x_ref, da_ref, db_ref, dhid_ref, g_ref, hid_ref, fa_ref, fb_ref, grad_ref, out_ref
):
    xhat, inv = norm_parts(x_ref[...])
    da = da_ref[...].astype(F32) + db_ref[...].astype(F32)
    grad_ref[...] = dhid_ref[...] + norm_back(da, xhat, inv, g_ref[0:1, :])
    out_ref[...] = hid_ref[...] + (fa_ref[...].astype(F32) + fb_ref[...].astype(F32))


def head_swap(x):
    if lax.axis_size("head") == 1:
        return jnp.zeros_like(x)
    return swap(x, "head", 1)


def layer(
    inputs, cotangent, weights, gains, weight_moment, weight_second, gain_moment, gain_second
):
    heads = lax.axis_size("head")
    width = HEADS // heads * HEAD_DIM
    units = FF // heads
    toks, d = inputs.shape
    rows = weights.shape[0]
    n = lax.axis_size(TOKENS_AX)
    seq = toks * n
    me = lax.axis_index(TOKENS_AX).astype(jnp.int32)
    order = me.reshape(1)
    pairs = width // 128

    wb = weights.astype(BF16)
    gb = gains.astype(BF16)
    wq_cols = 4 * width + 128
    rest_pad = -(3 * units) % 128
    rest_cols = 3 * units + rest_pad
    w_first = jnp.concatenate([wb[:, : 4 * width], jnp.pad(gb.T, ((0, 0), (0, 126)))], axis=1)
    w_rest = jnp.pad(wb[:, 4 * width :], ((0, 0), (0, rest_pad)))
    first_chunks = gather(w_first)
    cos, sin = rotary_tables(me * toks + jnp.arange(toks, dtype=jnp.int32))

    nw = len(first_chunks)
    wsem = pltpu.SemaphoreType.DMA((nw,))
    parts = 4 if staged() else 1

    a_t, q, kv, g = call(
        partial(qkv_kernel, nw),
        [sds((d, toks), BF16), sds((toks, width), BF16), sds((toks, 2 * width), BF16), sds((8, d), F32)],
        [SM, VM, VM, VM] + [ANY] * nw,
        [pltpu.VMEM((d, wq_cols), BF16), wsem],
        [order, inputs, cos, sin] + first_chunks,
    )
    keys = gather(kv)
    rest_chunks = gather(w_rest)
    nk = len(keys)
    block_rows = min(KEY_ROWS, seq)
    blocks = seq // block_rows
    ksem = pltpu.SemaphoreType.DMA((nk,))

    attn, lse, out_part = call(
        partial(attend_kernel, nk, nw, blocks),
        [sds((toks, width), BF16), sds((8, 2 * toks), F32), sds((toks, d), BF16)],
        [SM, VM] + [ANY] * (nk + nw),
        [
            pltpu.VMEM((block_rows, 2 * width), BF16),
            pltpu.VMEM((d, width), BF16),
            pltpu.VMEM((pairs, 2 * toks, 1), F32),
            pltpu.VMEM((pairs, 2 * toks, 1), F32),
            pltpu.VMEM((pairs, 2 * toks, 128), F32),
            ksem,
            wsem,
        ],
        [order, q] + keys + first_chunks,
    )
    out_other = head_swap(out_part)

    hidden, ffn_part, db_part, b, dz, mixed = call(
        partial(ffn_kernel, nw),
        [
            sds((toks, d), F32),
            sds((toks, d), BF16),
            sds((toks, d), BF16),
            sds((toks, d), BF16),
            sds((toks, 2 * units), BF16),
            sds((toks, units), BF16),
        ],
        [SM] + [VM] * 5 + [ANY] * nw,
        [pltpu.VMEM((d, rest_cols), BF16), wsem],
        [order, inputs, out_part, near(out_other), cotangent, g] + rest_chunks,
    )
    db_other = head_swap(db_part)
    ffn_other = head_swap(ffn_part)
    grad_cols = rest_cols + 2 * width
    part_sem = pltpu.SemaphoreType.DMA((parts,))
    group = [sds((d // parts, grad_cols), BF16)] * parts
    rest_grads = pl.pallas_call(
        partial(ffn_grad_kernel, parts),
        out_shape=group,
        in_specs=[SM] + [VM] * 4,
        out_specs=[HBM] * parts,
        scratch_shapes=[
            pltpu.VMEM((d, rest_cols), F32),
            pltpu.VMEM((d, rest_cols), BF16),
            part_sem,
        ],
        name="ffngrad",
    )(order, b, dz, cotangent, mixed)

    both = (pairs, 2 * toks, 128)
    *kv_groups, dhid, dqp = call(
        partial(back_kernel, nk, nw, parts, blocks),
        [sds((seq // parts, 2 * width), BF16)] * parts
        + [sds((toks, d), F32), sds((toks, width), BF16)],
        [SM] + [VM] * 10 + [ANY] * (nk + nw),
        [
            pltpu.VMEM((block_rows, 2 * width), BF16),
            pltpu.VMEM((d, width), BF16),
            pltpu.VMEM(both, F32),
            pltpu.VMEM(both, BF16),
            pltpu.VMEM(both, BF16),
            pltpu.VMEM((8, 2 * toks), F32),
            ksem,
            wsem,
        ],
        [order, q, attn, lse, hidden, cotangent, g, db_part, near(db_other), cos, sin]
        + keys
        + first_chunks,
    )
    rest_grads = pl.pallas_call(
        partial(oq_grad_kernel, parts, rest_cols),
        out_shape=group,
        in_specs=[SM] + [VM] * 4 + [HBM] * parts,
        out_specs=[HBM] * parts,
        scratch_shapes=[pltpu.VMEM((d, toks), BF16), pltpu.VMEM((d, 2 * width), BF16), part_sem],
        input_output_aliases={5 + i: i for i in range(parts)},
        name="oqgrad",
    )(order, a_t, dqp, dhid, attn, *rest_grads)
    if staged():
        kv_terms = scatter_sum(kv_groups, pair_swap(kv_groups))
        rest_terms = scatter_sum(rest_grads, pair_swap(rest_grads))
    else:
        kv_terms = native_sum(*kv_groups)
        rest_terms = native_sum(*rest_grads)
    nt = len(kv_terms)
    *w_groups, da_part = call(
        partial(qkv_grad_kernel, nw, nt, parts),
        [sds((d // parts, 2 * width), BF16)] * parts + [sds((toks, d), BF16)],
        [SM] + [VM] * 4 + [VM] * nt + [ANY] * nw,
        [pltpu.VMEM((d, 3 * width), BF16), wsem],
        [order, a_t, dqp, cos, sin] + [near(x) for x in kv_terms] + first_chunks,
    )
    da_other = head_swap(da_part)
    input_grad, outputs = call(
        lnback_kernel,
        [sds((toks, d), F32)] * 2,
        [VM] * 8,
        [],
        [inputs, da_part, near(da_other), dhid, g, hidden, ffn_part, near(ffn_other)],
    )
    if staged():
        first_terms = scatter_sum(w_groups, pair_swap(w_groups))
    else:
        first_terms = native_sum(*w_groups)
    full = weights.shape
    weight_grad, gain_part = call(
        partial(gsum_kernel, nt, width, units),
        [sds(full, F32), sds(gains.shape, F32)],
        [VM] * (1 + 2 * nt),
        [],
        [weights] + [near(x) for x in first_terms + rest_terms],
    )
    gain_other = head_swap(gain_part)
    step_rows = rows // 2 if rows % 16 == 0 else rows
    cells = pl.BlockSpec((step_rows, full[1]), lambda i: (i, 0))
    new_weights, new_weight_moment, new_weight_second = pl.pallas_call(
        adam_kernel,
        grid=(rows // step_rows,),
        out_shape=[sds(full, F32)] * 3,
        in_specs=[cells] * 4,
        out_specs=[cells] * 3,
        name="adam",
    )(weights, weight_grad, weight_moment, weight_second)
    gain_grad, new_gains, new_gain_moment, new_gain_second = call(
        gadam_kernel,
        [sds(gains.shape, F32)] * 4,
        [VM] * 5,
        [],
        [gain_part, near(gain_other), gains, gain_moment, gain_second],
    )
    return (
        outputs,
        input_grad,
        weight_grad,
        gain_grad,
        new_weights,
        new_weight_moment,
        new_weight_second,
        new_gains,
        new_gain_moment,
        new_gain_second,
    )


def solution(mesh):
    rows = P(("blk", "shard"), None)
    cells = P(("blk", "shard"), "head")
    lanes = P(None, ("blk", "shard"))
    return jax.shard_map(
        layer,
        mesh=mesh,
        in_specs=(rows, rows, cells, lanes, cells, cells, lanes, lanes),
        out_specs=(rows, rows, cells, lanes, cells, cells, cells, lanes, lanes, lanes),
        check_vma=False,
    )
```

```python
from functools import partial
import math

import jax
import jax.numpy as jnp
from jax import lax
from jax.experimental import pallas as pl
from jax.experimental.pallas import tpu as pltpu
from jax.sharding import PartitionSpec as P


HEADS = 12
HEAD_DIM = 64
FF = 1152
STEP = 3

NORM_EPS = 1e-05
THETA = 160000.0
BETA_ONE = 0.9
BETA_TWO = 0.98
LEARN_RATE = 0.2
ADAM_EPS = 1e-06
DECAY = 0.01
NEG_LARGE = -1e30
SCALE = 1.0 / math.sqrt(HEAD_DIM)
TOKENS_AX = ("blk", "shard")
F32 = jnp.float32
BF16 = jnp.bfloat16
KEY_ROWS = 2048
SUB_ROWS = 512


VM = pl.BlockSpec(memory_space=pltpu.VMEM)
SM = pl.BlockSpec(memory_space=pltpu.SMEM)
ANY = pl.BlockSpec(memory_space=pl.ANY)
HBM = pl.BlockSpec(memory_space=pltpu.HBM)


def near(x):
    return pltpu.with_memory_space_constraint(x, pltpu.VMEM) if staged() else x


def near_out(shape, dtype):
    return pltpu.VMEM(shape, dtype) if staged() else jax.ShapeDtypeStruct(shape, dtype)


def sds(shape, dtype):
    return jax.ShapeDtypeStruct(shape, dtype)


def dot_nn(a, b):
    return lax.dot_general(a, b, (((1,), (0,)), ((), ())), preferred_element_type=F32)


def dot_nt(a, b):
    return lax.dot_general(a, b, (((1,), (1,)), ((), ())), preferred_element_type=F32)


def dot_tn(a, b):
    return lax.dot_general(a, b, (((0,), (0,)), ((), ())), preferred_element_type=F32)


def swap(x, axis, bits):
    size = lax.axis_size(axis)
    return lax.ppermute(x, axis, [(i, i ^ bits) for i in range(size)])


def staged():
    return lax.axis_size("blk") == 4 and lax.axis_size("shard") == 4


def chunk_order():
    return [z * 4 + x * 2 + c for c in range(2) for x in range(2) for z in range(4)]


def gather(x):
    if not staged():
        return [lax.all_gather(x, TOKENS_AX, axis=0, tiled=True)]
    got = {0: x}
    got[8] = swap(x, "blk", 2)
    got[4] = swap(x, "blk", 1)
    got[12] = swap(got[8], "blk", 1)
    for z in range(4):
        got[z * 4 + 2] = swap(got[z * 4], "shard", 2)
    for z in range(4):
        for h in (0, 2):
            got[z * 4 + h + 1] = swap(got[z * 4 + h], "shard", 1)
    return [got[j] for j in chunk_order()]


def add_kernel(keep, got, *rest):
    outs = rest[:4]
    kept, done, sems = rest[4:]
    rows = outs[0].shape[0]
    at = [pl.ds(i * rows, rows) for i in range(4)]
    loads = [
        pltpu.make_async_copy(keep.at[at[i], :], kept.at[at[i], :], sems.at[0, i])
        for i in range(4)
    ]
    stores = [pltpu.make_async_copy(done.at[at[i], :], outs[i], sems.at[1, i]) for i in range(4)]
    for copy in loads:
        copy.start()
    for i in range(4):
        loads[i].wait()
        done[at[i], :] = (kept[at[i], :].astype(F32) + got[at[i], :].astype(F32)).astype(BF16)
        stores[i].start()
    for copy in stores:
        copy.wait()


def pair_add(keep, recv):
    rows, cols = keep.shape[0] // 4, keep.shape[1]
    return pl.pallas_call(
        add_kernel,
        out_shape=[sds((rows, cols), BF16)] * 4,
        in_specs=[HBM, VM],
        out_specs=[HBM] * 4,
        scratch_shapes=[pltpu.VMEM(keep.shape, BF16)] * 2 + [pltpu.SemaphoreType.DMA((2, 4))],
        name="pair_add",
    )(keep, near(recv))


def native_sum(part):
    return [lax.psum_scatter(part, TOKENS_AX, scatter_dimension=0, tiled=True)]


def pair_swap(groups):
    return [swap(groups[2 + x], "shard", 1) for x in (1, 0)][::-1]


def scatter_sum(groups, recv):
    s = pair_add(groups[1], recv[1])
    got = {z: swap(s[z], "shard", 2) for z in (3, 2, 1, 0)}
    keep = pair_add(groups[0], recv[0])

    def block(z, *more):
        return total([keep[z], got[z], *more]).astype(BF16)

    far = swap(block(3), "blk", 1)
    two = swap(block(2, far), "blk", 2)
    one = swap(block(1), "blk", 1)
    return [keep[0], got[0], one, two]


def total(terms):
    out = terms[0].astype(F32)
    for term in terms[1:]:
        out = out + term.astype(F32)
    return out


def weight_copies(order_ref, chunks, dst, sems, cols=None):
    rows = chunks[0].shape[0]
    copies = []
    for i, chunk in enumerate(chunks):
        src = chunk if cols is None else chunk.at[:, pl.ds(cols[0], cols[1])]
        if len(chunks) == 1:
            at = pl.ds(0, rows)
        else:
            at = pl.ds(pl.multiple_of((order_ref[0] ^ chunk_order()[i]) * rows, 16), rows)
        copies.append(pltpu.make_async_copy(src, dst.at[at, :], sems.at[i]))
    for copy in copies:
        copy.start()
    return copies


def group_copies(src, outs, sems, first_col):
    rows, cols = src.shape[0] // len(outs), src.shape[1]
    copies = [
        pltpu.make_async_copy(
            src.at[pl.ds(i * rows, rows), :], out.at[:, pl.ds(first_col, cols)], sems.at[i]
        )
        for i, out in enumerate(outs)
    ]
    for copy in copies:
        copy.start()
    for copy in copies:
        copy.wait()


def emit_blocks(order_ref, acc, dst, staged_rows):
    if not staged_rows:
        dst[...] = acc[...].astype(BF16)
        return
    rows = acc.shape[0] // 16
    for i, j in enumerate(chunk_order()):
        at = pl.ds(pl.multiple_of((order_ref[0] ^ j) * rows, 8), rows)
        dst[pl.ds(i * rows, rows), :] = acc[at, :].astype(BF16)


def norm_parts(v):
    centre = v - jnp.mean(v, axis=-1, keepdims=True)
    inv = lax.rsqrt(jnp.mean(centre * centre, axis=-1, keepdims=True) + NORM_EPS)
    return centre * inv, inv


def norm_back(u, xhat, inv, g):
    s = u * g
    return inv * (
        s
        - jnp.mean(s, axis=-1, keepdims=True)
        - xhat * jnp.mean(s * xhat, axis=-1, keepdims=True)
    )


def low_half(shape):
    lane = lax.broadcasted_iota(jnp.int32, shape, 1)
    return (lane & (HEAD_DIM - 1)) < HEAD_DIM // 2


def turn(u):
    width = u.shape[1]
    half = HEAD_DIM // 2
    left = pltpu.roll(u, width - half, 1)
    right = pltpu.roll(u, half, 1)
    return left, right, low_half(u.shape)


def rope(u, cos, sin):
    left, right, low = turn(u)
    return u * cos + jnp.where(low, -left, right) * sin


def rope_back(w, cos, sin):
    left, right, low = turn(w * sin)
    return w * cos + jnp.where(low, left, -right)


def wide(table, width):
    return jnp.concatenate([table] * (width // table.shape[1]), axis=1)


def two_heads(pair):
    lane = lax.broadcasted_iota(jnp.int32, pair.shape, 1)
    zero = jnp.zeros_like(pair)
    first = lane < HEAD_DIM
    return jnp.concatenate(
        [jnp.where(first, pair, zero), jnp.where(first, zero, pair)], axis=0
    )


def join_heads(both):
    rows = both.shape[0] // 2
    lane = lax.broadcasted_iota(jnp.int32, (rows, both.shape[1]), 1)
    return jnp.where(lane < HEAD_DIM, both[:rows], both[rows:])


def as_row(col):
    return jnp.transpose(jnp.broadcast_to(col, (col.shape[0], 128)))[0:1, :]


def qkv_kernel(n, order_ref, x_ref, cos_ref, sin_ref, *rest):
    chunks = rest[:n]
    at_ref, q_ref, kv_ref, g_ref, w, sems = rest[n:]
    width = q_ref.shape[1]
    copies = weight_copies(order_ref, chunks, w, sems)
    xhat, _ = norm_parts(x_ref[...])
    for copy in copies:
        copy.wait()
    row = lax.broadcasted_iota(jnp.int32, (8, 128), 0)
    lane = lax.broadcasted_iota(jnp.int32, (8, 128), 1)
    pick = jnp.where(row == lane, 1.0, 0.0).astype(BF16)
    g = dot_nt(pick, w[:, 4 * width : 4 * width + 128])
    g_ref[...] = g
    a = (xhat * g[0:1, :]).astype(BF16)
    at_ref[...] = jnp.transpose(a)
    cos = wide(cos_ref[...], width)
    sin = wide(sin_ref[...], width)
    q_ref[...] = rope(dot_nn(a, w[:, :width]), cos, sin).astype(BF16)
    kv_ref[:, :width] = rope(dot_nn(a, w[:, width : 2 * width]), cos, sin).astype(BF16)
    kv_ref[:, width:] = dot_nn(a, w[:, 2 * width : 3 * width]).astype(BF16)


def key_copies(chunks, dst, sems, block):
    if len(chunks) == 1:
        rows = dst.shape[0]
        at = pl.ds(pl.multiple_of(block * rows, rows), rows)
        copies = [pltpu.make_async_copy(chunks[0].at[at, :], dst, sems.at[0])]
    else:
        rows = chunks[0].shape[0]
        copies = [
            pltpu.make_async_copy(chunk, dst.at[pl.ds(i * rows, rows), :], sems.at[i])
            for i, chunk in enumerate(chunks)
        ]
    for copy in copies:
        copy.start()
    return copies


def each(count, body):
    if count == 1:
        body(0)
    else:
        lax.fori_loop(0, count, lambda i, c: (body(i), c)[1], 0)


def attend_kernel(n, nw, blocks, order_ref, q_ref, *rest):
    keys = rest[:n]
    wos = rest[n : n + nw]
    attn_ref, lse_ref, out_ref, kv, wo, m_s, l_s, acc_s, ksem, wsem = rest[n + nw :]
    width = q_ref.shape[1]
    pairs = width // 128
    wcopies = weight_copies(order_ref, wos, wo, wsem, (3 * width, width))
    m_s[...] = jnp.full(m_s.shape, NEG_LARGE, F32)
    l_s[...] = jnp.zeros(l_s.shape, F32)
    acc_s[...] = jnp.zeros(acc_s.shape, F32)

    def block_work(block):
        for copy in key_copies(keys, kv, ksem, block):
            copy.wait()
        for p in range(pairs):
            at = slice(p * 128, p * 128 + 128)
            qm = two_heads(q_ref[:, at]) * jnp.asarray(SCALE, BF16)
            s = dot_nt(qm, kv[:, at])
            m_old = m_s[p]
            m_new = jnp.maximum(m_old, jnp.max(s, axis=1, keepdims=True))
            factor = jnp.exp(m_old - m_new)
            e = jnp.exp(s - m_new)
            l_s[p] = l_s[p] * factor + jnp.sum(e, axis=1, keepdims=True)
            m_s[p] = m_new
            acc_s[p] = acc_s[p] * factor + dot_nn(
                e.astype(BF16), kv[:, width + p * 128 : width + p * 128 + 128]
            )

    each(blocks, block_work)
    for p in range(pairs):
        attn_ref[:, p * 128 : p * 128 + 128] = join_heads(acc_s[p] / l_s[p]).astype(BF16)
        lse_ref[p : p + 1, :] = as_row(m_s[p] + jnp.log(l_s[p]))
    for copy in wcopies:
        copy.wait()
    out_ref[...] = dot_nt(attn_ref[...], wo[...]).astype(BF16)


def gelu_parts(z):
    cdf = 0.5 * (1.0 + lax.erf(z * 0.7071067811865476))
    density = jnp.exp(-0.5 * z * z) * 0.3989422804014327
    return z * cdf, cdf + z * density


def ffn_kernel(nw, order_ref, x_ref, pa_ref, pb_ref, cot_ref, g_ref, *rest):
    ws = rest[:nw]
    hid_ref, out_ref, db_ref, b_ref, dz_ref, mixed_ref, w, wsem = rest[nw:]
    units = mixed_ref.shape[1]
    copies = weight_copies(order_ref, ws, w, wsem)
    hidden = x_ref[...] + (pa_ref[...].astype(F32) + pb_ref[...].astype(F32))
    hid_ref[...] = hidden
    xhat, _ = norm_parts(hidden)
    b = (xhat * g_ref[1:2, :]).astype(BF16)
    b_ref[...] = b
    cb = cot_ref[...].astype(BF16)
    for copy in copies:
        copy.wait()
    z = dot_nn(b, w[:, : 2 * units])
    gate = z[:, units:]
    act, slope = gelu_parts(z[:, :units])
    dmix = dot_nn(cb, w[:, 2 * units : 3 * units])
    dz = jnp.concatenate([dmix * gate * slope, dmix * act], axis=1).astype(BF16)
    dz_ref[...] = dz
    db_ref[...] = dot_nt(dz, w[:, : 2 * units]).astype(BF16)
    mixed = (act * gate).astype(BF16)
    mixed_ref[...] = mixed
    out_ref[...] = dot_nt(mixed, w[:, 2 * units : 3 * units]).astype(BF16)


def ffn_grad_kernel(no, order_ref, b_ref, dz_ref, cot_ref, mixed_ref, *rest):
    outs = rest[:no]
    acc, dst, sems = rest[no:]
    two = dz_ref.shape[1]
    acc[:, :two] = dot_tn(b_ref[...], dz_ref[...])
    half = mixed_ref.shape[1]
    acc[:, two : two + half] = dot_tn(cot_ref[...].astype(BF16), mixed_ref[...])
    acc[:, two + half :] = jnp.zeros((acc.shape[0], acc.shape[1] - two - half), F32)
    emit_blocks(order_ref, acc, dst, no > 1)
    group_copies(dst, outs, sems, 0)


def oq_grad_kernel(no, first_col, order_ref, at_ref, dqp_ref, dhid_ref, attn_ref, *rest):
    outs = rest[no : 2 * no]
    ht, dst, sems = rest[2 * no :]
    width = dqp_ref.shape[1]
    ht[...] = jnp.transpose(dhid_ref[...].astype(BF16))
    a_t, h_t = rows_in_order(order_ref, at_ref, no), rows_in_order(order_ref, ht, no)
    dst[:, :width] = dot_nn(a_t, dqp_ref[...]).astype(BF16)
    dst[:, width:] = dot_nn(h_t, attn_ref[...]).astype(BF16)
    group_copies(dst, outs, sems, first_col)


def back_tile(k, v, qm, dom, lse_row, dot_row):
    prob = jnp.exp(dot_nt(k, qm) - lse_row)
    ds = (prob * (dot_nt(v, dom) - dot_row)).astype(BF16)
    return dot_nn(ds, qm), dot_nn(prob.astype(BF16), dom), dot_tn(ds, k)


def back_kernel(
    n, nw, no, blocks, order_ref, q_ref, attn_ref, lse_ref, hid_ref, cot_ref, g_ref,
    da_ref, db_ref, cos_ref, sin_ref, *rest
):
    keys = rest[:n]
    wos = rest[n : n + nw]
    outs = rest[n + nw : n + nw + no]
    dhid_ref, dqp_ref, kv, wo, dq_s, qm_s, dom_s, row_s, ksem, wsem = rest[n + nw + no :]
    width = q_ref.shape[1]
    pairs = width // 128
    wcopies = weight_copies(order_ref, wos, wo, wsem, (3 * width, width))
    first = key_copies(keys, kv, ksem, 0) if blocks == 1 else None
    xhat, inv = norm_parts(hid_ref[...])
    db = da_ref[...].astype(F32) + db_ref[...].astype(F32)
    dhid = cot_ref[...] + norm_back(db, xhat, inv, g_ref[1:2, :])
    dhid_ref[...] = dhid
    for copy in wcopies:
        copy.wait()
    dattn = dot_nn(dhid.astype(BF16), wo[...]).astype(BF16)
    for p in range(pairs):
        at = slice(p * 128, p * 128 + 128)
        qm_s[p] = two_heads(q_ref[:, at]) * jnp.asarray(SCALE, BF16)
        dom = two_heads(dattn[:, at])
        dom_s[p] = dom
        both = jnp.concatenate([attn_ref[:, at]] * 2, axis=0)
        dots = jnp.sum(dom.astype(F32) * both.astype(F32), axis=1, keepdims=True)
        row_s[p : p + 1, :] = as_row(dots)
    dq_s[...] = jnp.zeros(dq_s.shape, F32)
    block_rows = kv.shape[0]

    def block_work(block):
        for copy in first or key_copies(keys, kv, ksem, block):
            copy.wait()
        for group, out_ref in enumerate(outs):
            size = block_rows // no

            def sub_work(sub):
                start = group * size + sub * SUB_ROWS
                src = pl.ds(pl.multiple_of(start, SUB_ROWS), SUB_ROWS)
                dst = pl.ds(
                    pl.multiple_of(block * block_rows + sub * SUB_ROWS, SUB_ROWS), SUB_ROWS
                )
                for p in range(pairs):
                    at = slice(p * 128, p * 128 + 128)
                    vat = slice(width + p * 128, width + p * 128 + 128)
                    dk, dv, dq = back_tile(
                        kv[src, at], kv[src, vat], qm_s[p], dom_s[p],
                        lse_ref[p : p + 1, :], row_s[p : p + 1, :],
                    )
                    out_ref[dst, at] = dk.astype(BF16)
                    out_ref[dst, vat] = dv.astype(BF16)
                    dq_s[p] += dq

            each(size // SUB_ROWS, sub_work)

    each(blocks, block_work)
    dq = jnp.concatenate([join_heads(dq_s[p]) for p in range(pairs)], axis=1) * SCALE
    dqp_ref[...] = rope_back(
        dq, wide(cos_ref[...], width), wide(sin_ref[...], width)
    ).astype(BF16)


def rows_in_order(order_ref, ref, groups):
    if groups == 1:
        return ref[...]
    rows = ref.shape[0] // 16
    return jnp.concatenate(
        [
            ref[pl.ds(pl.multiple_of((order_ref[0] ^ j) * rows, 16), rows), :]
            for j in chunk_order()
        ],
        axis=0,
    )


def qkv_grad_kernel(n, nt, no, order_ref, at_ref, dqp_ref, cos_ref, sin_ref, *rest):
    terms = rest[:nt]
    chunks = rest[nt : nt + n]
    outs = rest[nt + n : nt + n + no]
    da_ref, w, sems = rest[nt + n + no :]
    width = dqp_ref.shape[1]
    copies = weight_copies(order_ref, chunks, w, sems, (0, 3 * width))
    dkv = total([term[...] for term in terms])
    dkp = rope_back(
        dkv[:, :width], wide(cos_ref[...], width), wide(sin_ref[...], width)
    ).astype(BF16)
    d = jnp.concatenate([dkp, dkv[:, width:].astype(BF16)], axis=1)
    both = dot_nn(rows_in_order(order_ref, at_ref, no), d).astype(BF16)
    size = both.shape[0] // no
    for i, out in enumerate(outs):
        out[...] = both[i * size : (i + 1) * size]
    for copy in copies:
        copy.wait()
    da = dot_nt(dqp_ref[...], w[:, :width]) + dot_nt(d, w[:, width:])
    da_ref[...] = da.astype(BF16)


def call(kernel, out_shape, specs, scratch, args):
    return pl.pallas_call(
        kernel,
        out_shape=out_shape,
        in_specs=specs,
        out_specs=jax.tree.map(lambda _: VM, out_shape),
        scratch_shapes=scratch,
    )(*args)


def rotary_tables(positions):
    half = HEAD_DIM // 2
    inverse = jnp.exp(jnp.arange(half, dtype=F32) * (-2.0 * math.log(THETA) / HEAD_DIM))
    angles = positions.astype(F32)[:, None] * inverse[None, :]
    angles = jnp.concatenate([angles] * 4, axis=-1)
    return jnp.cos(angles), jnp.sin(angles)


def adam_update(tensor, gradient, moment, second):
    moment = BETA_ONE * moment + (1.0 - BETA_ONE) * gradient
    second = BETA_TWO * second + (1.0 - BETA_TWO) * gradient * gradient
    first_hat = moment / (1.0 - BETA_ONE**STEP)
    second_hat = second / (1.0 - BETA_TWO**STEP)
    tensor = tensor - LEARN_RATE * (first_hat / (jnp.sqrt(second_hat) + ADAM_EPS) + DECAY * tensor)
    return tensor, moment, second


def gsum_kernel(nf, width, units, w_ref, *rest):
    firsts, lasts = rest[:nf], rest[nf : 2 * nf]
    g_ref, gain_ref = rest[2 * nf :]
    kv = total([term[...] for term in firsts])
    rest_sum = total([term[...] for term in lasts])
    two = rest_sum[:, : 3 * units]
    oq = rest_sum[:, rest_sum.shape[1] - 2 * width :]
    one = jnp.concatenate([oq[:, :width], kv, oq[:, width:]], axis=1)
    wf = w_ref[...].astype(BF16).astype(F32)
    cut = 4 * width
    sums = [
        jnp.sum(wf[:, : 3 * width] * one[:, : 3 * width], axis=1, keepdims=True),
        jnp.sum(wf[:, cut : cut + 2 * units] * two[:, : 2 * units], axis=1, keepdims=True),
    ]
    lane = lax.broadcasted_iota(jnp.int32, (wf.shape[0], 128), 1)
    cols = jnp.where(lane == 0, sums[0], jnp.where(lane == 1, sums[1], 0.0))
    gain_ref[...] = jnp.transpose(cols)[:2, :]
    g_ref[:, :cut] = one
    g_ref[:, cut:] = two


def adam_kernel(w_ref, g_ref, m_ref, v_ref, w_out, m_out, v_out):
    w_out[...], m_out[...], v_out[...] = adam_update(
        w_ref[...], g_ref[...], m_ref[...], v_ref[...]
    )


def gadam_kernel(a_ref, b_ref, w_ref, m_ref, v_ref, g_out, w_out, m_out, v_out):
    w = w_ref[...]
    grad = (a_ref[...] + b_ref[...]) / w.astype(BF16).astype(F32)
    g_out[...] = grad
    w_out[...], m_out[...], v_out[...] = adam_update(w, grad, m_ref[...], v_ref[...])


def lnback_kernel(
    x_ref, da_ref, db_ref, dhid_ref, g_ref, hid_ref, fa_ref, fb_ref, grad_ref, out_ref
):
    xhat, inv = norm_parts(x_ref[...])
    da = da_ref[...].astype(F32) + db_ref[...].astype(F32)
    grad_ref[...] = dhid_ref[...] + norm_back(da, xhat, inv, g_ref[0:1, :])
    out_ref[...] = hid_ref[...] + (fa_ref[...].astype(F32) + fb_ref[...].astype(F32))


def head_swap(x):
    if lax.axis_size("head") == 1:
        return jnp.zeros_like(x)
    return swap(x, "head", 1)


def layer(
    inputs, cotangent, weights, gains, weight_moment, weight_second, gain_moment, gain_second
):
    heads = lax.axis_size("head")
    width = HEADS // heads * HEAD_DIM
    units = FF // heads
    toks, d = inputs.shape
    rows = weights.shape[0]
    n = lax.axis_size(TOKENS_AX)
    seq = toks * n
    me = lax.axis_index(TOKENS_AX).astype(jnp.int32)
    order = me.reshape(1)
    pairs = width // 128

    wb = weights.astype(BF16)
    gb = gains.astype(BF16)
    wq_cols = 4 * width + 128
    rest_pad = -(3 * units) % 128
    rest_cols = 3 * units + rest_pad
    w_first = jnp.concatenate([wb[:, : 4 * width], jnp.pad(gb.T, ((0, 0), (0, 126)))], axis=1)
    w_rest = jnp.pad(wb[:, 4 * width :], ((0, 0), (0, rest_pad)))
    first_chunks = gather(w_first)
    cos, sin = rotary_tables(me * toks + jnp.arange(toks, dtype=jnp.int32))

    nw = len(first_chunks)
    wsem = pltpu.SemaphoreType.DMA((nw,))
    parts = 4 if staged() else 1

    a_t, q, kv, g = call(
        partial(qkv_kernel, nw),
        [sds((d, toks), BF16), sds((toks, width), BF16), sds((toks, 2 * width), BF16), sds((8, d), F32)],
        [SM, VM, VM, VM] + [ANY] * nw,
        [pltpu.VMEM((d, wq_cols), BF16), wsem],
        [order, inputs, cos, sin] + first_chunks,
    )
    keys = gather(kv)
    rest_chunks = gather(w_rest)
    nk = len(keys)
    block_rows = min(KEY_ROWS, seq)
    blocks = seq // block_rows
    ksem = pltpu.SemaphoreType.DMA((nk,))

    attn, lse, out_part = call(
        partial(attend_kernel, nk, nw, blocks),
        [sds((toks, width), BF16), sds((8, 2 * toks), F32), near_out((toks, d), BF16)],
        [SM, VM] + [ANY] * (nk + nw),
        [
            pltpu.VMEM((block_rows, 2 * width), BF16),
            pltpu.VMEM((d, width), BF16),
            pltpu.VMEM((pairs, 2 * toks, 1), F32),
            pltpu.VMEM((pairs, 2 * toks, 1), F32),
            pltpu.VMEM((pairs, 2 * toks, 128), F32),
            ksem,
            wsem,
        ],
        [order, q] + keys + first_chunks,
    )
    out_other = head_swap(out_part)

    hidden, ffn_part, db_part, b, dz, mixed = call(
        partial(ffn_kernel, nw),
        [
            sds((toks, d), F32),
            sds((toks, d), BF16),
            near_out((toks, d), BF16),
            sds((toks, d), BF16),
            sds((toks, 2 * units), BF16),
            sds((toks, units), BF16),
        ],
        [SM] + [VM] * 5 + [ANY] * nw,
        [pltpu.VMEM((d, rest_cols), BF16), wsem],
        [order, inputs, near(out_part), near(out_other), cotangent, g] + rest_chunks,
    )
    db_other = head_swap(db_part)
    ffn_other = head_swap(ffn_part)
    grad_cols = rest_cols + 2 * width
    part_sem = pltpu.SemaphoreType.DMA((parts,))
    group = [sds((d // parts, grad_cols), BF16)] * parts
    rest_grads = pl.pallas_call(
        partial(ffn_grad_kernel, parts),
        out_shape=group,
        in_specs=[SM] + [VM] * 4,
        out_specs=[HBM] * parts,
        scratch_shapes=[
            pltpu.VMEM((d, rest_cols), F32),
            pltpu.VMEM((d, rest_cols), BF16),
            part_sem,
        ],
        name="ffngrad",
    )(order, b, dz, cotangent, mixed)

    both = (pairs, 2 * toks, 128)
    *kv_groups, dhid, dqp = call(
        partial(back_kernel, nk, nw, parts, blocks),
        [sds((seq // parts, 2 * width), BF16)] * parts
        + [sds((toks, d), F32), sds((toks, width), BF16)],
        [SM] + [VM] * 10 + [ANY] * (nk + nw),
        [
            pltpu.VMEM((block_rows, 2 * width), BF16),
            pltpu.VMEM((d, width), BF16),
            pltpu.VMEM(both, F32),
            pltpu.VMEM(both, BF16),
            pltpu.VMEM(both, BF16),
            pltpu.VMEM((8, 2 * toks), F32),
            ksem,
            wsem,
        ],
        [order, q, attn, lse, hidden, cotangent, g, near(db_part), near(db_other), cos, sin]
        + keys
        + first_chunks,
    )
    rest_grads = pl.pallas_call(
        partial(oq_grad_kernel, parts, rest_cols),
        out_shape=group,
        in_specs=[SM] + [VM] * 4 + [HBM] * parts,
        out_specs=[HBM] * parts,
        scratch_shapes=[pltpu.VMEM((d, toks), BF16), pltpu.VMEM((d, 2 * width), BF16), part_sem],
        input_output_aliases={5 + i: i for i in range(parts)},
        name="oqgrad",
    )(order, a_t, dqp, dhid, attn, *rest_grads)
    if staged():
        kv_terms = scatter_sum(kv_groups, pair_swap(kv_groups))
        rest_terms = scatter_sum(rest_grads, pair_swap(rest_grads))
    else:
        kv_terms = native_sum(*kv_groups)
        rest_terms = native_sum(*rest_grads)
    nt = len(kv_terms)
    *w_groups, da_part = call(
        partial(qkv_grad_kernel, nw, nt, parts),
        [sds((d // parts, 2 * width), BF16)] * parts + [sds((toks, d), BF16)],
        [SM] + [VM] * 4 + [VM] * nt + [ANY] * nw,
        [pltpu.VMEM((d, 3 * width), BF16), wsem],
        [order, a_t, dqp, cos, sin] + [near(x) for x in kv_terms] + first_chunks,
    )
    da_other = head_swap(da_part)
    input_grad, outputs = call(
        lnback_kernel,
        [sds((toks, d), F32)] * 2,
        [VM] * 8,
        [],
        [inputs, da_part, near(da_other), dhid, g, hidden, ffn_part, near(ffn_other)],
    )
    if staged():
        first_terms = scatter_sum(w_groups, pair_swap(w_groups))
    else:
        first_terms = native_sum(*w_groups)
    full = weights.shape
    weight_grad, gain_part = call(
        partial(gsum_kernel, nt, width, units),
        [sds(full, F32), near_out(gains.shape, F32)],
        [VM] * (1 + 2 * nt),
        [],
        [weights] + [near(x) for x in first_terms + rest_terms],
    )
    gain_other = head_swap(gain_part)
    step_rows = rows // 2 if rows % 16 == 0 else rows
    cells = pl.BlockSpec((step_rows, full[1]), lambda i: (i, 0))
    new_weights, new_weight_moment, new_weight_second = pl.pallas_call(
        adam_kernel,
        grid=(rows // step_rows,),
        out_shape=[sds(full, F32)] * 3,
        in_specs=[cells] * 4,
        out_specs=[cells] * 3,
        name="adam",
    )(weights, weight_grad, weight_moment, weight_second)
    gain_grad, new_gains, new_gain_moment, new_gain_second = call(
        gadam_kernel,
        [sds(gains.shape, F32)] * 4,
        [VM] * 5,
        [],
        [near(gain_part), near(gain_other), gains, gain_moment, gain_second],
    )
    return (
        outputs,
        input_grad,
        weight_grad,
        gain_grad,
        new_weights,
        new_weight_moment,
        new_weight_second,
        new_gains,
        new_gain_moment,
        new_gain_second,
    )


def solution(mesh):
    rows = P(("blk", "shard"), None)
    cells = P(("blk", "shard"), "head")
    lanes = P(None, ("blk", "shard"))
    return jax.shard_map(
        layer,
        mesh=mesh,
        in_specs=(rows, rows, cells, lanes, cells, cells, lanes, lanes),
        out_specs=(rows, rows, cells, lanes, cells, cells, cells, lanes, lanes, lanes),
        check_vma=False,
    )
```

```python
from functools import partial
import math

import jax
import jax.numpy as jnp
from jax import lax
from jax.experimental import pallas as pl
from jax.experimental.pallas import tpu as pltpu
from jax.sharding import PartitionSpec as P


HEADS = 12
HEAD_DIM = 64
FF = 1152
STEP = 3

NORM_EPS = 1e-05
THETA = 160000.0
BETA_ONE = 0.9
BETA_TWO = 0.98
LEARN_RATE = 0.2
ADAM_EPS = 1e-06
DECAY = 0.01
NEG_LARGE = -1e30
SCALE = 1.0 / math.sqrt(HEAD_DIM)
TOKENS_AX = ("blk", "shard")
F32 = jnp.float32
BF16 = jnp.bfloat16
KEY_ROWS = 2048
SUB_ROWS = 512


VM = pl.BlockSpec(memory_space=pltpu.VMEM)
SM = pl.BlockSpec(memory_space=pltpu.SMEM)
ANY = pl.BlockSpec(memory_space=pl.ANY)
HBM = pl.BlockSpec(memory_space=pltpu.HBM)


def near(x):
    return pltpu.with_memory_space_constraint(x, pltpu.VMEM) if staged() else x


def near_out(shape, dtype):
    return pltpu.VMEM(shape, dtype) if staged() else jax.ShapeDtypeStruct(shape, dtype)


def sds(shape, dtype):
    return jax.ShapeDtypeStruct(shape, dtype)


def dot_nn(a, b):
    return lax.dot_general(a, b, (((1,), (0,)), ((), ())), preferred_element_type=F32)


def dot_nt(a, b):
    return lax.dot_general(a, b, (((1,), (1,)), ((), ())), preferred_element_type=F32)


def dot_tn(a, b):
    return lax.dot_general(a, b, (((0,), (0,)), ((), ())), preferred_element_type=F32)


def swap(x, axis, bits):
    size = lax.axis_size(axis)
    return lax.ppermute(x, axis, [(i, i ^ bits) for i in range(size)])


def staged():
    return lax.axis_size("blk") == 4 and lax.axis_size("shard") == 4


def chunk_order():
    return [z * 4 + x * 2 + c for c in range(2) for x in range(2) for z in range(4)]


def gather(x):
    if not staged():
        return [lax.all_gather(x, TOKENS_AX, axis=0, tiled=True)]
    got = {0: x}
    got[8] = swap(x, "blk", 2)
    got[4] = swap(x, "blk", 1)
    got[12] = swap(got[8], "blk", 1)
    for z in range(4):
        got[z * 4 + 2] = swap(got[z * 4], "shard", 2)
    for z in range(4):
        for h in (0, 2):
            got[z * 4 + h + 1] = swap(got[z * 4 + h], "shard", 1)
    return [got[j] for j in chunk_order()]


def add_kernel(keep, recv, *outs):
    for i, out in enumerate(outs):
        rows = out.shape[0]
        at = pl.ds(i * rows, rows)
        out[...] = (keep[at, :].astype(F32) + recv[at, :].astype(F32)).astype(BF16)


def add_far_kernel(keep, got, *rest):
    outs = rest[:4]
    kept, done, sems = rest[4:]
    rows = outs[0].shape[0]
    at = [pl.ds(i * rows, rows) for i in range(4)]
    loads = [
        pltpu.make_async_copy(keep.at[at[i], :], kept.at[at[i], :], sems.at[0, i])
        for i in range(4)
    ]
    stores = [pltpu.make_async_copy(done.at[at[i], :], outs[i], sems.at[1, i]) for i in range(4)]
    for copy in loads:
        copy.start()
    for i in range(4):
        loads[i].wait()
        done[at[i], :] = (kept[at[i], :].astype(F32) + got[at[i], :].astype(F32)).astype(BF16)
        stores[i].start()
    for copy in stores:
        copy.wait()


def pair_add(keep, recv, name):
    rows, cols = keep.shape[0] // 4, keep.shape[1]
    close = name[0] == "d"
    scratch = [pltpu.VMEM(keep.shape, BF16)] * 2 + [pltpu.SemaphoreType.DMA((2, 4))]
    return pl.pallas_call(
        add_kernel if close else add_far_kernel,
        out_shape=[(near_out if close else sds)((rows, cols), BF16)] * 4,
        in_specs=[VM if close else HBM, VM],
        out_specs=[VM if close else HBM] * 4,
        scratch_shapes=[] if close else scratch,
        name="pair_add",
    )(near(keep) if close else keep, near(recv))


def native_sum(part):
    return [lax.psum_scatter(part, TOKENS_AX, scatter_dimension=0, tiled=True)]


def pair_swap(groups):
    return [swap(groups[2 + x], "shard", 1) for x in (1, 0)][::-1]


def scatter_sum(groups, recv, tag):
    s = pair_add(groups[1], recv[1], f"{tag}add1")
    got = {z: swap(s[z], "shard", 2) for z in (3, 2, 1, 0)}
    keep = pair_add(groups[0], recv[0], f"{tag}add0")

    def block(z, *more):
        return total([keep[z], got[z], *more]).astype(BF16)

    far = swap(block(3), "blk", 1)
    two = swap(block(2, far), "blk", 2)
    one = swap(block(1), "blk", 1)
    return [keep[0], got[0], one, two]


def total(terms):
    out = terms[0].astype(F32)
    for term in terms[1:]:
        out = out + term.astype(F32)
    return out


def weight_copies(order_ref, chunks, dst, sems, cols=None):
    rows = chunks[0].shape[0]
    copies = []
    for i, chunk in enumerate(chunks):
        src = chunk if cols is None else chunk.at[:, pl.ds(cols[0], cols[1])]
        if len(chunks) == 1:
            at = pl.ds(0, rows)
        else:
            at = pl.ds(pl.multiple_of((order_ref[0] ^ chunk_order()[i]) * rows, 16), rows)
        copies.append(pltpu.make_async_copy(src, dst.at[at, :], sems.at[i]))
    for copy in copies:
        copy.start()
    return copies


def group_copies(src, outs, sems, first_col):
    rows, cols = src.shape[0] // len(outs), src.shape[1]
    copies = [
        pltpu.make_async_copy(
            src.at[pl.ds(i * rows, rows), :], out.at[:, pl.ds(first_col, cols)], sems.at[i]
        )
        for i, out in enumerate(outs)
    ]
    for copy in copies:
        copy.start()
    for copy in copies:
        copy.wait()


def emit_blocks(order_ref, acc, dst, staged_rows):
    if not staged_rows:
        dst[...] = acc[...].astype(BF16)
        return
    rows = acc.shape[0] // 16
    for i, j in enumerate(chunk_order()):
        at = pl.ds(pl.multiple_of((order_ref[0] ^ j) * rows, 8), rows)
        dst[pl.ds(i * rows, rows), :] = acc[at, :].astype(BF16)


def norm_parts(v):
    centre = v - jnp.mean(v, axis=-1, keepdims=True)
    inv = lax.rsqrt(jnp.mean(centre * centre, axis=-1, keepdims=True) + NORM_EPS)
    return centre * inv, inv


def norm_back(u, xhat, inv, g):
    s = u * g
    return inv * (
        s
        - jnp.mean(s, axis=-1, keepdims=True)
        - xhat * jnp.mean(s * xhat, axis=-1, keepdims=True)
    )


def low_half(shape):
    lane = lax.broadcasted_iota(jnp.int32, shape, 1)
    return (lane & (HEAD_DIM - 1)) < HEAD_DIM // 2


def turn(u):
    width = u.shape[1]
    half = HEAD_DIM // 2
    left = pltpu.roll(u, width - half, 1)
    right = pltpu.roll(u, half, 1)
    return left, right, low_half(u.shape)


def rope(u, cos, sin):
    left, right, low = turn(u)
    return u * cos + jnp.where(low, -left, right) * sin


def rope_back(w, cos, sin):
    left, right, low = turn(w * sin)
    return w * cos + jnp.where(low, left, -right)


def wide(table, width):
    return jnp.concatenate([table] * (width // table.shape[1]), axis=1)


def two_heads(pair):
    lane = lax.broadcasted_iota(jnp.int32, pair.shape, 1)
    zero = jnp.zeros_like(pair)
    first = lane < HEAD_DIM
    return jnp.concatenate(
        [jnp.where(first, pair, zero), jnp.where(first, zero, pair)], axis=0
    )


def join_heads(both):
    rows = both.shape[0] // 2
    lane = lax.broadcasted_iota(jnp.int32, (rows, both.shape[1]), 1)
    return jnp.where(lane < HEAD_DIM, both[:rows], both[rows:])


def as_row(col):
    return jnp.transpose(jnp.broadcast_to(col, (col.shape[0], 128)))[0:1, :]


def qkv_kernel(n, order_ref, x_ref, cos_ref, sin_ref, *rest):
    chunks = rest[:n]
    at_ref, q_ref, kv_ref, g_ref, w, sems = rest[n:]
    width = q_ref.shape[1]
    copies = weight_copies(order_ref, chunks, w, sems)
    xhat, _ = norm_parts(x_ref[...])
    for copy in copies:
        copy.wait()
    row = lax.broadcasted_iota(jnp.int32, (8, 128), 0)
    lane = lax.broadcasted_iota(jnp.int32, (8, 128), 1)
    pick = jnp.where(row == lane, 1.0, 0.0).astype(BF16)
    g = dot_nt(pick, w[:, 4 * width : 4 * width + 128])
    g_ref[...] = g
    a = (xhat * g[0:1, :]).astype(BF16)
    at_ref[...] = jnp.transpose(a)
    cos = wide(cos_ref[...], width)
    sin = wide(sin_ref[...], width)
    q_ref[...] = rope(dot_nn(a, w[:, :width]), cos, sin).astype(BF16)
    kv_ref[:, :width] = rope(dot_nn(a, w[:, width : 2 * width]), cos, sin).astype(BF16)
    kv_ref[:, width:] = dot_nn(a, w[:, 2 * width : 3 * width]).astype(BF16)


def key_copies(chunks, dst, sems, block):
    if len(chunks) == 1:
        rows = dst.shape[0]
        at = pl.ds(pl.multiple_of(block * rows, rows), rows)
        copies = [pltpu.make_async_copy(chunks[0].at[at, :], dst, sems.at[0])]
    else:
        rows = chunks[0].shape[0]
        copies = [
            pltpu.make_async_copy(chunk, dst.at[pl.ds(i * rows, rows), :], sems.at[i])
            for i, chunk in enumerate(chunks)
        ]
    for copy in copies:
        copy.start()
    return copies


def each(count, body):
    if count == 1:
        body(0)
    else:
        lax.fori_loop(0, count, lambda i, c: (body(i), c)[1], 0)


def attend_kernel(n, nw, blocks, order_ref, q_ref, *rest):
    keys = rest[:n]
    wos = rest[n : n + nw]
    attn_ref, lse_ref, out_ref, kv, wo, m_s, l_s, acc_s, ksem, wsem = rest[n + nw :]
    width = q_ref.shape[1]
    pairs = width // 128
    wcopies = weight_copies(order_ref, wos, wo, wsem, (3 * width, width))
    m_s[...] = jnp.full(m_s.shape, NEG_LARGE, F32)
    l_s[...] = jnp.zeros(l_s.shape, F32)
    acc_s[...] = jnp.zeros(acc_s.shape, F32)

    def block_work(block):
        for copy in key_copies(keys, kv, ksem, block):
            copy.wait()
        for p in range(pairs):
            at = slice(p * 128, p * 128 + 128)
            qm = two_heads(q_ref[:, at]) * jnp.asarray(SCALE, BF16)
            s = dot_nt(qm, kv[:, at])
            m_old = m_s[p]
            m_new = jnp.maximum(m_old, jnp.max(s, axis=1, keepdims=True))
            factor = jnp.exp(m_old - m_new)
            e = jnp.exp(s - m_new)
            l_s[p] = l_s[p] * factor + jnp.sum(e, axis=1, keepdims=True)
            m_s[p] = m_new
            acc_s[p] = acc_s[p] * factor + dot_nn(
                e.astype(BF16), kv[:, width + p * 128 : width + p * 128 + 128]
            )

    each(blocks, block_work)
    for p in range(pairs):
        attn_ref[:, p * 128 : p * 128 + 128] = join_heads(acc_s[p] / l_s[p]).astype(BF16)
        lse_ref[p : p + 1, :] = as_row(m_s[p] + jnp.log(l_s[p]))
    for copy in wcopies:
        copy.wait()
    out_ref[...] = dot_nt(attn_ref[...], wo[...]).astype(BF16)


def gelu_parts(z):
    cdf = 0.5 * (1.0 + lax.erf(z * 0.7071067811865476))
    density = jnp.exp(-0.5 * z * z) * 0.3989422804014327
    return z * cdf, cdf + z * density


def ffn_kernel(nw, order_ref, x_ref, pa_ref, pb_ref, cot_ref, g_ref, *rest):
    ws = rest[:nw]
    hid_ref, out_ref, db_ref, b_ref, dz_ref, mixed_ref, w, wsem = rest[nw:]
    units = mixed_ref.shape[1]
    copies = weight_copies(order_ref, ws, w, wsem)
    hidden = x_ref[...] + (pa_ref[...].astype(F32) + pb_ref[...].astype(F32))
    hid_ref[...] = hidden
    xhat, _ = norm_parts(hidden)
    b = (xhat * g_ref[1:2, :]).astype(BF16)
    b_ref[...] = b
    cb = cot_ref[...].astype(BF16)
    for copy in copies:
        copy.wait()
    z = dot_nn(b, w[:, : 2 * units])
    gate = z[:, units:]
    act, slope = gelu_parts(z[:, :units])
    dmix = dot_nn(cb, w[:, 2 * units : 3 * units])
    dz = jnp.concatenate([dmix * gate * slope, dmix * act], axis=1).astype(BF16)
    dz_ref[...] = dz
    db_ref[...] = dot_nt(dz, w[:, : 2 * units]).astype(BF16)
    mixed = (act * gate).astype(BF16)
    mixed_ref[...] = mixed
    out_ref[...] = dot_nt(mixed, w[:, 2 * units : 3 * units]).astype(BF16)


def ffn_grad_kernel(no, order_ref, b_ref, dz_ref, cot_ref, mixed_ref, *rest):
    outs = rest[:no]
    acc, dst, sems = rest[no:]
    two = dz_ref.shape[1]
    acc[:, :two] = dot_tn(b_ref[...], dz_ref[...])
    half = mixed_ref.shape[1]
    acc[:, two : two + half] = dot_tn(cot_ref[...].astype(BF16), mixed_ref[...])
    acc[:, two + half :] = jnp.zeros((acc.shape[0], acc.shape[1] - two - half), F32)
    emit_blocks(order_ref, acc, dst, no > 1)
    group_copies(dst, outs, sems, 0)


def oq_grad_kernel(no, first_col, order_ref, at_ref, dqp_ref, dhid_ref, attn_ref, *rest):
    outs = rest[no : 2 * no]
    ht, dst, sems = rest[2 * no :]
    width = dqp_ref.shape[1]
    ht[...] = jnp.transpose(dhid_ref[...].astype(BF16))
    a_t, h_t = rows_in_order(order_ref, at_ref, no), rows_in_order(order_ref, ht, no)
    dst[:, :width] = dot_nn(a_t, dqp_ref[...]).astype(BF16)
    dst[:, width:] = dot_nn(h_t, attn_ref[...]).astype(BF16)
    group_copies(dst, outs, sems, first_col)


def back_tile(k, v, qm, dom, lse_row, dot_row):
    prob = jnp.exp(dot_nt(k, qm) - lse_row)
    ds = (prob * (dot_nt(v, dom) - dot_row)).astype(BF16)
    return dot_nn(ds, qm), dot_nn(prob.astype(BF16), dom), dot_tn(ds, k)


def back_kernel(
    n, nw, no, blocks, order_ref, q_ref, attn_ref, lse_ref, hid_ref, cot_ref, g_ref,
    da_ref, db_ref, cos_ref, sin_ref, *rest
):
    keys = rest[:n]
    wos = rest[n : n + nw]
    outs = rest[n + nw : n + nw + no]
    dhid_ref, dqp_ref, kv, wo, dq_s, qm_s, dom_s, row_s, ksem, wsem = rest[n + nw + no :]
    width = q_ref.shape[1]
    pairs = width // 128
    wcopies = weight_copies(order_ref, wos, wo, wsem, (3 * width, width))
    first = key_copies(keys, kv, ksem, 0) if blocks == 1 else None
    xhat, inv = norm_parts(hid_ref[...])
    db = da_ref[...].astype(F32) + db_ref[...].astype(F32)
    dhid = cot_ref[...] + norm_back(db, xhat, inv, g_ref[1:2, :])
    dhid_ref[...] = dhid
    for copy in wcopies:
        copy.wait()
    dattn = dot_nn(dhid.astype(BF16), wo[...]).astype(BF16)
    for p in range(pairs):
        at = slice(p * 128, p * 128 + 128)
        qm_s[p] = two_heads(q_ref[:, at]) * jnp.asarray(SCALE, BF16)
        dom = two_heads(dattn[:, at])
        dom_s[p] = dom
        both = jnp.concatenate([attn_ref[:, at]] * 2, axis=0)
        dots = jnp.sum(dom.astype(F32) * both.astype(F32), axis=1, keepdims=True)
        row_s[p : p + 1, :] = as_row(dots)
    dq_s[...] = jnp.zeros(dq_s.shape, F32)
    block_rows = kv.shape[0]

    def block_work(block):
        for copy in first or key_copies(keys, kv, ksem, block):
            copy.wait()
        for group, out_ref in enumerate(outs):
            size = block_rows // no

            def sub_work(sub):
                start = group * size + sub * SUB_ROWS
                src = pl.ds(pl.multiple_of(start, SUB_ROWS), SUB_ROWS)
                dst = pl.ds(
                    pl.multiple_of(block * block_rows + sub * SUB_ROWS, SUB_ROWS), SUB_ROWS
                )
                for p in range(pairs):
                    at = slice(p * 128, p * 128 + 128)
                    vat = slice(width + p * 128, width + p * 128 + 128)
                    dk, dv, dq = back_tile(
                        kv[src, at], kv[src, vat], qm_s[p], dom_s[p],
                        lse_ref[p : p + 1, :], row_s[p : p + 1, :],
                    )
                    out_ref[dst, at] = dk.astype(BF16)
                    out_ref[dst, vat] = dv.astype(BF16)
                    dq_s[p] += dq

            each(size // SUB_ROWS, sub_work)

    each(blocks, block_work)
    dq = jnp.concatenate([join_heads(dq_s[p]) for p in range(pairs)], axis=1) * SCALE
    dqp_ref[...] = rope_back(
        dq, wide(cos_ref[...], width), wide(sin_ref[...], width)
    ).astype(BF16)


def rows_in_order(order_ref, ref, groups):
    if groups == 1:
        return ref[...]
    rows = ref.shape[0] // 16
    return jnp.concatenate(
        [
            ref[pl.ds(pl.multiple_of((order_ref[0] ^ j) * rows, 16), rows), :]
            for j in chunk_order()
        ],
        axis=0,
    )


def qkv_grad_kernel(n, nt, no, order_ref, at_ref, dqp_ref, cos_ref, sin_ref, *rest):
    terms = rest[:nt]
    chunks = rest[nt : nt + n]
    outs = rest[nt + n : nt + n + no]
    da_ref, w, sems = rest[nt + n + no :]
    width = dqp_ref.shape[1]
    copies = weight_copies(order_ref, chunks, w, sems, (0, 3 * width))
    dkv = total([term[...] for term in terms])
    dkp = rope_back(
        dkv[:, :width], wide(cos_ref[...], width), wide(sin_ref[...], width)
    ).astype(BF16)
    d = jnp.concatenate([dkp, dkv[:, width:].astype(BF16)], axis=1)
    both = dot_nn(rows_in_order(order_ref, at_ref, no), d).astype(BF16)
    size = both.shape[0] // no
    for i, out in enumerate(outs):
        out[...] = both[i * size : (i + 1) * size]
    for copy in copies:
        copy.wait()
    da = dot_nt(dqp_ref[...], w[:, :width]) + dot_nt(d, w[:, width:])
    da_ref[...] = da.astype(BF16)


def call(kernel, out_shape, specs, scratch, args):
    return pl.pallas_call(
        kernel,
        out_shape=out_shape,
        in_specs=specs,
        out_specs=jax.tree.map(lambda _: VM, out_shape),
        scratch_shapes=scratch,
    )(*args)


def rotary_tables(positions):
    half = HEAD_DIM // 2
    inverse = jnp.exp(jnp.arange(half, dtype=F32) * (-2.0 * math.log(THETA) / HEAD_DIM))
    angles = positions.astype(F32)[:, None] * inverse[None, :]
    angles = jnp.concatenate([angles] * 4, axis=-1)
    return jnp.cos(angles), jnp.sin(angles)


def adam_update(tensor, gradient, moment, second):
    moment = BETA_ONE * moment + (1.0 - BETA_ONE) * gradient
    second = BETA_TWO * second + (1.0 - BETA_TWO) * gradient * gradient
    first_hat = moment / (1.0 - BETA_ONE**STEP)
    second_hat = second / (1.0 - BETA_TWO**STEP)
    tensor = tensor - LEARN_RATE * (first_hat / (jnp.sqrt(second_hat) + ADAM_EPS) + DECAY * tensor)
    return tensor, moment, second


def gsum_kernel(nf, width, units, w_ref, *rest):
    firsts, lasts = rest[:nf], rest[nf : 2 * nf]
    g_ref, gain_ref = rest[2 * nf :]
    kv = total([term[...] for term in firsts])
    rest_sum = total([term[...] for term in lasts])
    two = rest_sum[:, : 3 * units]
    oq = rest_sum[:, rest_sum.shape[1] - 2 * width :]
    one = jnp.concatenate([oq[:, :width], kv, oq[:, width:]], axis=1)
    wf = w_ref[...].astype(BF16).astype(F32)
    cut = 4 * width
    sums = [
        jnp.sum(wf[:, : 3 * width] * one[:, : 3 * width], axis=1, keepdims=True),
        jnp.sum(wf[:, cut : cut + 2 * units] * two[:, : 2 * units], axis=1, keepdims=True),
    ]
    lane = lax.broadcasted_iota(jnp.int32, (wf.shape[0], 128), 1)
    cols = jnp.where(lane == 0, sums[0], jnp.where(lane == 1, sums[1], 0.0))
    gain_ref[...] = jnp.transpose(cols)[:2, :]
    g_ref[:, :cut] = one
    g_ref[:, cut:] = two


def adam_kernel(w_ref, g_ref, m_ref, v_ref, w_out, m_out, v_out):
    w_out[...], m_out[...], v_out[...] = adam_update(
        w_ref[...], g_ref[...], m_ref[...], v_ref[...]
    )


def gadam_kernel(a_ref, b_ref, w_ref, m_ref, v_ref, g_out, w_out, m_out, v_out):
    w = w_ref[...]
    grad = (a_ref[...] + b_ref[...]) / w.astype(BF16).astype(F32)
    g_out[...] = grad
    w_out[...], m_out[...], v_out[...] = adam_update(w, grad, m_ref[...], v_ref[...])


def lnback_kernel(
    x_ref, da_ref, db_ref, dhid_ref, g_ref, hid_ref, fa_ref, fb_ref, grad_ref, out_ref
):
    xhat, inv = norm_parts(x_ref[...])
    da = da_ref[...].astype(F32) + db_ref[...].astype(F32)
    grad_ref[...] = dhid_ref[...] + norm_back(da, xhat, inv, g_ref[0:1, :])
    out_ref[...] = hid_ref[...] + (fa_ref[...].astype(F32) + fb_ref[...].astype(F32))


def head_swap(x):
    if lax.axis_size("head") == 1:
        return jnp.zeros_like(x)
    return swap(x, "head", 1)


def layer(
    inputs, cotangent, weights, gains, weight_moment, weight_second, gain_moment, gain_second
):
    heads = lax.axis_size("head")
    width = HEADS // heads * HEAD_DIM
    units = FF // heads
    toks, d = inputs.shape
    rows = weights.shape[0]
    n = lax.axis_size(TOKENS_AX)
    seq = toks * n
    me = lax.axis_index(TOKENS_AX).astype(jnp.int32)
    order = me.reshape(1)
    pairs = width // 128

    wb = weights.astype(BF16)
    gb = gains.astype(BF16)
    wq_cols = 4 * width + 128
    rest_pad = -(3 * units) % 128
    rest_cols = 3 * units + rest_pad
    w_first = jnp.concatenate([wb[:, : 4 * width], jnp.pad(gb.T, ((0, 0), (0, 126)))], axis=1)
    w_rest = jnp.pad(wb[:, 4 * width :], ((0, 0), (0, rest_pad)))
    first_chunks = gather(w_first)
    cos, sin = rotary_tables(me * toks + jnp.arange(toks, dtype=jnp.int32))

    nw = len(first_chunks)
    wsem = pltpu.SemaphoreType.DMA((nw,))
    parts = 4 if staged() else 1

    a_t, q, kv, g = call(
        partial(qkv_kernel, nw),
        [sds((d, toks), BF16), sds((toks, width), BF16), sds((toks, 2 * width), BF16), sds((8, d), F32)],
        [SM, VM, VM, VM] + [ANY] * nw,
        [pltpu.VMEM((d, wq_cols), BF16), wsem],
        [order, inputs, cos, sin] + first_chunks,
    )
    keys = gather(kv)
    rest_chunks = gather(w_rest)
    nk = len(keys)
    block_rows = min(KEY_ROWS, seq)
    blocks = seq // block_rows
    ksem = pltpu.SemaphoreType.DMA((nk,))

    attn, lse, out_part = call(
        partial(attend_kernel, nk, nw, blocks),
        [sds((toks, width), BF16), sds((8, 2 * toks), F32), near_out((toks, d), BF16)],
        [SM, VM] + [ANY] * (nk + nw),
        [
            pltpu.VMEM((block_rows, 2 * width), BF16),
            pltpu.VMEM((d, width), BF16),
            pltpu.VMEM((pairs, 2 * toks, 1), F32),
            pltpu.VMEM((pairs, 2 * toks, 1), F32),
            pltpu.VMEM((pairs, 2 * toks, 128), F32),
            ksem,
            wsem,
        ],
        [order, q] + keys + first_chunks,
    )
    out_other = head_swap(out_part)

    hidden, ffn_part, db_part, b, dz, mixed = call(
        partial(ffn_kernel, nw),
        [
            sds((toks, d), F32),
            sds((toks, d), BF16),
            near_out((toks, d), BF16),
            sds((toks, d), BF16),
            sds((toks, 2 * units), BF16),
            sds((toks, units), BF16),
        ],
        [SM] + [VM] * 5 + [ANY] * nw,
        [pltpu.VMEM((d, rest_cols), BF16), wsem],
        [order, inputs, near(out_part), near(out_other), cotangent, g] + rest_chunks,
    )
    db_other = head_swap(db_part)
    ffn_other = head_swap(ffn_part)
    grad_cols = rest_cols + 2 * width
    part_sem = pltpu.SemaphoreType.DMA((parts,))
    group = [sds((d // parts, grad_cols), BF16)] * parts
    rest_grads = pl.pallas_call(
        partial(ffn_grad_kernel, parts),
        out_shape=group,
        in_specs=[SM] + [VM] * 4,
        out_specs=[HBM] * parts,
        scratch_shapes=[
            pltpu.VMEM((d, rest_cols), F32),
            pltpu.VMEM((d, rest_cols), BF16),
            part_sem,
        ],
        name="ffngrad",
    )(order, b, dz, cotangent, mixed)

    both = (pairs, 2 * toks, 128)
    *kv_groups, dhid, dqp = call(
        partial(back_kernel, nk, nw, parts, blocks),
        [sds((seq // parts, 2 * width), BF16)] * parts
        + [sds((toks, d), F32), sds((toks, width), BF16)],
        [SM] + [VM] * 10 + [ANY] * (nk + nw),
        [
            pltpu.VMEM((block_rows, 2 * width), BF16),
            pltpu.VMEM((d, width), BF16),
            pltpu.VMEM(both, F32),
            pltpu.VMEM(both, BF16),
            pltpu.VMEM(both, BF16),
            pltpu.VMEM((8, 2 * toks), F32),
            ksem,
            wsem,
        ],
        [order, q, attn, lse, hidden, cotangent, g, near(db_part), near(db_other), cos, sin]
        + keys
        + first_chunks,
    )
    rest_grads = pl.pallas_call(
        partial(oq_grad_kernel, parts, rest_cols),
        out_shape=group,
        in_specs=[SM] + [VM] * 4 + [HBM] * parts,
        out_specs=[HBM] * parts,
        scratch_shapes=[pltpu.VMEM((d, toks), BF16), pltpu.VMEM((d, 2 * width), BF16), part_sem],
        input_output_aliases={5 + i: i for i in range(parts)},
        name="oqgrad",
    )(order, a_t, dqp, dhid, attn, *rest_grads)
    if staged():
        kv_terms = scatter_sum(kv_groups, pair_swap(kv_groups), "b")
        rest_terms = scatter_sum(rest_grads, pair_swap(rest_grads), "f")
    else:
        kv_terms = native_sum(*kv_groups)
        rest_terms = native_sum(*rest_grads)
    nt = len(kv_terms)
    *w_groups, da_part = call(
        partial(qkv_grad_kernel, nw, nt, parts),
        [near_out((d // parts, 2 * width), BF16)] * parts + [near_out((toks, d), BF16)],
        [SM] + [VM] * 4 + [VM] * nt + [ANY] * nw,
        [pltpu.VMEM((d, 3 * width), BF16), wsem],
        [order, a_t, dqp, cos, sin] + [near(x) for x in kv_terms] + first_chunks,
    )
    da_other = head_swap(da_part)
    input_grad, outputs = call(
        lnback_kernel,
        [sds((toks, d), F32)] * 2,
        [VM] * 8,
        [],
        [inputs, near(da_part), near(da_other), dhid, g, hidden, ffn_part, near(ffn_other)],
    )
    if staged():
        first_terms = scatter_sum(w_groups, pair_swap(w_groups), "d")
    else:
        first_terms = native_sum(*w_groups)
    full = weights.shape
    weight_grad, gain_part = call(
        partial(gsum_kernel, nt, width, units),
        [sds(full, F32), near_out(gains.shape, F32)],
        [VM] * (1 + 2 * nt),
        [],
        [weights] + [near(x) for x in first_terms + rest_terms],
    )
    gain_other = head_swap(gain_part)
    step_rows = rows // 2 if rows % 16 == 0 else rows
    cells = pl.BlockSpec((step_rows, full[1]), lambda i: (i, 0))
    new_weights, new_weight_moment, new_weight_second = pl.pallas_call(
        adam_kernel,
        grid=(rows // step_rows,),
        out_shape=[sds(full, F32)] * 3,
        in_specs=[cells] * 4,
        out_specs=[cells] * 3,
        name="adam",
    )(weights, weight_grad, weight_moment, weight_second)
    gain_grad, new_gains, new_gain_moment, new_gain_second = call(
        gadam_kernel,
        [sds(gains.shape, F32)] * 4,
        [VM] * 5,
        [],
        [near(gain_part), near(gain_other), gains, gain_moment, gain_second],
    )
    return (
        outputs,
        input_grad,
        weight_grad,
        gain_grad,
        new_weights,
        new_weight_moment,
        new_weight_second,
        new_gains,
        new_gain_moment,
        new_gain_second,
    )


def solution(mesh):
    rows = P(("blk", "shard"), None)
    cells = P(("blk", "shard"), "head")
    lanes = P(None, ("blk", "shard"))
    return jax.shard_map(
        layer,
        mesh=mesh,
        in_specs=(rows, rows, cells, lanes, cells, cells, lanes, lanes),
        out_specs=(rows, rows, cells, lanes, cells, cells, cells, lanes, lanes, lanes),
        check_vma=False,
    )
```
